128 devices in a mesh: elem: 128 (over y, x, z, core).
Axes of the slice: x: 4, y: 4, z: 4, core: 2. Of those that a mesh axis runs over, the one named last changes fastest.
Arguments:
- a_blocks: float32 [4096, 7, 4096], P('elem'), may hold values from -0.25 to 0.25
- p_blocks: float32 [4096, 2, 4096], P('elem'), may hold values from -1.2 to 1.2
- a_slot: int32 [4096, 7], P('elem'), may hold values from 0 to 285
- serve_rows: int32 [128, 127, 2], P('elem'), may hold values from 0 to 31
- row_count: int32 [128], P('elem'), may hold values from 8 to 32, as said below
- contrib_slot: int32 [4096, 28], P('elem'), may hold values from 0 to 511
- recv_tile: int32 [128, 128, 4], P('elem'), may hold values from 0 to 7
Outputs:
- coarse: float32 [1024, 4096], P('elem')
The draws below stay inside these ranges and needn't reach their ends.
Inputs may be any that keep to these rules, and one draw needn't show every extreme that they name: `row_count`: rows of a device at or beyond its count are padding and contribute nothing; some device has exactly 32.
All inputs are finite; a program needn't handle non-finite values.
Results may differ from the reference program's by a relative error of at most 0.0003.
Values sent between devices are 32-bit elements; how exact they have to be, the bound alone decides.
A program may use at most 192 MiB of HBM per device.

```python
import jax
import jax.numpy as jnp
from jax import lax

B = 64
KA = 7
KP = 2
S = 2
CAP = 4
TO = 8
R = 32
NB = 127
NO = 128
NF = 4096
N_ELEM = 128


def draw_row_count(key, part):
    first, second = jax.random.split(jax.random.fold_in(key, 17))
    counts = jax.random.randint(first, (N_ELEM,), R // 4, R + 1)
    chosen = jax.random.randint(second, (), 0, N_ELEM)
    return jnp.where(jnp.arange(N_ELEM) == chosen, R, counts).astype(jnp.int32)


def draw_a_slot(key, part):
    first, second, third = jax.random.split(jax.random.fold_in(key, 23), 3)
    pick = jax.random.randint(first, (NF, KA), 0, 2)
    own = jax.random.randint(second, (NF, KA), 0, R)
    far = jax.random.randint(third, (NF, KA), R, R + (N_ELEM - 1) * S)
    return jnp.where(pick == 0, own, far).astype(jnp.int32)


def draw_contrib_slot(key, part):
    first, second, third = jax.random.split(jax.random.fold_in(key, 29), 3)
    shape = (NF, KP * KA * KP)
    pick = jax.random.randint(first, shape, 0, 2)
    home = jax.random.randint(second, shape, 0, CAP)
    spread = jax.random.randint(third, shape, 0, N_ELEM * CAP)
    return jnp.where(pick == 0, home, spread).astype(jnp.int32)


def with_ends(drawn, stream_key, least, largest):
    shape = drawn.shape
    spot = [jax.random.randint(jax.random.fold_in(stream_key, axis), (), 0, shape[axis]) for axis in range(len(shape))]
    drawn = drawn.at[tuple(spot)].set(least)
    longest = shape.index(max(shape))
    spot[longest] = (spot[longest] + 1) % shape[longest]
    return drawn.at[tuple(spot)].set(largest)


def shard_levels(key, dims, cuts, low, high):
    def one(dim, parts):
        draws = jax.random.uniform(jax.random.fold_in(jax.random.fold_in(key, 6), dim), (parts,), jnp.float32, low / len(cuts), high / len(cuts))
        return jnp.repeat(jnp.exp(draws), dims[dim] // parts).reshape((-1,) + (1,) * (len(dims) - dim - 1))

    factor_of = one(*cuts[0])
    for cut in cuts[1:]:
        factor_of = factor_of * one(*cut)
    return factor_of


def bell_draw(rng, dims, scale, reach, cuts=(), kind=jnp.bfloat16):
    drawn = scale * jax.random.normal(rng, dims, jnp.float32)
    if cuts:
        drawn = drawn * shard_levels(rng, dims, cuts, -0.22, 0.18)
    return jnp.clip(drawn, -reach, reach).astype(kind)


def setup_inputs(seed: int = 0) -> dict:
    splits = jax.random.split(jax.random.key(seed), 8)
    return {
        "a_blocks": bell_draw(splits[0], (NF, KA, B * B), (B * KA) ** -0.5, 0.25, ((0, 128),), jnp.float32),
        "p_blocks": bell_draw(splits[1], (NF, KP, B * B), 0.15, 1.2, ((0, 128),), jnp.float32),
        "a_slot": draw_a_slot(jax.random.fold_in(splits[7], 71), 0),
        "serve_rows": with_ends(jax.random.randint(splits[3], (N_ELEM, NB, S), 0, R), jax.random.fold_in(splits[3], 1), 0, R - 1).astype(jnp.int32),
        "row_count": draw_row_count(jax.random.fold_in(splits[7], 71), 0),
        "contrib_slot": draw_contrib_slot(jax.random.fold_in(splits[7], 71), 0),
        "recv_tile": with_ends(jax.random.randint(splits[6], (N_ELEM, NO, CAP), 0, TO), jax.random.fold_in(splits[6], 1), 0, TO - 1).astype(jnp.int32),
    }


def reference(a_blocks, p_blocks, a_slot, serve_rows, row_count, contrib_slot, recv_tile):
    ndev = N_ELEM
    count_near = N_ELEM - 1
    count_all = N_ELEM
    a_four = a_blocks.reshape(ndev, R, KA, B, B)
    p_four = p_blocks.reshape(ndev, R, KP, B, B)
    p_flat = p_blocks.reshape(ndev * R, KP, B, B)
    slot_three = a_slot.reshape(ndev, R, KA)
    contrib = contrib_slot.reshape(ndev, R * KP * KA * KP)
    near = jnp.arange(count_near, dtype=jnp.int32) + 1
    every = jnp.arange(count_all, dtype=jnp.int32)
    positions = jnp.arange(count_near, dtype=jnp.int32)
    sources = jnp.arange(ndev, dtype=jnp.int32)
    slot_ids = jnp.arange(count_all * CAP, dtype=jnp.int32)
    which = slot_ids // CAP
    within = slot_ids % CAP
    local_rows = jnp.arange(R, dtype=jnp.int32)

    def one_device(total, device):
        servers = (device - near) % ndev
        row_ids = (servers[:, None] * R + serve_rows[servers, positions]).reshape(-1)
        fetched = p_flat[row_ids]
        own = p_four[device]
        extended = jnp.concatenate([own, fetched], axis=0)
        neigh = extended[slot_three[device]]
        product = jnp.einsum('ikxy,ikqyz->ikqxz', a_four[device], neigh, precision=lax.Precision.HIGHEST)
        part = jnp.einsum('ipyx,ikqyz->ipkqxz', own, product, precision=lax.Precision.HIGHEST)
        live = (local_rows < row_count[device]).astype(jnp.float32)
        part = part * live[:, None, None, None, None, None]
        slots = jax.ops.segment_sum(part.reshape(-1, B * B), contrib[device], num_segments=count_all * CAP)
        owners = (device + every[which]) % ndev
        target = owners * TO + recv_tile[owners, which, within]
        return total.at[target].add(slots), None

    coarse, _ = lax.scan(one_device, jnp.zeros((ndev * TO, B * B), jnp.float32), sources)
    return coarse
```

```python
import jax
import jax.numpy as jnp
from jax import lax
from jax.experimental import pallas as pl
from jax.experimental.pallas import tpu as pltpu
from jax.sharding import PartitionSpec as P

B = 64
KA = 7
KP = 2
S = 2
CAP = 4
TO = 8
R = 32
N = 128
RING = 4
LANES = 128
TILE_ROWS = B * B // LANES
OWNER_ROWS = TO * TILE_ROWS
EXT = R + N * S
MESH = pl.DeviceIdType.MESH

GROUPS = ((0, 88), (88, 88), (176, 80))
ORDERS = ((0, 1, 2), (1, 2, 0), (2, 0, 1))


def serve_kernel(index_ref, rows_ref, out_ref, sem):
    def send(n, carry):
        pltpu.make_async_copy(rows_ref.at[index_ref[n]], out_ref.at[n], sem).start()
        return carry

    lax.fori_loop(0, N * S, send, 0)
    pltpu.make_async_copy(out_ref, out_ref, sem).wait()


def split(value):
    high = value.astype(jnp.bfloat16)
    low = (value - high.astype(jnp.float32)).astype(jnp.bfloat16)
    return high, low


def left_kernel(count_ref, p_ref, a_ref, out_ref):
    row = pl.program_id(0)
    high, low = split(p_ref[0].T)
    left = jnp.concatenate([high, low], axis=1)
    lane = lax.broadcasted_iota(jnp.int32, (KP * B, LANES), 1)
    for k in range(KA):
        a_high, a_low = split(a_ref[0, k])
        wide = jnp.concatenate([a_high, a_low], axis=1)
        both = jnp.dot(left, jnp.concatenate([wide, wide], axis=0), preferred_element_type=jnp.float32)
        twice = both + pltpu.roll(both, B, 1)
        twice = jnp.where(row < count_ref[0], twice, 0.0)
        m_high = twice.astype(jnp.bfloat16).astype(jnp.float32)
        out_ref[0, k] = jnp.where(lane < B, m_high, twice - m_high).astype(jnp.bfloat16)


def tile_kernel(index_ref, slot_ref, table_ref, m_ref, own_ref, far_ref, out_ref, ext, acc, load_sem, out_sem):
    row = pl.program_id(0)

    @pl.when(row == 0)
    def _():
        own = pltpu.make_async_copy(own_ref, ext.at[pl.ds(0, R)], load_sem.at[0])
        far = pltpu.make_async_copy(far_ref, ext.at[pl.ds(R, N * S)], load_sem.at[1])
        own.start()
        far.start()

        def clear(n, carry):
            acc[pl.ds(n * 8, 8)] = jnp.zeros((8, TILE_ROWS, LANES), jnp.float32)
            return carry

        lax.fori_loop(0, N * TO // 8, clear, 0)
        own.wait()
        far.wait()

    lane = lax.broadcasted_iota(jnp.int32, (TILE_ROWS, LANES), 1)
    for k in range(KA):
        high, low = split(ext[index_ref[row * KA + k]])
        wide = jnp.concatenate([high, low], axis=1)
        both = jnp.dot(m_ref[0, k], jnp.concatenate([wide, wide], axis=0), preferred_element_type=jnp.float32)
        part = both[:, :LANES] + both[:, LANES:]
        turned = pltpu.roll(part, B, 1)
        for p in range(KP):
            top, bottom = p * B, p * B + TILE_ROWS
            upper, lower = part[top : top + TILE_ROWS], part[bottom : bottom + TILE_ROWS]
            upper_t, lower_t = turned[top : top + TILE_ROWS], turned[bottom : bottom + TILE_ROWS]
            tiles = (jnp.where(lane < B, upper, lower_t), jnp.where(lane < B, upper_t, lower))
            for q in range(KP):
                target = table_ref[slot_ref[row * (KP * KA * KP) + p * (KA * KP) + k * KP + q]]
                acc[target] += tiles[q]

    @pl.when(row == R - 1)
    def _():
        done = pltpu.make_async_copy(acc, out_ref, out_sem)
        done.start()
        done.wait()


def ring_shapes():
    shapes = []
    for _, length in GROUPS:
        for stage in range(3):
            lead = (RING,) * (2 - stage)
            slab = lead + (length, LANES)
            shapes += [pltpu.VMEM(slab, jnp.float32)] * 3
    return shapes


def add(target, *terms):
    lead = target.shape[:-2]
    total = 1
    for size in lead:
        total *= size

    def one(n, carry):
        at = []
        for size in reversed(lead):
            at.insert(0, n % size)
            n = n // size
        at = tuple(at) + (slice(None), slice(None))
        value = target[at]
        for term in terms:
            value = value + term[at]
        target[at] = value
        return carry

    if total == 1:
        one(0, 0)
    else:
        lax.fori_loop(0, total, one, 0)


def reduce_kernel(acc_ref, out_ref, mine, theirs, *rest):
    bufs, (in_send, in_recv, in_load, ring_send, ring_recv) = rest[:27], rest[27:]
    me = lax.axis_index("elem")
    core = me % 2
    chip = me // 2
    place = (chip // (RING * RING), (chip // RING) % RING, chip % RING)
    partner = me + 1 - 2 * core

    def device_at(axis, step):
        at = list(place)
        at[axis] = (at[axis] + step) % RING
        return ((at[0] * RING + at[1]) * RING + at[2]) * 2 + core

    barrier = pltpu.get_barrier_semaphore()
    near = [partner] + [device_at(axis, step) for axis in range(3) for step in (1, 3)]
    for other in near:
        pl.semaphore_signal(barrier, inc=1, device_id=(other,), device_id_type=MESH)
    pl.semaphore_wait(barrier, len(near))

    def window(group, fixed, part):
        free = [axis for axis in range(3) if axis not in fixed]
        at = [fixed.get(axis, slice(None)) for axis in range(3)]
        inner = [slice(None)] * len(free)
        first, length = GROUPS[group]
        rows = (0, length)
        if part is not None:
            if free:
                at[free[0]] = inner[0] = pl.ds(part * (RING // 2), RING // 2)
            else:
                half = (length + 8) // 16 * 8
                rows = (half * part, length - half if part else half)
        return (
            tuple(at) + (pl.ds(first + rows[0], rows[1]), slice(None)),
            tuple(inner) + (pl.ds(rows[0], rows[1]), slice(None)),
        )

    def across(group, fixed, core_at):
        at, _ = window(group, fixed, None)
        return at[:3] + (core_at,) + at[3:]

    loads = {}
    for offset in (2, 1, 3, 0):
        for group in range(3):
            axis = ORDERS[group][0]
            fixed = {axis: (place[axis] + offset) % RING}
            n = group * RING + offset
            at, _ = window(group, fixed, None)
            give = pltpu.make_async_remote_copy(
                src_ref=acc_ref.at[across(group, fixed, 1 - core)],
                dst_ref=theirs.at[at],
                send_sem=in_send.at[n],
                recv_sem=in_recv.at[n],
                device_id=(partner,),
                device_id_type=MESH,
            )
            keep = pltpu.make_async_copy(acc_ref.at[across(group, fixed, core)], mine.at[at], in_load.at[n])
            give.start()
            keep.start()
            loads[group, offset] = (give, keep, at)

    def arrive(group, offset):
        give, keep, at = loads[group, offset]
        keep.wait()
        give.wait_recv()
        add(mine.at[at], theirs.at[at])

    sends = [give for give, _, _ in loads.values()]
    flights = {}

    def fixed_at(group, stage, step):
        order = ORDERS[group]
        fixed = {axis: place[axis] for axis in order[:stage]}
        fixed[order[stage]] = (place[order[stage]] + step) % RING
        return fixed

    def start(group, stage, kind, step, part, towards, buffer):
        n = (group * 3 + stage) * 6 + kind
        at, inner = window(group, fixed_at(group, stage, step), part)
        copy = pltpu.make_async_remote_copy(
            src_ref=mine.at[at],
            dst_ref=bufs[(group * 3 + stage) * 3 + buffer].at[inner],
            send_sem=ring_send.at[n],
            recv_sem=ring_recv.at[n],
            device_id=(device_at(ORDERS[group][stage], towards),),
            device_id_type=MESH,
        )
        copy.start()
        flights[group, stage, kind] = copy
        sends.append(copy)

    def first_wave(group, stage):
        if stage == 0:
            arrive(group, 2)
        start(group, stage, 0, 2, 0, 1, 0)
        start(group, stage, 1, 2, 1, 3, 0)
        if stage == 0:
            arrive(group, 1)
        start(group, stage, 2, 1, 1, 1, 1)
        if stage == 0:
            arrive(group, 3)
        start(group, stage, 3, 3, 0, 3, 2)

    def second_wave(group, stage):
        buffer = bufs[(group * 3 + stage) * 3]
        for kind, part, step in ((0, 0, 1), (1, 1, 3)):
            flights[group, stage, kind].wait_recv()
            at, inner = window(group, fixed_at(group, stage, step), part)
            add(mine.at[at], buffer.at[inner])
            start(group, stage, 4 + kind, step, part, step, 1 + kind)

    def third_wave(group, stage):
        for kind in (2, 3, 4, 5):
            flights[group, stage, kind].wait_recv()
        at, _ = window(group, fixed_at(group, stage, 0), None)
        _, plus, minus = bufs[(group * 3 + stage) * 3 : (group * 3 + stage) * 3 + 3]
        if stage < 2:
            add(mine.at[at], plus, minus)
        else:
            first, length = GROUPS[group]
            out_ref[pl.ds(first, length), :] = mine[at] + plus[...] + minus[...]

    for group in range(3):
        first_wave(group, 0)
    for stage in range(3):
        for group in range(3):
            second_wave(group, stage)
        for group in range(3):
            if stage == 0:
                arrive(group, 0)
            third_wave(group, stage)
            if stage < 2:
                first_wave(group, stage + 1)
    for copy in sends:
        copy.wait_send()


def reduce_scatter(acc):
    return pl.pallas_call(
        reduce_kernel,
        out_shape=jax.ShapeDtypeStruct((OWNER_ROWS, LANES), jnp.float32),
        in_specs=[pl.BlockSpec(memory_space=pl.ANY)],
        out_specs=pl.BlockSpec(memory_space=pltpu.VMEM),
        scratch_shapes=[
            pltpu.VMEM((RING, RING, RING, OWNER_ROWS, LANES), jnp.float32),
            pltpu.VMEM((RING, RING, RING, OWNER_ROWS, LANES), jnp.float32),
            *ring_shapes(),
            pltpu.SemaphoreType.DMA((12,)),
            pltpu.SemaphoreType.DMA((12,)),
            pltpu.SemaphoreType.DMA((12,)),
            pltpu.SemaphoreType.DMA((54,)),
            pltpu.SemaphoreType.DMA((54,)),
        ],
        compiler_params=pltpu.CompilerParams(collective_id=0, has_side_effects=True, vmem_limit_bytes=48 * 2**20),
        name="reduce_scatter",
    )(acc.reshape(RING, RING, RING, 2, OWNER_ROWS, LANES))


def body(a_blocks, p_blocks, a_slot, serve_rows, row_count, contrib_slot, recv_tile):
    me = lax.axis_index("elem")
    every = jnp.arange(N, dtype=jnp.int32)
    rows = p_blocks.reshape(R, KP, B, B).transpose(0, 2, 1, 3).reshape(R, B, LANES)

    by_offset = jnp.concatenate([jnp.zeros((1, S), jnp.int32), serve_rows[0]], axis=0)
    serve_index = jnp.roll(by_offset, me, axis=0).reshape(N * S)
    outgoing = pl.pallas_call(
        serve_kernel,
        grid_spec=pltpu.PrefetchScalarGridSpec(
            num_scalar_prefetch=1,
            in_specs=[pl.BlockSpec(memory_space=pltpu.VMEM)],
            out_specs=pl.BlockSpec(memory_space=pl.ANY),
            scratch_shapes=[pltpu.SemaphoreType.DMA],
        ),
        out_shape=jax.ShapeDtypeStruct((N * S, B, LANES), jnp.float32),
        name="serve",
    )(serve_index, rows)
    arrived = lax.all_to_all(outgoing, "elem", split_axis=0, concat_axis=0, tiled=True)

    back = jnp.roll(recv_tile[0][::-1], me + 1, axis=0)
    told = lax.all_to_all(back, "elem", split_axis=0, concat_axis=0, tiled=True)
    table = jnp.roll(told + every[:, None] * TO, -me, axis=0).reshape(N * CAP)

    left = pl.pallas_call(
        left_kernel,
        grid_spec=pltpu.PrefetchScalarGridSpec(
            num_scalar_prefetch=1,
            grid=(R,),
            in_specs=[
                pl.BlockSpec((1, B, LANES), lambda i, c: (i, 0, 0)),
                pl.BlockSpec((1, KA, B, B), lambda i, c: (i, 0, 0, 0)),
            ],
            out_specs=pl.BlockSpec((1, KA, KP * B, LANES), lambda i, c: (i, 0, 0, 0)),
        ),
        out_shape=jax.ShapeDtypeStruct((R, KA, KP * B, LANES), jnp.bfloat16),
        cost_estimate=pl.CostEstimate(flops=4 * 2 * R * KA * 128 * 64 * 64, bytes_accessed=16 * 2**20, transcendentals=0),
        name="left_products",
    )(row_count, rows, a_blocks.reshape(R, KA, B, B))

    slot = a_slot.reshape(R * KA)
    source = lax.rem(me + (2 * N - 1) - (slot - R) // S, N)
    ext_index = jnp.where(slot < R, slot, R + source * S + (slot - R) % S)
    acc = pl.pallas_call(
        tile_kernel,
        grid_spec=pltpu.PrefetchScalarGridSpec(
            num_scalar_prefetch=3,
            grid=(R,),
            in_specs=[
                pl.BlockSpec((1, KA, KP * B, LANES), lambda i, a, b, c: (i, 0, 0, 0)),
                pl.BlockSpec(memory_space=pl.ANY),
                pl.BlockSpec(memory_space=pl.ANY),
            ],
            out_specs=pl.BlockSpec(memory_space=pl.ANY),
            scratch_shapes=[
                pltpu.VMEM((EXT, B, LANES), jnp.float32),
                pltpu.VMEM((N * TO, TILE_ROWS, LANES), jnp.float32),
                pltpu.SemaphoreType.DMA((2,)),
                pltpu.SemaphoreType.DMA,
            ],
        ),
        out_shape=jax.ShapeDtypeStruct((N * TO, TILE_ROWS, LANES), jnp.float32),
        compiler_params=pltpu.CompilerParams(vmem_limit_bytes=40 * 2**20),
        cost_estimate=pl.CostEstimate(flops=4 * 2 * R * KA * 128 * 64 * 128, bytes_accessed=34 * 2**20, transcendentals=0),
        name="tiles",
    )(ext_index, contrib_slot.reshape(-1), table, left, rows, arrived)

    tiles = reduce_scatter(acc)
    return tiles.reshape(TO, TILE_ROWS, 2, B).transpose(0, 2, 1, 3).reshape(TO, B * B)


def solution(mesh):
    in_specs = (
        P("elem", None, None),
        P("elem", None, None),
        P("elem", None),
        P("elem", None, None),
        P("elem"),
        P("elem", None),
        P("elem", None, None),
    )
    return jax.shard_map(body, mesh=mesh, in_specs=in_specs, out_specs=P("elem", None), check_vma=False)
```

```python
import jax
import jax.numpy as jnp
from jax import lax
from jax.experimental import pallas as pl
from jax.experimental.pallas import tpu as pltpu
from jax.sharding import PartitionSpec as P


B = 64
KA = 7
KP = 2
S = 2
CAP = 4
TO = 8
R = 32
N = 128
RING = 4
LANES = 128
TILE_ROWS = B * B // LANES
OWNER_ROWS = TO * TILE_ROWS
EXT = R + N * S
PARTS = 4
MESH = pl.DeviceIdType.MESH

GROUPS = ((0, 40), (40, 48), (88, 40), (128, 48), (176, 40), (216, 40))
ORDERS = ((0, 1, 2), (1, 2, 0), (2, 0, 1)) * 2
SETS = ((0, 1, 2), (3, 4, 5))


def serve_kernel(serve_ref, raw_ref, rows_ref, out_ref, sem):
    me = lax.axis_index("elem")
    lane = lax.broadcasted_iota(jnp.int32, (B, LANES), 1) < B
    even = lax.broadcasted_iota(jnp.int32, (B, LANES), 0) % 2 == 0

    def turn(n, carry):
        raw = raw_ref[n]
        halves = pltpu.roll(raw, B, 1)
        other = jnp.where(even, pltpu.roll(halves, B - 1, 0), pltpu.roll(halves, 1, 0))
        rows_ref[n] = jnp.where(lane == even, raw, other)
        return carry

    lax.fori_loop(0, R, turn, 0, unroll=4)

    def send(n, carry):
        to = lax.rem(me + 1 + n, N)
        for c in range(S):
            pltpu.make_async_copy(rows_ref.at[serve_ref[c, n]], out_ref.at[to * S + c], sem).start()
        return carry

    lax.fori_loop(0, N - 1, send, 0)
    for c in range(S):
        pltpu.make_async_copy(rows_ref.at[0], out_ref.at[me * S + c], sem).start()
    pltpu.make_async_copy(out_ref, out_ref, sem).wait()


def table_kernel(tiles_ref, out_ref, send_sem, recv_sem, own_sem):
    me = lax.axis_index("elem")

    def greet(m, carry):
        pl.semaphore_signal(barrier, inc=1, device_id=(lax.rem(me + m, N),), device_id_type=MESH)
        return carry

    def send(m, carry):
        pltpu.make_async_remote_copy(
            src_ref=tiles_ref.at[m],
            dst_ref=out_ref.at[m],
            send_sem=send_sem,
            recv_sem=recv_sem,
            device_id=(lax.rem(me + N - m, N),),
            device_id_type=MESH,
        ).start()
        return carry

    own = pltpu.make_async_copy(tiles_ref.at[0], out_ref.at[0], own_sem)
    own.start()
    barrier = pltpu.get_barrier_semaphore()
    lax.fori_loop(1, N, greet, 0)
    pl.semaphore_wait(barrier, N - 1)
    lax.fori_loop(1, N, send, 0)
    own.wait()
    rest = pl.ds(1, N - 1)
    pltpu.make_async_copy(tiles_ref.at[rest], tiles_ref.at[rest], send_sem).wait()
    pltpu.make_async_copy(out_ref.at[rest], out_ref.at[rest], recv_sem).wait()


def split(value):
    high = value.astype(jnp.bfloat16)
    low = (value - high.astype(jnp.float32)).astype(jnp.bfloat16)
    return high, low


def left_kernel(count_ref, p_ref, a_ref, out_ref):
    row = pl.program_id(0)
    high, low = split(p_ref[row].T)
    left = jnp.concatenate([high, low], axis=1)
    lane = lax.broadcasted_iota(jnp.int32, (KP * B, LANES), 1)
    for k in range(KA):
        a_high, a_low = split(a_ref[0, k])
        wide = jnp.concatenate([a_high, a_low], axis=1)
        both = jnp.dot(left, jnp.concatenate([wide, wide], axis=0), preferred_element_type=jnp.float32)
        twice = both + pltpu.roll(both, B, 1)
        twice = jnp.where(row < count_ref[0], twice, 0.0)
        m_high = twice.astype(jnp.bfloat16).astype(jnp.float32)
        out_ref[0, k] = jnp.where(lane < B, m_high, twice - m_high).astype(jnp.bfloat16)


def tile_kernel(index_ref, slot_ref, table_ref, left_ref, own_ref, far_ref, acc, ext, m_ref, load_sem, left_sem):
    own = pltpu.make_async_copy(own_ref, ext.at[pl.ds(0, R)], load_sem.at[0])
    far = pltpu.make_async_copy(far_ref, ext.at[pl.ds(R, N * S)], load_sem.at[1])
    far.start()
    own.start()
    parts = []
    for n in range(PARTS):
        some = pl.ds(n * (R // PARTS), R // PARTS)
        parts.append(pltpu.make_async_copy(left_ref.at[some], m_ref.at[some], left_sem.at[n]))
        parts[n].start()

    def clear(n, carry):
        acc[pl.ds(n * 8, 8)] = jnp.zeros((8, TILE_ROWS, LANES), jnp.float32)
        return carry

    lax.fori_loop(0, N * TO // 8, clear, 0)
    own.wait()
    far.wait()
    lane = lax.broadcasted_iota(jnp.int32, (TILE_ROWS, LANES), 1)

    def step(row, carry):
        for k in range(KA):
            high, low = split(ext[index_ref[row * KA + k]])
            wide = jnp.concatenate([high, low], axis=1)
            both = jnp.dot(m_ref[row, k], jnp.concatenate([wide, wide], axis=0), preferred_element_type=jnp.float32)
            part = both[:, :LANES] + both[:, LANES:]
            turned = pltpu.roll(part, B, 1)
            for p in range(KP):
                top, bottom = p * B, p * B + TILE_ROWS
                upper, lower = part[top : top + TILE_ROWS], part[bottom : bottom + TILE_ROWS]
                upper_t, lower_t = turned[top : top + TILE_ROWS], turned[bottom : bottom + TILE_ROWS]
                tiles = (jnp.where(lane < B, upper, lower_t), jnp.where(lane < B, upper_t, lower))
                for q in range(KP):
                    target = table_ref[slot_ref[row * (KP * KA * KP) + p * (KA * KP) + k * KP + q]]
                    acc[target] += tiles[q]
        return carry

    for n in range(PARTS):
        parts[n].wait()
        lax.fori_loop(n * (R // PARTS), (n + 1) * (R // PARTS), step, 0)


def ring_shapes():
    shapes = []
    for _, length in GROUPS:
        for stage in range(3):
            lead = (RING,) * (2 - stage)
            slab = lead + (length, LANES)
            shapes += [pltpu.VMEM(slab, jnp.float32)] * 3
    return shapes


def add(target, *terms):
    lead = target.shape[:-2]
    total = 1
    for size in lead:
        total *= size

    def one(n, carry):
        at = []
        for size in reversed(lead):
            at.insert(0, n % size)
            n = n // size
        at = tuple(at) + (slice(None), slice(None))
        value = target[at]
        for term in terms:
            value = value + term[at]
        target[at] = value
        return carry

    if total == 1:
        one(0, 0)
    else:
        lax.fori_loop(0, total, one, 0)


def reduce_kernel(acc_ref, out_ref, mine, *rest):
    bufs, (in_send, in_recv, ring_send, ring_recv) = rest[:-4], rest[-4:]
    me = lax.axis_index("elem")
    core = me % 2
    chip = me // 2
    place = (chip // (RING * RING), (chip // RING) % RING, chip % RING)
    partner = me + 1 - 2 * core

    def device_at(axis, step):
        at = list(place)
        at[axis] = (at[axis] + step) % RING
        return ((at[0] * RING + at[1]) * RING + at[2]) * 2 + core

    barrier = pltpu.get_barrier_semaphore()
    near = [partner] + [device_at(axis, step) for axis in range(3) for step in (1, 3)]
    for other in near:
        pl.semaphore_signal(barrier, inc=1, device_id=(other,), device_id_type=MESH)
    pl.semaphore_wait(barrier, len(near))

    def window(group, fixed, part):
        free = [axis for axis in range(3) if axis not in fixed]
        at = [fixed.get(axis, slice(None)) for axis in range(3)]
        inner = [slice(None)] * len(free)
        first, length = GROUPS[group]
        rows = (0, length)
        if part is not None:
            if free:
                at[free[0]] = inner[0] = pl.ds(part * (RING // 2), RING // 2)
            else:
                half = (length + 8) // 16 * 8
                rows = (half * part, length - half if part else half)
        return (
            tuple(at) + (pl.ds(first + rows[0], rows[1]), slice(None)),
            tuple(inner) + (pl.ds(rows[0], rows[1]), slice(None)),
        )

    def across(group, fixed, core_at):
        at, _ = window(group, fixed, None)
        return at[:3] + (core_at,) + at[3:]

    loads = {}
    for groups, offset in ((0, 2), (0, 1), (0, 3), (1, 2), (1, 1), (1, 3), (0, 0), (1, 0)):
        for group in SETS[groups]:
            axis = ORDERS[group][0]
            fixed = {axis: (place[axis] + offset) % RING}
            n = group * RING + offset
            at, _ = window(group, fixed, None)
            give = pltpu.make_async_remote_copy(
                src_ref=acc_ref.at[across(group, fixed, 1 - core)],
                dst_ref=mine.at[at],
                send_sem=in_send.at[n],
                recv_sem=in_recv.at[n],
                device_id=(partner,),
                device_id_type=MESH,
            )
            give.start()
            loads[group, offset] = (give, acc_ref.at[across(group, fixed, core)], mine.at[at])

    def arrive(group, offset):
        give, own, target = loads[group, offset]
        give.wait_recv()
        add(target, own)

    sends = [give for give, _, _ in loads.values()]
    flights = {}

    def fixed_at(group, stage, step):
        order = ORDERS[group]
        fixed = {axis: place[axis] for axis in order[:stage]}
        fixed[order[stage]] = (place[order[stage]] + step) % RING
        return fixed

    def start(group, stage, kind, step, part, towards, buffer):
        n = (group * 3 + stage) * 6 + kind
        at, inner = window(group, fixed_at(group, stage, step), part)
        copy = pltpu.make_async_remote_copy(
            src_ref=mine.at[at],
            dst_ref=bufs[(group * 3 + stage) * 3 + buffer].at[inner],
            send_sem=ring_send.at[n],
            recv_sem=ring_recv.at[n],
            device_id=(device_at(ORDERS[group][stage], towards),),
            device_id_type=MESH,
        )
        copy.start()
        flights[group, stage, kind] = copy
        sends.append(copy)

    def first_wave(group, stage):
        if stage == 0:
            arrive(group, 2)
        start(group, stage, 0, 2, 0, 1, 0)
        start(group, stage, 1, 2, 1, 3, 0)
        if stage == 0:
            arrive(group, 1)
        start(group, stage, 2, 1, 1, 1, 1)
        if stage == 0:
            arrive(group, 3)
        start(group, stage, 3, 3, 0, 3, 2)

    def second_wave(group, stage):
        buffer = bufs[(group * 3 + stage) * 3]
        for kind, part, step in ((0, 0, 1), (1, 1, 3)):
            flights[group, stage, kind].wait_recv()
            at, inner = window(group, fixed_at(group, stage, step), part)
            add(mine.at[at], buffer.at[inner])
            start(group, stage, 4 + kind, step, part, step, 1 + kind)

    def third_wave(group, stage):
        for kind in (2, 3, 4, 5):
            flights[group, stage, kind].wait_recv()
        at, _ = window(group, fixed_at(group, stage, 0), None)
        _, plus, minus = bufs[(group * 3 + stage) * 3 : (group * 3 + stage) * 3 + 3]
        if stage < 2:
            add(mine.at[at], plus, minus)
        else:
            first, length = GROUPS[group]
            out_ref[pl.ds(first, length), :] = mine[at] + plus[...] + minus[...]

    for groups in SETS:
        for group in groups:
            first_wave(group, 0)
    for stage in range(3):
        for groups in SETS:
            for group in groups:
                second_wave(group, stage)
        for groups in SETS:
            for group in groups:
                if stage == 0:
                    arrive(group, 0)
                third_wave(group, stage)
                if stage < 2:
                    first_wave(group, stage + 1)
    for copy in sends:
        copy.wait_send()


def reduce_scatter(acc):
    return pl.pallas_call(
        reduce_kernel,
        out_shape=jax.ShapeDtypeStruct((OWNER_ROWS, LANES), jnp.float32),
        in_specs=[pl.BlockSpec(memory_space=pltpu.VMEM)],
        out_specs=pl.BlockSpec(memory_space=pltpu.VMEM),
        scratch_shapes=[
            pltpu.VMEM((RING, RING, RING, OWNER_ROWS, LANES), jnp.float32),
            *ring_shapes(),
            pltpu.SemaphoreType.DMA((RING * len(GROUPS),)),
            pltpu.SemaphoreType.DMA((RING * len(GROUPS),)),
            pltpu.SemaphoreType.DMA((18 * len(GROUPS),)),
            pltpu.SemaphoreType.DMA((18 * len(GROUPS),)),
        ],
        compiler_params=pltpu.CompilerParams(collective_id=0, has_side_effects=True, vmem_limit_bytes=24 * 2**20),
        name="reduce_scatter",
    )(acc.reshape(RING, RING, RING, 2, OWNER_ROWS, LANES))


def body(a_blocks, p_blocks, a_slot, serve_rows, row_count, contrib_slot, recv_tile):
    me = lax.axis_index("elem")
    every = jnp.arange(N, dtype=jnp.int32)
    raw = p_blocks.reshape(R, KP, TILE_ROWS, LANES).transpose(0, 2, 1, 3).reshape(R, B, LANES)
    rows, outgoing = pl.pallas_call(
        serve_kernel,
        grid_spec=pltpu.PrefetchScalarGridSpec(
            num_scalar_prefetch=1,
            in_specs=[pl.BlockSpec(memory_space=pltpu.VMEM)],
            out_specs=(pl.BlockSpec(memory_space=pltpu.VMEM), pl.BlockSpec(memory_space=pltpu.HBM)),
            scratch_shapes=[pltpu.SemaphoreType.DMA],
        ),
        out_shape=(
            pltpu.VMEM((R, B, LANES), jnp.float32),
            pltpu.HBM((N * S, B, LANES), jnp.float32),
        ),
        compiler_params=pltpu.CompilerParams(vmem_limit_bytes=8 * 2**20),
        name="serve",
    )(serve_rows[0].T, raw)
    arrived = lax.all_to_all(outgoing, "elem", split_axis=0, concat_axis=0, tiled=True)

    mine = jnp.pad(recv_tile[0], ((0, 0), (0, LANES - CAP))).reshape(N, 1, LANES)
    told = pl.pallas_call(
        table_kernel,
        out_shape=jax.ShapeDtypeStruct((N, 1, LANES), jnp.int32),
        in_specs=[pl.BlockSpec(memory_space=pltpu.VMEM)],
        out_specs=pl.BlockSpec(memory_space=pltpu.VMEM),
        scratch_shapes=[pltpu.SemaphoreType.DMA] * 3,
        compiler_params=pltpu.CompilerParams(collective_id=1, has_side_effects=True, vmem_limit_bytes=4 * 2**20),
        cost_estimate=pl.CostEstimate(flops=0, bytes_accessed=2**20, transcendentals=0),
        name="table",
    )(mine)
    owner = lax.rem(me + every, N)
    table = (told[:, 0, :CAP] + owner[:, None] * TO).reshape(N * CAP)

    left = pl.pallas_call(
        left_kernel,
        grid_spec=pltpu.PrefetchScalarGridSpec(
            num_scalar_prefetch=1,
            grid=(R,),
            in_specs=[
                pl.BlockSpec(memory_space=pltpu.VMEM),
                pl.BlockSpec((1, KA, B, B), lambda i, c: (i, 0, 0, 0)),
            ],
            out_specs=pl.BlockSpec((1, KA, KP * B, LANES), lambda i, c: (i, 0, 0, 0), memory_space=pltpu.VMEM),
        ),
        out_shape=pltpu.HBM((R, KA, KP * B, LANES), jnp.bfloat16),
        compiler_params=pltpu.CompilerParams(vmem_limit_bytes=48 * 2**20),
        cost_estimate=pl.CostEstimate(flops=4 * 2 * R * KA * 128 * 64 * 64, bytes_accessed=16 * 2**20, transcendentals=0),
        name="left_products",
    )(row_count, rows, a_blocks.reshape(R, KA, B, B))

    slot = a_slot.reshape(R * KA)
    source = lax.rem(me + (2 * N - 1) - (slot - R) // S, N)
    ext_index = jnp.where(slot < R, slot, R + source * S + (slot - R) % S)
    acc = pl.pallas_call(
        tile_kernel,
        grid_spec=pltpu.PrefetchScalarGridSpec(
            num_scalar_prefetch=3,
            in_specs=[
                pl.BlockSpec(memory_space=pltpu.HBM),
                pl.BlockSpec(memory_space=pltpu.VMEM),
                pl.BlockSpec(memory_space=pltpu.HBM),
            ],
            out_specs=pl.BlockSpec(memory_space=pltpu.VMEM),
            scratch_shapes=[
                pltpu.VMEM((EXT, B, LANES), jnp.float32),
                pltpu.VMEM((R, KA, KP * B, LANES), jnp.bfloat16),
                pltpu.SemaphoreType.DMA((2,)),
                pltpu.SemaphoreType.DMA((PARTS,)),
            ],
        ),
        out_shape=pltpu.VMEM((N * TO, TILE_ROWS, LANES), jnp.float32),
        compiler_params=pltpu.CompilerParams(vmem_limit_bytes=42 * 2**20),
        cost_estimate=pl.CostEstimate(flops=4 * 2 * R * KA * 128 * 64 * 128, bytes_accessed=34 * 2**20, transcendentals=0),
        name="tiles",
    )(ext_index, contrib_slot.reshape(-1), table, left, rows, arrived)

    tiles = reduce_scatter(acc)
    return tiles.reshape(TO, TILE_ROWS, 2, B).transpose(0, 2, 1, 3).reshape(TO, B * B)


def solution(mesh):
    in_specs = (
        P("elem", None, None),
        P("elem", None, None),
        P("elem", None),
        P("elem", None, None),
        P("elem"),
        P("elem", None),
        P("elem", None, None),
    )

    return jax.shard_map(body, mesh=mesh, in_specs=in_specs, out_specs=P("elem", None), check_vma=False)
```

```python
import jax
import jax.numpy as jnp
from jax import lax
from jax.experimental import pallas as pl
from jax.experimental.pallas import tpu as pltpu
from jax.sharding import PartitionSpec as P


B = 64
KA = 7
KP = 2
S = 2
CAP = 4
TO = 8
R = 32
N = 128
RING = 4
LANES = 128
TILE_ROWS = B * B // LANES
OWNER_ROWS = TO * TILE_ROWS
EXT = R + N * S
PARTS = 4
MESH = pl.DeviceIdType.MESH

GROUPS = ((0, 40), (40, 48), (88, 40), (128, 48), (176, 40), (216, 40))
ORDERS = ((0, 1, 2), (1, 2, 0), (2, 0, 1)) * 2
SETS = ((0, 1, 2), (3, 4, 5))


def serve_kernel(serve_ref, raw_ref, rows_ref, out_ref, sem):
    me = lax.axis_index("elem")
    lane = lax.broadcasted_iota(jnp.int32, (B, LANES), 1) < B
    even = lax.broadcasted_iota(jnp.int32, (B, LANES), 0) % 2 == 0

    def turn(n, carry):
        raw = raw_ref[n]
        halves = pltpu.roll(raw, B, 1)
        other = jnp.where(even, pltpu.roll(halves, B - 1, 0), pltpu.roll(halves, 1, 0))
        rows_ref[n] = jnp.where(lane == even, raw, other)
        return carry

    lax.fori_loop(0, R, turn, 0, unroll=4)

    def send(n, carry):
        to = lax.rem(me + 1 + n, N)
        for c in range(S):
            pltpu.make_async_copy(rows_ref.at[serve_ref[c, n]], out_ref.at[to * S + c], sem).start()
        return carry

    lax.fori_loop(0, N - 1, send, 0)
    for c in range(S):
        pltpu.make_async_copy(rows_ref.at[0], out_ref.at[me * S + c], sem).start()
    pltpu.make_async_copy(out_ref, out_ref, sem).wait()


def table_kernel(tiles_ref, after_ref, out_ref, send_sem, recv_sem, own_sem):
    me = lax.axis_index("elem")

    def greet(m, carry):
        pl.semaphore_signal(barrier, inc=1, device_id=(lax.rem(me + m, N),), device_id_type=MESH)
        return carry

    def send(m, carry):
        pltpu.make_async_remote_copy(
            src_ref=tiles_ref.at[m],
            dst_ref=out_ref.at[m],
            send_sem=send_sem,
            recv_sem=recv_sem,
            device_id=(lax.rem(me + N - m, N),),
            device_id_type=MESH,
        ).start()
        return carry

    own = pltpu.make_async_copy(tiles_ref.at[0], out_ref.at[0], own_sem)
    own.start()
    barrier = pltpu.get_barrier_semaphore()
    lax.fori_loop(1, N, greet, 0)
    pl.semaphore_wait(barrier, N - 1)
    lax.fori_loop(1, N, send, 0)
    own.wait()
    rest = pl.ds(1, N - 1)
    pltpu.make_async_copy(tiles_ref.at[rest], tiles_ref.at[rest], send_sem).wait()
    pltpu.make_async_copy(out_ref.at[rest], out_ref.at[rest], recv_sem).wait()


def split(value):
    high = value.astype(jnp.bfloat16)
    low = (value - high.astype(jnp.float32)).astype(jnp.bfloat16)
    return high, low


def left_kernel(count_ref, p_ref, a_ref, out_ref):
    row = pl.program_id(0)
    high, low = split(p_ref[row].T)
    left = jnp.concatenate([high, low], axis=1)
    lane = lax.broadcasted_iota(jnp.int32, (KP * B, LANES), 1)
    for k in range(KA):
        a_high, a_low = split(a_ref[0, k])
        wide = jnp.concatenate([a_high, a_low], axis=1)
        both = jnp.dot(left, jnp.concatenate([wide, wide], axis=0), preferred_element_type=jnp.float32)
        twice = both + pltpu.roll(both, B, 1)
        twice = jnp.where(row < count_ref[0], twice, 0.0)
        m_high = twice.astype(jnp.bfloat16).astype(jnp.float32)
        out_ref[0, k] = jnp.where(lane < B, m_high, twice - m_high).astype(jnp.bfloat16)


def tile_kernel(index_ref, slot_ref, table_ref, left_ref, own_ref, far_ref, acc, ext, m_ref, load_sem, left_sem):
    own = pltpu.make_async_copy(own_ref, ext.at[pl.ds(0, R)], load_sem.at[0])
    far = pltpu.make_async_copy(far_ref, ext.at[pl.ds(R, N * S)], load_sem.at[1])
    far.start()
    own.start()
    parts = []
    for n in range(PARTS):
        some = pl.ds(n * (R // PARTS), R // PARTS)
        parts.append(pltpu.make_async_copy(left_ref.at[some], m_ref.at[some], left_sem.at[n]))
        parts[n].start()

    def clear(n, carry):
        acc[pl.ds(n * 8, 8)] = jnp.zeros((8, TILE_ROWS, LANES), jnp.float32)
        return carry

    lax.fori_loop(0, N * TO // 8, clear, 0)
    own.wait()
    far.wait()
    lane = lax.broadcasted_iota(jnp.int32, (TILE_ROWS, LANES), 1)

    def step(row, carry):
        for k in range(KA):
            high, low = split(ext[index_ref[row * KA + k]])
            wide = jnp.concatenate([high, low], axis=1)
            both = jnp.dot(m_ref[row, k], jnp.concatenate([wide, wide], axis=0), preferred_element_type=jnp.float32)
            part = both[:, :LANES] + both[:, LANES:]
            turned = pltpu.roll(part, B, 1)
            for p in range(KP):
                top, bottom = p * B, p * B + TILE_ROWS
                upper, lower = part[top : top + TILE_ROWS], part[bottom : bottom + TILE_ROWS]
                upper_t, lower_t = turned[top : top + TILE_ROWS], turned[bottom : bottom + TILE_ROWS]
                tiles = (jnp.where(lane < B, upper, lower_t), jnp.where(lane < B, upper_t, lower))
                for q in range(KP):
                    target = table_ref[slot_ref[row * (KP * KA * KP) + p * (KA * KP) + k * KP + q]]
                    acc[target] += tiles[q]
        return carry

    for n in range(PARTS):
        parts[n].wait()
        lax.fori_loop(n * (R // PARTS), (n + 1) * (R // PARTS), step, 0)


def ring_shapes():
    shapes = []
    for _, length in GROUPS:
        for stage in range(3):
            lead = (RING,) * (2 - stage)
            slab = lead + (length, LANES)
            shapes += [pltpu.VMEM(slab, jnp.float32)] * 3
    return shapes


def add(target, *terms):
    lead = target.shape[:-2]
    total = 1
    for size in lead:
        total *= size

    def one(n, carry):
        at = []
        for size in reversed(lead):
            at.insert(0, n % size)
            n = n // size
        at = tuple(at) + (slice(None), slice(None))
        value = target[at]
        for term in terms:
            value = value + term[at]
        target[at] = value
        return carry

    if total == 1:
        one(0, 0)
    else:
        lax.fori_loop(0, total, one, 0)


def reduce_kernel(acc_ref, out_ref, mine, *rest):
    bufs, (in_send, in_recv, ring_send, ring_recv) = rest[:-4], rest[-4:]
    me = lax.axis_index("elem")
    core = me % 2
    chip = me // 2
    place = (chip // (RING * RING), (chip // RING) % RING, chip % RING)
    partner = me + 1 - 2 * core

    def device_at(axis, step):
        at = list(place)
        at[axis] = (at[axis] + step) % RING
        return ((at[0] * RING + at[1]) * RING + at[2]) * 2 + core

    barrier = pltpu.get_barrier_semaphore()
    near = [partner] + [device_at(axis, step) for axis in range(3) for step in (1, 2, 3)]
    for other in near:
        pl.semaphore_signal(barrier, inc=1, device_id=(other,), device_id_type=MESH)
    pl.semaphore_wait(barrier, len(near))

    def window(group, fixed, part):
        free = [axis for axis in range(3) if axis not in fixed]
        at = [fixed.get(axis, slice(None)) for axis in range(3)]
        inner = [slice(None)] * len(free)
        first, length = GROUPS[group]
        rows = (0, length)
        if part is not None:
            if free:
                at[free[0]] = inner[0] = pl.ds(part * (RING // 2), RING // 2)
            else:
                half = (length + 8) // 16 * 8
                rows = (half * part, length - half if part else half)
        return (
            tuple(at) + (pl.ds(first + rows[0], rows[1]), slice(None)),
            tuple(inner) + (pl.ds(rows[0], rows[1]), slice(None)),
        )

    def across(group, fixed, core_at):
        at, _ = window(group, fixed, None)
        return at[:3] + (core_at,) + at[3:]

    loads = {}
    for groups, offset in ((0, 2), (0, 1), (0, 3), (1, 2), (1, 1), (1, 3), (0, 0), (1, 0)):
        for group in SETS[groups]:
            axis = ORDERS[group][0]
            fixed = {axis: (place[axis] + offset) % RING}
            n = group * RING + offset
            at, _ = window(group, fixed, None)
            give = pltpu.make_async_remote_copy(
                src_ref=acc_ref.at[across(group, fixed, 1 - core)],
                dst_ref=mine.at[at],
                send_sem=in_send.at[n],
                recv_sem=in_recv.at[n],
                device_id=(partner,),
                device_id_type=MESH,
            )
            give.start()
            loads[group, offset] = (give, acc_ref.at[across(group, fixed, core)], mine.at[at])

    def arrive(group, offset):
        give, own, target = loads[group, offset]
        give.wait_recv()
        add(target, own)

    sends = [give for give, _, _ in loads.values()]
    flights = {}

    def fixed_at(group, stage, step):
        order = ORDERS[group]
        fixed = {axis: place[axis] for axis in order[:stage]}
        fixed[order[stage]] = (place[order[stage]] + step) % RING
        return fixed

    def start(group, stage, kind, step, part, towards, buffer):
        n = (group * 3 + stage) * 6 + kind
        at, inner = window(group, fixed_at(group, stage, step), part)
        copy = pltpu.make_async_remote_copy(
            src_ref=mine.at[at],
            dst_ref=bufs[(group * 3 + stage) * 3 + buffer].at[inner],
            send_sem=ring_send.at[n],
            recv_sem=ring_recv.at[n],
            device_id=(device_at(ORDERS[group][stage], towards),),
            device_id_type=MESH,
        )
        copy.start()
        flights[group, stage, kind] = copy
        sends.append(copy)

    def first_wave(groups, stage):
        for step, sends_of in ((2, ((0, 0, 1, 0), (1, 1, 3, 0))), (1, ((2, 1, 1, 1),)), (3, ((3, 0, 3, 2),))):
            for group in groups:
                if stage == 0:
                    arrive(group, step)
                for kind, part, towards, buffer in sends_of:
                    start(group, stage, kind, step, part, towards, buffer)

    def last_wave(groups):
        for kind, step in ((1, 2), (0, 1), (2, 3)):
            for group in groups:
                start(group, 2, kind, step, None, step, kind)
        for group in groups:
            for kind in range(3):
                flights[group, 2, kind].wait_recv()
            at, _ = window(group, fixed_at(group, 2, 0), None)
            first, length = GROUPS[group]
            terms = bufs[(group * 3 + 2) * 3 : (group * 3 + 2) * 3 + 3]
            out_ref[pl.ds(first, length), :] = mine[at] + terms[0][...] + terms[1][...] + terms[2][...]

    def second_wave(group, stage):
        buffer = bufs[(group * 3 + stage) * 3]
        for kind, part, step in ((0, 0, 1), (1, 1, 3)):
            flights[group, stage, kind].wait_recv()
            at, inner = window(group, fixed_at(group, stage, step), part)
            add(mine.at[at], buffer.at[inner])
            start(group, stage, 4 + kind, step, part, step, 1 + kind)

    def third_wave(group, stage):
        for kind in (2, 3, 4, 5):
            flights[group, stage, kind].wait_recv()
        at, _ = window(group, fixed_at(group, stage, 0), None)
        _, plus, minus = bufs[(group * 3 + stage) * 3 : (group * 3 + stage) * 3 + 3]
        add(mine.at[at], plus, minus)

    for groups in SETS:
        first_wave(groups, 0)
    for stage in range(2):
        for groups in SETS:
            for group in groups:
                second_wave(group, stage)
        for groups in SETS:
            for group in groups:
                if stage == 0:
                    arrive(group, 0)
                third_wave(group, stage)
            if stage == 0:
                first_wave(groups, 1)
    for groups in SETS:
        last_wave(groups)
    for copy in sends:
        copy.wait_send()


def reduce_scatter(acc):
    return pl.pallas_call(
        reduce_kernel,
        out_shape=jax.ShapeDtypeStruct((OWNER_ROWS, LANES), jnp.float32),
        in_specs=[pl.BlockSpec(memory_space=pltpu.VMEM)],
        out_specs=pl.BlockSpec(memory_space=pltpu.VMEM),
        scratch_shapes=[
            pltpu.VMEM((RING, RING, RING, OWNER_ROWS, LANES), jnp.float32),
            *ring_shapes(),
            pltpu.SemaphoreType.DMA((RING * len(GROUPS),)),
            pltpu.SemaphoreType.DMA((RING * len(GROUPS),)),
            pltpu.SemaphoreType.DMA((18 * len(GROUPS),)),
            pltpu.SemaphoreType.DMA((18 * len(GROUPS),)),
        ],
        compiler_params=pltpu.CompilerParams(collective_id=0, has_side_effects=True, vmem_limit_bytes=24 * 2**20),
        name="reduce_scatter",
    )(acc.reshape(RING, RING, RING, 2, OWNER_ROWS, LANES))


def body(a_blocks, p_blocks, a_slot, serve_rows, row_count, contrib_slot, recv_tile):
    me = lax.axis_index("elem")
    every = jnp.arange(N, dtype=jnp.int32)
    raw = p_blocks.reshape(R, KP, TILE_ROWS, LANES).transpose(0, 2, 1, 3).reshape(R, B, LANES)
    rows, outgoing = pl.pallas_call(
        serve_kernel,
        grid_spec=pltpu.PrefetchScalarGridSpec(
            num_scalar_prefetch=1,
            in_specs=[pl.BlockSpec(memory_space=pltpu.VMEM)],
            out_specs=(pl.BlockSpec(memory_space=pltpu.VMEM), pl.BlockSpec(memory_space=pltpu.HBM)),
            scratch_shapes=[pltpu.SemaphoreType.DMA],
        ),
        out_shape=(
            pltpu.VMEM((R, B, LANES), jnp.float32),
            pltpu.HBM((N * S, B, LANES), jnp.float32),
        ),
        compiler_params=pltpu.CompilerParams(vmem_limit_bytes=8 * 2**20),
        name="serve",
    )(serve_rows[0].T, raw)
    arrived = lax.all_to_all(outgoing, "elem", split_axis=0, concat_axis=0, tiled=True)

    left = pl.pallas_call(
        left_kernel,
        grid_spec=pltpu.PrefetchScalarGridSpec(
            num_scalar_prefetch=1,
            grid=(R,),
            in_specs=[
                pl.BlockSpec(memory_space=pltpu.VMEM),
                pl.BlockSpec((1, KA, B, B), lambda i, c: (i, 0, 0, 0)),
            ],
            out_specs=pl.BlockSpec((1, KA, KP * B, LANES), lambda i, c: (i, 0, 0, 0), memory_space=pltpu.VMEM),
        ),
        out_shape=pltpu.HBM((R, KA, KP * B, LANES), jnp.bfloat16),
        compiler_params=pltpu.CompilerParams(vmem_limit_bytes=48 * 2**20),
        cost_estimate=pl.CostEstimate(flops=4 * 2 * R * KA * 128 * 64 * 64, bytes_accessed=16 * 2**20, transcendentals=0),
        name="left_products",
    )(row_count, rows, a_blocks.reshape(R, KA, B, B))

    mine = jnp.pad(recv_tile[0], ((0, 0), (0, LANES - CAP))).reshape(N, 1, LANES)
    told = pl.pallas_call(
        table_kernel,
        out_shape=jax.ShapeDtypeStruct((N, 1, LANES), jnp.int32),
        in_specs=[pl.BlockSpec(memory_space=pltpu.VMEM), pl.BlockSpec(memory_space=pltpu.HBM)],
        out_specs=pl.BlockSpec(memory_space=pltpu.VMEM),
        scratch_shapes=[pltpu.SemaphoreType.DMA] * 3,
        compiler_params=pltpu.CompilerParams(collective_id=1, has_side_effects=True, vmem_limit_bytes=58 * 2**20),
        cost_estimate=pl.CostEstimate(flops=0, bytes_accessed=2**20, transcendentals=0),
        name="table",
    )(mine, left)
    owner = lax.rem(me + every, N)
    table = (told[:, 0, :CAP] + owner[:, None] * TO).reshape(N * CAP)

    slot = a_slot.reshape(R * KA)
    source = lax.rem(me + (2 * N - 1) - (slot - R) // S, N)
    ext_index = jnp.where(slot < R, slot, R + source * S + (slot - R) % S)
    acc = pl.pallas_call(
        tile_kernel,
        grid_spec=pltpu.PrefetchScalarGridSpec(
            num_scalar_prefetch=3,
            in_specs=[
                pl.BlockSpec(memory_space=pltpu.HBM),
                pl.BlockSpec(memory_space=pltpu.VMEM),
                pl.BlockSpec(memory_space=pltpu.HBM),
            ],
            out_specs=pl.BlockSpec(memory_space=pltpu.VMEM),
            scratch_shapes=[
                pltpu.VMEM((EXT, B, LANES), jnp.float32),
                pltpu.VMEM((R, KA, KP * B, LANES), jnp.bfloat16),
                pltpu.SemaphoreType.DMA((2,)),
                pltpu.SemaphoreType.DMA((PARTS,)),
            ],
        ),
        out_shape=pltpu.VMEM((N * TO, TILE_ROWS, LANES), jnp.float32),
        compiler_params=pltpu.CompilerParams(vmem_limit_bytes=42 * 2**20),
        cost_estimate=pl.CostEstimate(flops=4 * 2 * R * KA * 128 * 64 * 128, bytes_accessed=34 * 2**20, transcendentals=0),
        name="tiles",
    )(ext_index, contrib_slot.reshape(-1), table, left, rows, arrived)

    tiles = reduce_scatter(acc)
    return tiles.reshape(TO, TILE_ROWS, 2, B).transpose(0, 2, 1, 3).reshape(TO, B * B)


def solution(mesh):
    in_specs = (
        P("elem", None, None),
        P("elem", None, None),
        P("elem", None),
        P("elem", None, None),
        P("elem"),
        P("elem", None),
        P("elem", None, None),
    )

    return jax.shard_map(body, mesh=mesh, in_specs=in_specs, out_specs=P("elem", None), check_vma=False)
```

```python
import jax
import jax.numpy as jnp
from jax import lax
from jax.experimental import pallas as pl
from jax.experimental.pallas import tpu as pltpu
from jax.sharding import PartitionSpec as P


B = 64
KA = 7
KP = 2
S = 2
CAP = 4
TO = 8
R = 32
N = 128
RING = 4
LANES = 128
TILE_ROWS = B * B // LANES
OWNER_ROWS = TO * TILE_ROWS
MESH = pl.DeviceIdType.MESH

GROUPS = ((0, 40), (40, 48), (88, 40), (128, 48), (176, 40), (216, 40))
ORDERS = ((0, 1, 2), (1, 2, 0), (2, 0, 1)) * 2
SETS = ((0, 1, 2), (3, 4, 5))


def split(value):
    high = value.astype(jnp.bfloat16)
    low = (value - high.astype(jnp.float32)).astype(jnp.bfloat16)
    return high, low


LINES = ((0, 24), (24, 24), (48, 16), (64, 16), (80, 24), (104, 24))
SHARES = (8, 8, 6, 6, 4)


def relay_shapes():
    return [pltpu.VMEM((RING, RING, length, LANES), jnp.float32) for _, length in LINES for _ in range(6)]


def exchange_kernel(serve_ref, count_ref, raw_ref, tiles_ref, a_hbm, rows_ref, far_ref, left_ref, told_ref, *rest):
    out, first_hop, second_hop, a_ref = rest[:4]
    relays = rest[4:40]
    send, recv, local, a_sem, told_send, told_recv, told_own = rest[40:]
    hops = (out, first_hop, second_hop, far_ref)
    me = lax.axis_index("elem")
    core = me % 2
    chip = me // 2
    place = (chip // (RING * RING), (chip // RING) % RING, chip % RING)

    def device_at(axis, step, core_at):
        at = list(place)
        at[axis] = (at[axis] + step) % RING
        return ((at[0] * RING + at[1]) * RING + at[2]) * 2 + core_at

    barrier = pltpu.get_barrier_semaphore()

    def greet(m, carry):
        pl.semaphore_signal(barrier, inc=1, device_id=(lax.rem(me + m, N),), device_id_type=MESH)
        return carry

    lax.fori_loop(1, N, greet, 0)
    a_copy = pltpu.make_async_copy(a_hbm, a_ref, a_sem)
    a_copy.start()
    own_tiles = pltpu.make_async_copy(tiles_ref.at[0], told_ref.at[0], told_own)
    own_tiles.start()

    lane = lax.broadcasted_iota(jnp.int32, (B, LANES), 1) < B
    even = lax.broadcasted_iota(jnp.int32, (B, LANES), 0) % 2 == 0

    def turn(n, carry):
        raw = raw_ref[n]
        halves = pltpu.roll(raw, B, 1)
        other = jnp.where(even, pltpu.roll(halves, B - 1, 0), pltpu.roll(halves, 1, 0))
        rows_ref[n] = jnp.where(lane == even, raw, other)
        return carry

    lax.fori_loop(0, R, turn, 0)

    def place_of(device):
        return device // (2 * RING * RING), (device // (2 * RING)) % RING, (device // 2) % RING, device % 2

    def gather(n, carry):
        y, x, z, k = place_of(lax.rem(me + 1 + n, N))
        for c in range(S):
            out[y, x, z, k, c * B : (c + 1) * B, :] = rows_ref[serve_ref[c, n]]
        return carry

    lax.fori_loop(0, N - 1, gather, 0)
    out[place[0], place[1], place[2], core] = jnp.zeros((S * B, LANES), jnp.float32)
    pl.semaphore_wait(barrier, N - 1)

    def tell(m, carry):
        pltpu.make_async_remote_copy(
            src_ref=tiles_ref.at[m],
            dst_ref=told_ref.at[m],
            send_sem=told_send,
            recv_sem=told_recv,
            device_id=(lax.rem(me + N - m, N),),
            device_id_type=MESH,
        ).start()
        return carry

    lax.fori_loop(1, N, tell, 0)

    def window(group, axis, at_axis, core_at):
        at = [slice(None)] * 3
        at[axis] = at_axis
        return tuple(at) + (slice(None) if core_at is None else core_at, pl.ds(*LINES[group]), slice(None))

    sent = []
    arrivals = {}

    def fly(group, phase, kind, source, target, device, lane_of=0):
        base = (group * 3 + phase) * 9
        copy = pltpu.make_async_remote_copy(
            src_ref=source,
            dst_ref=target,
            send_sem=send.at[base + kind],
            recv_sem=recv.at[base + lane_of],
            device_id=(device,),
            device_id_type=MESH,
        )
        copy.start()
        sent.append(copy)

    def land(group, phase, lane_of, like):
        pltpu.make_async_copy(like, like, recv.at[(group * 3 + phase) * 9 + lane_of]).wait()

    def first_wave(groups, phase):
        source, target = hops[phase], hops[phase + 1]
        for group in groups:
            axis = ORDERS[group][phase]
            u = place[axis]
            for part, step in ((0, 1), (1, 3)):
                relay = relays[(group * 3 + phase) * 2 + part]
                src = source.at[window(group, axis, (u + 2) % RING, part)]
                fly(group, phase, part, src, relay, device_at(axis, step, core), part)
        for side, step in ((0, 1), (1, 3)):
            for group in groups:
                axis = ORDERS[group][phase]
                u = place[axis]
                to = (u + step) % RING
                if phase < 2:
                    at = window(group, axis, u, None)
                    fly(group, phase, 2 + side, source.at[window(group, axis, to, None)], target.at[at], device_at(axis, step, core), 2 + side)
                else:
                    at = window(group, axis, u, core)
                    for part in range(2):
                        kind = 2 + 2 * side + part
                        src = source.at[window(group, axis, to, part)]
                        fly(group, phase, kind, src, target.at[at], device_at(axis, step, part), 2 + 2 * side + core)
        for group in groups:
            axis = ORDERS[group][phase]
            u = place[axis]
            at = window(group, axis, u, None if phase < 2 else core)
            keep = pltpu.make_async_copy(source.at[at], target.at[at], local.at[group * 3 + phase])
            keep.start()
            arrivals[group, phase] = keep
            if phase == 2:
                src = source.at[window(group, axis, u, 1 - core)]
                fly(group, phase, 8, src, target.at[at], device_at(axis, 0, 1 - core), 8)

    def second_wave(groups, phase):
        target = hops[phase + 1]
        for group in groups:
            axis = ORDERS[group][phase]
            u = place[axis]
            for part, step in ((0, 1), (1, 3)):
                relay = relays[(group * 3 + phase) * 2 + part]
                land(group, phase, part, relay)
                origin = (u + RING - step) % RING
                if phase < 2:
                    at = window(group, axis, origin, part)
                    fly(group, phase, 6 + part, relay, target.at[at], device_at(axis, step, core), 6 + part)
                else:
                    at = window(group, axis, origin, core)
                    fly(group, phase, 6 + part, relay, target.at[at], device_at(axis, step, part), 6 + core)

    def third_wave(groups, phase):
        target = hops[phase + 1]
        for group in groups:
            axis = ORDERS[group][phase]
            u = place[axis]
            arrivals[group, phase].wait()
            for side in range(2):
                if phase < 2:
                    land(group, phase, 2 + side, target.at[window(group, axis, u, None)])
                else:
                    land(group, phase, 2 + 2 * side, target.at[window(group, axis, u, core)])
                    land(group, phase, 3 + 2 * side, target.at[window(group, axis, u, core)])
            land(group, phase, 6, target.at[window(group, axis, u, core)])
            land(group, phase, 7, target.at[window(group, axis, u, core)])
            if phase == 2:
                land(group, phase, 8, target.at[window(group, axis, u, core)])

    def left_row(row, carry):
        low_half = lax.broadcasted_iota(jnp.int32, (TILE_ROWS, LANES), 1) < B
        stack = [rows_ref[row, pl.ds(h, TILE_ROWS, stride=2), :] for h in range(2)]
        high, low = split(jnp.concatenate(stack, axis=0).T)
        factor = jnp.concatenate([high, low], axis=1)
        for k in range(KA):
            block = a_ref[k * (R // 8) + row // 8, pl.ds(row % 8, TILE_ROWS, stride=8), :]
            turned = pltpu.roll(block, B, 1)
            value = jnp.concatenate([jnp.where(low_half, block, turned), jnp.where(low_half, turned, block)], axis=0)
            top = value.astype(jnp.bfloat16).astype(jnp.float32)
            wide = jnp.where(lane, top, value - top).astype(jnp.bfloat16)
            both = jnp.dot(factor, jnp.concatenate([wide, wide], axis=0), preferred_element_type=jnp.float32)
            twice = both + pltpu.roll(both, B, 1)
            m_high = twice.astype(jnp.bfloat16).astype(jnp.float32)
            wide_lane = lax.broadcasted_iota(jnp.int32, (KP * B, LANES), 1) < B
            left_ref[row, k] = jnp.where(wide_lane, m_high, twice - m_high).astype(jnp.bfloat16)
        return carry

    def left_share(n):
        done = sum(SHARES[:n])
        lax.fori_loop(done, done + SHARES[n], left_row, 0)

    for groups in SETS:
        first_wave(groups, 0)
    a_copy.wait()
    left_share(0)
    for phase in range(3):
        for groups in SETS:
            second_wave(groups, phase)
        if phase < 2:
            left_share(2 * phase + 1)
        for groups in SETS:
            third_wave(groups, phase)
            if phase < 2:
                first_wave(groups, phase + 1)
        if phase < 2:
            left_share(2 * phase + 2)
    own_tiles.wait()
    others = pl.ds(1, N - 1)
    pltpu.make_async_copy(tiles_ref.at[others], tiles_ref.at[others], told_send).wait()
    pltpu.make_async_copy(told_ref.at[others], told_ref.at[others], told_recv).wait()
    for copy in sent:
        copy.wait_send()


def tile_kernel(count_ref, row_ref, slot_ref, left_ref, own_ref, far_ref, told_ref, acc, told, told_sem):
    me = lax.axis_index("elem")
    told_copy = pltpu.make_async_copy(told_ref, told, told_sem)
    told_copy.start()

    def clear(n, carry):
        acc[pl.ds(n * 8, 8)] = jnp.zeros((8, TILE_ROWS, LANES), jnp.float32)
        return carry

    lax.fori_loop(0, N * TO // 8, clear, 0)
    told_copy.wait()
    lane = lax.broadcasted_iota(jnp.int32, (TILE_ROWS, LANES), 1)

    def step(row, carry):
        for k in range(KA):
            index = row_ref[k, row]
            away = jnp.maximum(index - R, 0)
            own = own_ref[jnp.minimum(index, R - 1)]
            far = far_ref[((me + 2 * N - 1 - away // S) % N) * S + away % S]
            high, low = split(jnp.where(index < R, own, far))
            wide = jnp.concatenate([high, low], axis=1)
            both = jnp.dot(left_ref[row, k], jnp.concatenate([wide, wide], axis=0), preferred_element_type=jnp.float32)
            part = both[:, :LANES] + both[:, LANES:]
            turned = pltpu.roll(part, B, 1)
            for p in range(KP):
                top, bottom = p * B, p * B + TILE_ROWS
                upper, lower = part[top : top + TILE_ROWS], part[bottom : bottom + TILE_ROWS]
                upper_t, lower_t = turned[top : top + TILE_ROWS], turned[bottom : bottom + TILE_ROWS]
                tiles = (jnp.where(lane < B, upper, lower_t), jnp.where(lane < B, upper_t, lower))
                for q in range(KP):
                    slot = slot_ref[row, p * (KA * KP) + k * KP + q]
                    position = slot // CAP
                    target = ((me + position) % N) * TO + told[position, 0, slot % CAP]
                    acc[target] += tiles[q]
        return carry

    lax.fori_loop(0, jnp.minimum(count_ref[0], R), step, 0)


def ring_shapes():
    shapes = []
    for _, length in GROUPS:
        for stage in range(3):
            lead = (RING,) * (2 - stage)
            slab = lead + (length, LANES)
            shapes += [pltpu.VMEM(slab, jnp.float32)] * 3
    return shapes


def add(target, *terms):
    lead = target.shape[:-2]
    total = 1
    for size in lead:
        total *= size

    def one(n, carry):
        at = []
        for size in reversed(lead):
            at.insert(0, n % size)
            n = n // size
        at = tuple(at) + (slice(None), slice(None))
        value = target[at]
        for term in terms:
            value = value + term[at]
        target[at] = value
        return carry

    if total == 1:
        one(0, 0)
    else:
        lax.fori_loop(0, total, one, 0)


def reduce_kernel(acc_ref, out_ref, mine, *rest):
    bufs, (in_send, in_recv, ring_send, ring_recv) = rest[:-4], rest[-4:]
    me = lax.axis_index("elem")
    core = me % 2
    chip = me // 2
    place = (chip // (RING * RING), (chip // RING) % RING, chip % RING)
    partner = me + 1 - 2 * core

    def device_at(axis, step):
        at = list(place)
        at[axis] = (at[axis] + step) % RING
        return ((at[0] * RING + at[1]) * RING + at[2]) * 2 + core

    barrier = pltpu.get_barrier_semaphore()
    near = [partner] + [device_at(axis, step) for axis in range(3) for step in (1, 2, 3)]
    for other in near:
        pl.semaphore_signal(barrier, inc=1, device_id=(other,), device_id_type=MESH)
    pl.semaphore_wait(barrier, len(near))

    def window(group, fixed, part):
        free = [axis for axis in range(3) if axis not in fixed]
        at = [fixed.get(axis, slice(None)) for axis in range(3)]
        inner = [slice(None)] * len(free)
        first, length = GROUPS[group]
        rows = (0, length)
        if part is not None:
            if free:
                at[free[0]] = inner[0] = pl.ds(part * (RING // 2), RING // 2)
            else:
                half = (length + 8) // 16 * 8
                rows = (half * part, length - half if part else half)
        return (
            tuple(at) + (pl.ds(first + rows[0], rows[1]), slice(None)),
            tuple(inner) + (pl.ds(rows[0], rows[1]), slice(None)),
        )

    def across(group, fixed, core_at):
        at, _ = window(group, fixed, None)
        return at[:3] + (core_at,) + at[3:]

    loads = {}
    for groups, offset in ((0, 2), (0, 1), (0, 3), (1, 2), (1, 1), (1, 3), (0, 0), (1, 0)):
        for group in SETS[groups]:
            axis = ORDERS[group][0]
            fixed = {axis: (place[axis] + offset) % RING}
            n = group * RING + offset
            at, _ = window(group, fixed, None)
            give = pltpu.make_async_remote_copy(
                src_ref=acc_ref.at[across(group, fixed, 1 - core)],
                dst_ref=mine.at[at],
                send_sem=in_send.at[n],
                recv_sem=in_recv.at[n],
                device_id=(partner,),
                device_id_type=MESH,
            )
            give.start()
            loads[group, offset] = (give, acc_ref.at[across(group, fixed, core)], mine.at[at])

    def arrive(group, offset):
        give, own, target = loads[group, offset]
        give.wait_recv()
        add(target, own)

    sends = [give for give, _, _ in loads.values()]
    flights = {}

    def fixed_at(group, stage, step):
        order = ORDERS[group]
        fixed = {axis: place[axis] for axis in order[:stage]}
        fixed[order[stage]] = (place[order[stage]] + step) % RING
        return fixed

    def start(group, stage, kind, step, part, towards, buffer):
        n = (group * 3 + stage) * 6 + kind
        at, inner = window(group, fixed_at(group, stage, step), part)
        copy = pltpu.make_async_remote_copy(
            src_ref=mine.at[at],
            dst_ref=bufs[(group * 3 + stage) * 3 + buffer].at[inner],
            send_sem=ring_send.at[n],
            recv_sem=ring_recv.at[n],
            device_id=(device_at(ORDERS[group][stage], towards),),
            device_id_type=MESH,
        )
        copy.start()
        flights[group, stage, kind] = copy
        sends.append(copy)

    def first_wave(groups, stage):
        for step, sends_of in ((2, ((0, 0, 1, 0), (1, 1, 3, 0))), (1, ((2, 1, 1, 1),)), (3, ((3, 0, 3, 2),))):
            for group in groups:
                if stage == 0:
                    arrive(group, step)
                for kind, part, towards, buffer in sends_of:
                    start(group, stage, kind, step, part, towards, buffer)

    def last_wave(groups):
        for kind, step in ((1, 2), (0, 1), (2, 3)):
            for group in groups:
                start(group, 2, kind, step, None, step, kind)
        for group in groups:
            for kind in range(3):
                flights[group, 2, kind].wait_recv()
            at, _ = window(group, fixed_at(group, 2, 0), None)
            first, length = GROUPS[group]
            terms = bufs[(group * 3 + 2) * 3 : (group * 3 + 2) * 3 + 3]
            out_ref[pl.ds(first, length), :] = mine[at] + terms[0][...] + terms[1][...] + terms[2][...]

    def second_wave(group, stage):
        buffer = bufs[(group * 3 + stage) * 3]
        for kind, part, step in ((0, 0, 1), (1, 1, 3)):
            flights[group, stage, kind].wait_recv()
            at, inner = window(group, fixed_at(group, stage, step), part)
            add(mine.at[at], buffer.at[inner])
            start(group, stage, 4 + kind, step, part, step, 1 + kind)

    def third_wave(group, stage):
        for kind in (2, 3, 4, 5):
            flights[group, stage, kind].wait_recv()
        at, _ = window(group, fixed_at(group, stage, 0), None)
        _, plus, minus = bufs[(group * 3 + stage) * 3 : (group * 3 + stage) * 3 + 3]
        add(mine.at[at], plus, minus)

    for groups in SETS:
        first_wave(groups, 0)
    for stage in range(2):
        for groups in SETS:
            for group in groups:
                second_wave(group, stage)
        for groups in SETS:
            for group in groups:
                if stage == 0:
                    arrive(group, 0)
                third_wave(group, stage)
            if stage == 0:
                first_wave(groups, 1)
    for groups in SETS:
        last_wave(groups)
    for copy in sends:
        copy.wait_send()


def reduce_scatter(acc):
    return pl.pallas_call(
        reduce_kernel,
        out_shape=jax.ShapeDtypeStruct((OWNER_ROWS, LANES), jnp.float32),
        in_specs=[pl.BlockSpec(memory_space=pltpu.VMEM)],
        out_specs=pl.BlockSpec(memory_space=pltpu.VMEM),
        scratch_shapes=[
            pltpu.VMEM((RING, RING, RING, OWNER_ROWS, LANES), jnp.float32),
            *ring_shapes(),
            pltpu.SemaphoreType.DMA((RING * len(GROUPS),)),
            pltpu.SemaphoreType.DMA((RING * len(GROUPS),)),
            pltpu.SemaphoreType.DMA((18 * len(GROUPS),)),
            pltpu.SemaphoreType.DMA((18 * len(GROUPS),)),
        ],
        compiler_params=pltpu.CompilerParams(collective_id=0, has_side_effects=True, vmem_limit_bytes=20 * 2**20),
        name="reduce_scatter",
    )(acc.reshape(RING, RING, RING, 2, OWNER_ROWS, LANES))


def body(a_blocks, p_blocks, a_slot, serve_rows, row_count, contrib_slot, recv_tile):
    raw = p_blocks.reshape(R, KP, TILE_ROWS, LANES).transpose(0, 2, 1, 3).reshape(R, B, LANES)
    a_native = a_blocks.transpose(1, 0, 2).reshape(KA, R // 8, 8, TILE_ROWS, LANES).transpose(0, 1, 3, 2, 4)
    tiles = jnp.pad(recv_tile[0], ((0, 0), (0, LANES - CAP))).reshape(N, 1, LANES)
    block = (RING, RING, RING, 2, S * B, LANES)
    vmem = pl.BlockSpec(memory_space=pltpu.VMEM)
    smem = pl.BlockSpec(memory_space=pltpu.SMEM)
    rows, far, left, told = pl.pallas_call(
        exchange_kernel,
        in_specs=[smem, smem, vmem, vmem, pl.BlockSpec(memory_space=pl.ANY)],
        out_specs=(vmem,) * 4,
        out_shape=(
            pltpu.VMEM((R, B, LANES), jnp.float32),
            pltpu.VMEM(block, jnp.float32),
            pltpu.VMEM((R, KA, KP * B, LANES), jnp.bfloat16),
            pltpu.VMEM((N, 1, LANES), jnp.int32),
        ),
        scratch_shapes=[
            pltpu.VMEM(block, jnp.float32),
            pltpu.VMEM(block, jnp.float32),
            pltpu.VMEM(block, jnp.float32),
            pltpu.VMEM((KA * R // 8, 8 * TILE_ROWS, LANES), jnp.float32),
            *relay_shapes(),
            pltpu.SemaphoreType.DMA((27 * len(LINES),)),
            pltpu.SemaphoreType.DMA((27 * len(LINES),)),
            pltpu.SemaphoreType.DMA((3 * len(LINES),)),
            *[pltpu.SemaphoreType.DMA] * 4,
        ],
        compiler_params=pltpu.CompilerParams(collective_id=1, has_side_effects=True, vmem_limit_bytes=37 * 2**20),
        name="exchange",
    )(serve_rows[0].T, row_count, raw, tiles, a_native.reshape(KA * R // 8, 8 * TILE_ROWS, LANES))
    acc = pl.pallas_call(
        tile_kernel,
        grid_spec=pltpu.PrefetchScalarGridSpec(
            num_scalar_prefetch=3,
            in_specs=[vmem] * 4,
            out_specs=vmem,
            scratch_shapes=[pltpu.SMEM((N, 1, LANES), jnp.int32), pltpu.SemaphoreType.DMA],
        ),
        out_shape=pltpu.VMEM((N * TO, TILE_ROWS, LANES), jnp.float32),
        compiler_params=pltpu.CompilerParams(vmem_limit_bytes=2 * 2**20),
        name="tiles",
    )(row_count, a_slot.T, contrib_slot, left, rows, far.reshape(N * S, B, LANES), told)

    summed = reduce_scatter(acc)
    return summed.reshape(TO, TILE_ROWS, 2, B).transpose(0, 2, 1, 3).reshape(TO, B * B)


def solution(mesh):
    in_specs = (
        P("elem", None, None),
        P("elem", None, None),
        P("elem", None),
        P("elem", None, None),
        P("elem"),
        P("elem", None),
        P("elem", None, None),
    )
    return jax.shard_map(body, mesh=mesh, in_specs=in_specs, out_specs=P("elem", None), check_vma=False)
```

```python
import jax
import jax.numpy as jnp
from jax import lax
from jax.experimental import pallas as pl
from jax.experimental.pallas import tpu as pltpu
from jax.sharding import PartitionSpec as P


B = 64
KA = 7
KP = 2
S = 2
CAP = 4
TO = 8
R = 32
N = 128
RING = 4
LANES = 128
TILE_ROWS = B * B // LANES
OWNER_ROWS = TO * TILE_ROWS
MESH = pl.DeviceIdType.MESH

GROUPS = ((0, 40), (40, 48), (88, 40), (128, 48), (176, 40), (216, 40))
ORDERS = ((0, 1, 2), (1, 2, 0), (2, 0, 1)) * 2
SETS = ((0, 1, 2), (3, 4, 5))
AHEAD = 6


def split(value):
    high = value.astype(jnp.bfloat16)
    low = (value - high.astype(jnp.float32)).astype(jnp.bfloat16)
    return high, low


LINES = ((0, 16), (16, 16), (32, 16), (48, 16), (64, 8), (72, 16), (88, 8), (96, 16), (112, 16))
LINE_ORDERS = ((0, 1, 2), (1, 2, 0), (2, 0, 1)) * 3
LINE_SETS = ((0, 1, 2), (3, 4, 5), (6, 7, 8))
SHARES = (8, 8, 6, 6, 4)


def relay_shapes():
    return [pltpu.VMEM((RING, RING, length, LANES), jnp.float32) for _, length in LINES for _ in range(6)]


def exchange_kernel(serve_ref, count_ref, raw_ref, tiles_ref, a_hbm, slot_hbm, row_hbm, rows_ref, far_ref, left_ref, told_ref, slot_ref, row_ref, *rest):
    out, first_hop, second_hop, a_ref, turned_ref, first_told, second_told, third_told = rest[:8]
    relays = rest[8:-7]
    send, recv, local, pass_sem, told_send, told_recv, told_local = rest[-7:]
    hops = (out, first_hop, second_hop, far_ref)
    me = lax.axis_index("elem")
    core = me % 2
    chip = me // 2
    place = (chip // (RING * RING), (chip // RING) % RING, chip % RING)

    def device_at(axis, step, core_at):
        at = list(place)
        at[axis] = (at[axis] + step) % RING
        return ((at[0] * RING + at[1]) * RING + at[2]) * 2 + core_at

    barrier = pltpu.get_barrier_semaphore()

    near = [device_at(0, 0, 1 - core)]
    near += [device_at(axis, step, k) for axis in range(3) for step in (1, 2, 3) for k in range(2)]
    for other in near:
        pl.semaphore_signal(barrier, inc=1, device_id=(other,), device_id_type=MESH)
    passing = [
        pltpu.make_async_copy(source, target, pass_sem.at[n])
        for n, (source, target) in enumerate(((a_hbm, a_ref), (slot_hbm, slot_ref), (row_hbm, row_ref)))
    ]
    for copy in passing:
        copy.start()

    lane = lax.broadcasted_iota(jnp.int32, (B, LANES), 1) < B
    even = lax.broadcasted_iota(jnp.int32, (B, LANES), 0) % 2 == 0

    def turn(n, carry):
        raw = raw_ref[n]
        halves = pltpu.roll(raw, B, 1)
        other = jnp.where(even, pltpu.roll(halves, B - 1, 0), pltpu.roll(halves, 1, 0))
        rows_ref[n] = jnp.where(lane == even, raw, other)
        return carry

    lax.fori_loop(0, R, turn, 0)
    turned_ref[...] = jnp.zeros((N, LANES), jnp.int32)
    turned_ref[0:CAP, :] = tiles_ref[...]
    turned_ref[...] = turned_ref[...].T

    def gather(n, carry):
        y, x = n // RING, n % RING
        for z in range(RING):
            for k in range(2):
                ahead = lax.rem(n * (2 * RING) + (2 * z + k) + N - me, N)
                for c in range(S):
                    out[y, x, z, k, c * B : (c + 1) * B, :] = rows_ref[serve_ref[c, lax.rem(ahead + N - 2, N - 1)]]
                first_told[y, x, z, k] = turned_ref[pl.ds(lax.rem(N - ahead, N), 1), :]
        return carry

    lax.fori_loop(0, RING * RING, gather, 0)
    pl.semaphore_wait(barrier, len(near))
    tolds = (first_told, second_told, third_told, told_ref)

    def tell(phase):
        source, target = tolds[phase], tolds[phase + 1]
        u = place[phase]

        def at(index, core_at=slice(None)):
            spot = [slice(None)] * 3
            spot[phase] = index
            return tuple(spot) + (core_at, slice(None), slice(None))

        flights = []
        for step in range(RING):
            for part in range(2 if phase == 2 else 1):
                to = (u + step) % RING
                if phase == 2:
                    src, dst = source.at[at(to, part)], target.at[at(u, core)]
                    device = device_at(phase, step, part)
                else:
                    src, dst = source.at[at(to)], target.at[at(u)]
                    device = device_at(phase, step, core)
                if phase == 2 and step == 0:
                    continue
                if step == 0:
                    copy = pltpu.make_async_copy(src, dst, told_local.at[phase])
                    copy.start()
                    told_waits.append((phase, copy.wait))
                    continue
                lane_of = phase * 8 + 2 * step + (core if phase == 2 else 0)
                copy = pltpu.make_async_remote_copy(
                    src_ref=src,
                    dst_ref=dst,
                    send_sem=told_send.at[phase * 8 + 2 * step + part],
                    recv_sem=told_recv.at[lane_of],
                    device_id=(device,),
                    device_id_type=MESH,
                )
                copy.start()
                sent.append(copy)
        if phase == 2:
            copy = pltpu.make_async_copy(source.at[at(u, core)], target.at[at(u, core)], told_local.at[2])
            copy.start()
            told_waits.append((phase, copy.wait))
            copy = pltpu.make_async_remote_copy(
                src_ref=source.at[at(u, 1 - core)],
                dst_ref=target.at[at(u, core)],
                send_sem=told_send.at[phase * 8],
                recv_sem=told_recv.at[phase * 8],
                device_id=(device_at(phase, 0, 1 - core),),
                device_id_type=MESH,
            )
            copy.start()
            sent.append(copy)

    def told_wait(phase):
        target = tolds[phase + 1]
        for at_phase, wait in told_waits:
            if at_phase == phase:
                wait()
        spot = [slice(None)] * 3
        spot[phase] = place[phase]
        lanes = (0, 2, 3, 4, 5, 6, 7) if phase == 2 else (2, 4, 6)
        like = target.at[tuple(spot) + ((core if phase == 2 else slice(None)), slice(None), slice(None))]
        for lane_of in lanes:
            pltpu.make_async_copy(like, like, told_recv.at[phase * 8 + lane_of]).wait()

    told_waits = []
    def window(group, axis, at_axis, core_at):
        at = [slice(None)] * 3
        at[axis] = at_axis
        return tuple(at) + (slice(None) if core_at is None else core_at, pl.ds(*LINES[group]), slice(None))

    sent = []
    arrivals = {}

    def fly(group, phase, kind, source, target, device, lane_of=0):
        base = (group * 3 + phase) * 9
        copy = pltpu.make_async_remote_copy(
            src_ref=source,
            dst_ref=target,
            send_sem=send.at[base + kind],
            recv_sem=recv.at[base + lane_of],
            device_id=(device,),
            device_id_type=MESH,
        )
        copy.start()
        sent.append(copy)

    def land(group, phase, lane_of, like):
        pltpu.make_async_copy(like, like, recv.at[(group * 3 + phase) * 9 + lane_of]).wait()

    def first_wave(groups, phase):
        source, target = hops[phase], hops[phase + 1]
        for group in groups:
            axis = LINE_ORDERS[group][phase]
            u = place[axis]
            for part, step in ((0, 1), (1, 3)):
                relay = relays[(group * 3 + phase) * 2 + part]
                src = source.at[window(group, axis, (u + 2) % RING, part)]
                fly(group, phase, part, src, relay, device_at(axis, step, core), part)
        for side, step in ((0, 1), (1, 3)):
            for group in groups:
                axis = LINE_ORDERS[group][phase]
                u = place[axis]
                to = (u + step) % RING
                if phase < 2:
                    at = window(group, axis, u, None)
                    fly(group, phase, 2 + side, source.at[window(group, axis, to, None)], target.at[at], device_at(axis, step, core), 2 + side)
                else:
                    at = window(group, axis, u, core)
                    for part in range(2):
                        kind = 2 + 2 * side + part
                        src = source.at[window(group, axis, to, part)]
                        fly(group, phase, kind, src, target.at[at], device_at(axis, step, part), 2 + 2 * side + core)
        for group in groups:
            axis = LINE_ORDERS[group][phase]
            u = place[axis]
            at = window(group, axis, u, None if phase < 2 else core)
            keep = pltpu.make_async_copy(source.at[at], target.at[at], local.at[group * 3 + phase])
            keep.start()
            arrivals[group, phase] = keep
            if phase == 2:
                src = source.at[window(group, axis, u, 1 - core)]
                fly(group, phase, 8, src, target.at[at], device_at(axis, 0, 1 - core), 8)

    def second_wave(groups, phase):
        target = hops[phase + 1]
        for group in groups:
            axis = LINE_ORDERS[group][phase]
            u = place[axis]
            for part, step in ((0, 1), (1, 3)):
                relay = relays[(group * 3 + phase) * 2 + part]
                land(group, phase, part, relay)
                origin = (u + RING - step) % RING
                if phase < 2:
                    at = window(group, axis, origin, part)
                    fly(group, phase, 6 + part, relay, target.at[at], device_at(axis, step, core), 6 + part)
                else:
                    at = window(group, axis, origin, core)
                    fly(group, phase, 6 + part, relay, target.at[at], device_at(axis, step, part), 6 + core)

    def third_wave(groups, phase):
        target = hops[phase + 1]
        for group in groups:
            axis = LINE_ORDERS[group][phase]
            u = place[axis]
            arrivals[group, phase].wait()
            for side in range(2):
                if phase < 2:
                    land(group, phase, 2 + side, target.at[window(group, axis, u, None)])
                else:
                    land(group, phase, 2 + 2 * side, target.at[window(group, axis, u, core)])
                    land(group, phase, 3 + 2 * side, target.at[window(group, axis, u, core)])
            land(group, phase, 6, target.at[window(group, axis, u, core)])
            land(group, phase, 7, target.at[window(group, axis, u, core)])
            if phase == 2:
                land(group, phase, 8, target.at[window(group, axis, u, core)])

    def left_row(row, carry):
        low_half = lax.broadcasted_iota(jnp.int32, (TILE_ROWS, LANES), 1) < B
        stack = [rows_ref[row, pl.ds(h, TILE_ROWS, stride=2), :] for h in range(2)]
        high, low = split(jnp.concatenate(stack, axis=0).T)
        factor = jnp.concatenate([high, low], axis=1)
        for k in range(KA):
            block = a_ref[k * (R // 8) + row // 8, pl.ds(row % 8, TILE_ROWS, stride=8), :]
            turned = pltpu.roll(block, B, 1)
            value = jnp.concatenate([jnp.where(low_half, block, turned), jnp.where(low_half, turned, block)], axis=0)
            top = value.astype(jnp.bfloat16).astype(jnp.float32)
            wide = jnp.where(lane, top, value - top).astype(jnp.bfloat16)
            both = jnp.dot(factor, jnp.concatenate([wide, wide], axis=0), preferred_element_type=jnp.float32)
            twice = both + pltpu.roll(both, B, 1)
            m_high = twice.astype(jnp.bfloat16).astype(jnp.float32)
            wide_lane = lax.broadcasted_iota(jnp.int32, (KP * B, LANES), 1) < B
            left_ref[row, k] = jnp.where(wide_lane, m_high, twice - m_high).astype(jnp.bfloat16)
        return carry

    def left_share(n):
        done = sum(SHARES[:n])
        lax.fori_loop(done, done + SHARES[n], left_row, 0)

    for groups in LINE_SETS:
        first_wave(groups, 0)
    tell(0)
    for copy in passing:
        copy.wait()
    left_share(0)
    for phase in range(3):
        for groups in LINE_SETS:
            second_wave(groups, phase)
        if phase < 2:
            left_share(2 * phase + 1)
        for groups in LINE_SETS:
            third_wave(groups, phase)
            if phase < 2:
                first_wave(groups, phase + 1)
        told_wait(phase)
        if phase < 2:
            tell(phase + 1)
            left_share(2 * phase + 2)
    for copy in sent:
        copy.wait_send()


def tile_kernel(count_ref, left_ref, own_ref, far_ref, told_in, slot_in, row_in, acc, told, slot_ref, row_ref, sem):
    me = lax.axis_index("elem")
    tables = [
        pltpu.make_async_copy(source, target, sem.at[n])
        for n, (source, target) in enumerate(((told_in, told), (slot_in, slot_ref), (row_in, row_ref)))
    ]
    for copy in tables:
        copy.start()

    def clear(n, carry):
        acc[pl.ds(n * 8, 8)] = jnp.zeros((8, TILE_ROWS, LANES), jnp.float32)
        return carry

    lax.fori_loop(0, N * TO // 8, clear, 0)
    for copy in tables:
        copy.wait()
    lane = lax.broadcasted_iota(jnp.int32, (TILE_ROWS, LANES), 1)

    def step(row, carry):
        for k in range(KA):
            index = row_ref[k, row]
            away = jnp.maximum(index - R, 0)
            own = own_ref[jnp.minimum(index, R - 1)]
            far = far_ref[lax.rem(me + 2 * N - 1 - lax.div(away, S), N) * S + lax.rem(away, S)]
            high, low = split(jnp.where(index < R, own, far))
            wide = jnp.concatenate([high, low], axis=1)
            both = jnp.dot(left_ref[row, k], jnp.concatenate([wide, wide], axis=0), preferred_element_type=jnp.float32)
            part = both[:, :LANES] + both[:, LANES:]
            turned = pltpu.roll(part, B, 1)
            for p in range(KP):
                top, bottom = p * B, p * B + TILE_ROWS
                upper, lower = part[top : top + TILE_ROWS], part[bottom : bottom + TILE_ROWS]
                upper_t, lower_t = turned[top : top + TILE_ROWS], turned[bottom : bottom + TILE_ROWS]
                tiles = (jnp.where(lane < B, upper, lower_t), jnp.where(lane < B, upper_t, lower))
                for q in range(KP):
                    slot = slot_ref[row, p * (KA * KP) + k * KP + q]
                    owner = lax.rem(me + lax.div(slot, CAP), N)
                    target = owner * TO + told[owner, 0, lax.rem(slot, CAP)]
                    acc[target] += tiles[q]
        return carry

    lax.fori_loop(0, jnp.minimum(count_ref[0], R), step, 0)


def ring_shapes():
    shapes = []
    for _, length in GROUPS:
        for stage in range(3):
            lead = (RING,) * (2 - stage)
            slab = lead + (length, LANES)
            shapes += [pltpu.VMEM(slab, jnp.float32)] * 3
    return shapes


def add(target, *terms):
    def one(at):
        value = target[at]
        for term in terms:
            value = value + term[at]
        target[at] = value

    lead = target.shape[:-2]
    whole = (slice(None), slice(None))
    if not lead:
        one(whole)
        return

    def outer(n, carry):
        if len(lead) == 1:
            one((n,) + whole)
        else:
            for m in range(lead[1]):
                one((n, m) + whole)
        return carry

    lax.fori_loop(0, lead[0], outer, 0)


def reduce_kernel(acc_ref, out_ref, mine, *rest):
    bufs, (in_send, in_recv, ring_send, ring_recv) = rest[:-4], rest[-4:]
    me = lax.axis_index("elem")
    core = me % 2
    chip = me // 2
    place = (chip // (RING * RING), (chip // RING) % RING, chip % RING)
    partner = me + 1 - 2 * core

    def device_at(axis, step):
        at = list(place)
        at[axis] = (at[axis] + step) % RING
        return ((at[0] * RING + at[1]) * RING + at[2]) * 2 + core

    barrier = pltpu.get_barrier_semaphore()
    near = [partner] + [device_at(axis, step) for axis in range(3) for step in (1, 2, 3)]
    for other in near:
        pl.semaphore_signal(barrier, inc=1, device_id=(other,), device_id_type=MESH)
    pl.semaphore_wait(barrier, len(near))

    def window(group, fixed, part):
        free = [axis for axis in range(3) if axis not in fixed]
        at = [fixed.get(axis, slice(None)) for axis in range(3)]
        inner = [slice(None)] * len(free)
        first, length = GROUPS[group]
        rows = (0, length)
        if part is not None:
            if free:
                at[free[0]] = inner[0] = pl.ds(part * (RING // 2), RING // 2)
            else:
                half = (length + 8) // 16 * 8
                rows = (half * part, length - half if part else half)
        return (
            tuple(at) + (pl.ds(first + rows[0], rows[1]), slice(None)),
            tuple(inner) + (pl.ds(rows[0], rows[1]), slice(None)),
        )

    def across(group, fixed, core_at):
        at, _ = window(group, fixed, None)
        return at[:3] + (core_at,) + at[3:]

    queue = [(n, step) for n in range(len(SETS)) for step in (2, 1, 3)] + [(n, 0) for n in range(len(SETS))]
    queue = [(group, step) for n, step in queue for group in SETS[n]]
    loads, sends = {}, []

    def fetch():
        if len(loads) == len(queue):
            return
        group, offset = queue[len(loads)]
        axis = ORDERS[group][0]
        fixed = {axis: (place[axis] + offset) % RING}
        n = group * RING + offset
        at, _ = window(group, fixed, None)
        give = pltpu.make_async_remote_copy(
            src_ref=acc_ref.at[across(group, fixed, 1 - core)],
            dst_ref=mine.at[at],
            send_sem=in_send.at[n],
            recv_sem=in_recv.at[n],
            device_id=(partner,),
            device_id_type=MESH,
        )
        give.start()
        loads[group, offset] = (give, acc_ref.at[across(group, fixed, core)], mine.at[at])
        sends.append(give)

    for _ in range(AHEAD):
        fetch()

    def arrive(group, offset):
        give, own, target = loads[group, offset]
        give.wait_recv()
        fetch()
        add(target, own)

    flights = {}

    def fixed_at(group, stage, step):
        order = ORDERS[group]
        fixed = {axis: place[axis] for axis in order[:stage]}
        fixed[order[stage]] = (place[order[stage]] + step) % RING
        return fixed

    def start(group, stage, kind, step, part, towards, buffer):
        n = (group * 3 + stage) * 6 + kind
        at, inner = window(group, fixed_at(group, stage, step), part)
        copy = pltpu.make_async_remote_copy(
            src_ref=mine.at[at],
            dst_ref=bufs[(group * 3 + stage) * 3 + buffer].at[inner],
            send_sem=ring_send.at[n],
            recv_sem=ring_recv.at[n],
            device_id=(device_at(ORDERS[group][stage], towards),),
            device_id_type=MESH,
        )
        copy.start()
        flights[group, stage, kind] = copy
        sends.append(copy)

    def first_wave(groups, stage):
        for step, sends_of in ((2, ((0, 0, 1, 0), (1, 1, 3, 0))), (1, ((2, 1, 1, 1),)), (3, ((3, 0, 3, 2),))):
            for group in groups:
                if stage == 0:
                    arrive(group, step)
                for kind, part, towards, buffer in sends_of:
                    start(group, stage, kind, step, part, towards, buffer)

    def last_wave(groups):
        for kind, step in ((1, 2), (0, 1), (2, 3)):
            for group in groups:
                start(group, 2, kind, step, None, step, kind)
        for group in groups:
            for kind in range(3):
                flights[group, 2, kind].wait_recv()
            at, _ = window(group, fixed_at(group, 2, 0), None)
            first, length = GROUPS[group]
            terms = bufs[(group * 3 + 2) * 3 : (group * 3 + 2) * 3 + 3]
            out_ref[pl.ds(first, length), :] = mine[at] + terms[0][...] + terms[1][...] + terms[2][...]

    def second_wave(group, stage):
        buffer = bufs[(group * 3 + stage) * 3]
        for kind, part, step in ((0, 0, 1), (1, 1, 3)):
            flights[group, stage, kind].wait_recv()
            at, inner = window(group, fixed_at(group, stage, step), part)
            add(mine.at[at], buffer.at[inner])
            start(group, stage, 4 + kind, step, part, step, 1 + kind)

    def third_wave(group, stage):
        for kind in (2, 3, 4, 5):
            flights[group, stage, kind].wait_recv()
        at, _ = window(group, fixed_at(group, stage, 0), None)
        _, plus, minus = bufs[(group * 3 + stage) * 3 : (group * 3 + stage) * 3 + 3]
        add(mine.at[at], plus, minus)

    for groups in SETS:
        first_wave(groups, 0)
    for stage in range(2):
        for groups in SETS:
            for group in groups:
                second_wave(group, stage)
        for groups in SETS:
            for group in groups:
                if stage == 0:
                    arrive(group, 0)
                third_wave(group, stage)
            if stage == 0:
                first_wave(groups, 1)
    for groups in SETS:
        last_wave(groups)
    for copy in sends:
        copy.wait_send()


def reduce_scatter(acc):
    return pl.pallas_call(
        reduce_kernel,
        out_shape=jax.ShapeDtypeStruct((OWNER_ROWS, LANES), jnp.float32),
        in_specs=[pl.BlockSpec(memory_space=pltpu.VMEM)],
        out_specs=pl.BlockSpec(memory_space=pltpu.VMEM),
        scratch_shapes=[
            pltpu.VMEM((RING, RING, RING, OWNER_ROWS, LANES), jnp.float32),
            *ring_shapes(),
            pltpu.SemaphoreType.DMA((RING * len(GROUPS),)),
            pltpu.SemaphoreType.DMA((RING * len(GROUPS),)),
            pltpu.SemaphoreType.DMA((18 * len(GROUPS),)),
            pltpu.SemaphoreType.DMA((18 * len(GROUPS),)),
        ],
        compiler_params=pltpu.CompilerParams(collective_id=0, has_side_effects=True, vmem_limit_bytes=20 * 2**20),
        name="reduce_scatter",
    )(acc.reshape(RING, RING, RING, 2, OWNER_ROWS, LANES))


def body(a_blocks, p_blocks, a_slot, serve_rows, row_count, contrib_slot, recv_tile):
    raw = p_blocks.reshape(R, KP, TILE_ROWS, LANES).transpose(0, 2, 1, 3).reshape(R, B, LANES)
    a_native = a_blocks.transpose(1, 0, 2).reshape(KA, R // 8, 8, TILE_ROWS, LANES).transpose(0, 1, 3, 2, 4)
    block = (RING, RING, RING, 2, S * B, LANES)
    told_block = (RING, RING, RING, 2, 1, LANES)
    vmem = pl.BlockSpec(memory_space=pltpu.VMEM)
    smem = pl.BlockSpec(memory_space=pltpu.SMEM)
    rows, far, left, told, slots, slot_rows = pl.pallas_call(
        exchange_kernel,
        in_specs=[smem, smem, vmem, vmem] + [pl.BlockSpec(memory_space=pl.ANY)] * 3,
        out_specs=(vmem,) * 6,
        out_shape=(
            pltpu.VMEM((R, B, LANES), jnp.float32),
            pltpu.VMEM(block, jnp.float32),
            pltpu.VMEM((R, KA, KP * B, LANES), jnp.bfloat16),
            pltpu.VMEM(told_block, jnp.int32),
            pltpu.VMEM((R, KP * KA * KP), jnp.int32),
            pltpu.VMEM((KA, R), jnp.int32),
        ),
        scratch_shapes=[
            pltpu.VMEM(block, jnp.float32),
            pltpu.VMEM(block, jnp.float32),
            pltpu.VMEM(block, jnp.float32),
            pltpu.VMEM((KA * R // 8, 8 * TILE_ROWS, LANES), jnp.float32),
            pltpu.VMEM((N, LANES), jnp.int32),
            *[pltpu.VMEM(told_block, jnp.int32)] * 3,
            *relay_shapes(),
            pltpu.SemaphoreType.DMA((27 * len(LINES),)),
            pltpu.SemaphoreType.DMA((27 * len(LINES),)),
            pltpu.SemaphoreType.DMA((3 * len(LINES),)),
            pltpu.SemaphoreType.DMA((3,)),
            pltpu.SemaphoreType.DMA((24,)),
            pltpu.SemaphoreType.DMA((24,)),
            pltpu.SemaphoreType.DMA((3,)),
        ],
        compiler_params=pltpu.CompilerParams(collective_id=1, has_side_effects=True, vmem_limit_bytes=50100000),
        name="exchange",
    )(serve_rows[0].T, row_count, raw, recv_tile[0].T, a_native.reshape(KA * R // 8, 8 * TILE_ROWS, LANES), contrib_slot, a_slot.T)
    acc = pl.pallas_call(
        tile_kernel,
        grid_spec=pltpu.PrefetchScalarGridSpec(
            num_scalar_prefetch=1,
            in_specs=[vmem] * 6,
            out_specs=vmem,
            scratch_shapes=[
                pltpu.SMEM((N, 1, LANES), jnp.int32),
                pltpu.SMEM((R, KP * KA * KP), jnp.int32),
                pltpu.SMEM((KA, R), jnp.int32),
                pltpu.SemaphoreType.DMA((3,)),
            ],
        ),
        out_shape=pltpu.VMEM((N * TO, TILE_ROWS, LANES), jnp.float32),
        compiler_params=pltpu.CompilerParams(vmem_limit_bytes=2 * 2**20),
        name="tiles",
    )(row_count, left, rows, far.reshape(N * S, B, LANES), told.reshape(N, 1, LANES), slots, slot_rows)

    summed = reduce_scatter(acc)
    return summed.reshape(TO, TILE_ROWS, 2, B).transpose(0, 2, 1, 3).reshape(TO, B * B)


def solution(mesh):
    in_specs = (
        P("elem", None, None),
        P("elem", None, None),
        P("elem", None),
        P("elem", None, None),
        P("elem"),
        P("elem", None),
        P("elem", None, None),
    )
    return jax.shard_map(body, mesh=mesh, in_specs=in_specs, out_specs=P("elem", None), check_vma=False)
```

```python
import jax
import jax.numpy as jnp
from jax import lax
from jax.experimental import pallas as pl
from jax.experimental.pallas import tpu as pltpu
from jax.sharding import PartitionSpec as P


B = 64
KA = 7
KP = 2
S = 2
CAP = 4
TO = 8
R = 32
N = 128
RING = 4
LANES = 128
TILE_ROWS = B * B // LANES
OWNER_ROWS = TO * TILE_ROWS
MESH = pl.DeviceIdType.MESH

GROUPS = ((0, 40), (40, 48), (88, 40), (128, 48), (176, 40), (216, 40))
ORDERS = ((0, 1, 2), (1, 2, 0), (2, 0, 1)) * 2
SETS = ((0, 1, 2), (3, 4, 5))
AHEAD = 6


def split(value):
    high = value.astype(jnp.bfloat16)
    low = (value - high.astype(jnp.float32)).astype(jnp.bfloat16)
    return high, low


LINES = ((0, 16), (16, 16), (32, 16), (48, 16), (64, 8), (72, 16), (88, 8), (96, 16), (112, 16))
LINE_ORDERS = ((0, 1, 2), (1, 2, 0), (2, 0, 1)) * 3
LINE_SETS = ((0, 1, 2), (3, 4, 5), (6, 7, 8))
SHARES = (8, 8, 6, 6, 4)


def relay_shapes():
    return [pltpu.VMEM((RING, RING, length, LANES), jnp.float32) for _, length in LINES for _ in range(6)]


def exchange_kernel(serve_ref, count_ref, raw_ref, tiles_ref, a_hbm, slot_hbm, row_hbm, rows_ref, far_ref, left_ref, told_ref, slot_ref, row_ref, *rest):
    out, first_hop, second_hop, a_ref, turned_ref, first_told, second_told, third_told = rest[:8]
    relays = rest[8:-7]
    send, recv, local, pass_sem, told_send, told_recv, told_local = rest[-7:]
    hops = (out, first_hop, second_hop, far_ref)
    me = lax.axis_index("elem")
    core = me % 2
    chip = me // 2
    place = (chip // (RING * RING), (chip // RING) % RING, chip % RING)

    def device_at(axis, step, core_at):
        at = list(place)
        at[axis] = (at[axis] + step) % RING
        return ((at[0] * RING + at[1]) * RING + at[2]) * 2 + core_at

    barrier = pltpu.get_barrier_semaphore()

    near = [device_at(0, 0, 1 - core)]
    near += [device_at(axis, step, k) for axis in range(3) for step in (1, 2, 3) for k in range(2)]
    for other in near:
        pl.semaphore_signal(barrier, inc=1, device_id=(other,), device_id_type=MESH)
    passing = [
        pltpu.make_async_copy(source, target, pass_sem.at[n])
        for n, (source, target) in enumerate(((a_hbm, a_ref), (slot_hbm, slot_ref), (row_hbm, row_ref)))
    ]
    for copy in passing:
        copy.start()

    lane = lax.broadcasted_iota(jnp.int32, (B, LANES), 1) < B
    even = lax.broadcasted_iota(jnp.int32, (B, LANES), 0) % 2 == 0

    def turn(n, carry):
        raw = raw_ref[n]
        halves = pltpu.roll(raw, B, 1)
        other = jnp.where(even, pltpu.roll(halves, B - 1, 0), pltpu.roll(halves, 1, 0))
        rows_ref[n] = jnp.where(lane == even, raw, other)
        return carry

    lax.fori_loop(0, R, turn, 0)
    turned_ref[...] = jnp.zeros((N, LANES), jnp.int32)
    turned_ref[0:CAP, :] = tiles_ref[...]
    turned_ref[...] = turned_ref[...].T

    def gather(n, carry):
        y, x = n // RING, n % RING
        for z in range(RING):
            for k in range(2):
                ahead = lax.rem(n * (2 * RING) + (2 * z + k) + N - me, N)
                for c in range(S):
                    out[y, x, z, k, c * B : (c + 1) * B, :] = rows_ref[serve_ref[c, lax.rem(ahead + N - 2, N - 1)]]
                first_told[y, x, z, k] = turned_ref[pl.ds(lax.rem(N - ahead, N), 1), :]
        return carry

    lax.fori_loop(0, RING * RING, gather, 0)
    pl.semaphore_wait(barrier, len(near))
    tolds = (first_told, second_told, third_told, told_ref)

    def tell(phase):
        source, target = tolds[phase], tolds[phase + 1]
        u = place[phase]

        def at(index, core_at=slice(None)):
            spot = [slice(None)] * 3
            spot[phase] = index
            return tuple(spot) + (core_at, slice(None), slice(None))

        flights = []
        for step in range(RING):
            for part in range(2 if phase == 2 else 1):
                to = (u + step) % RING
                if phase == 2:
                    src, dst = source.at[at(to, part)], target.at[at(u, core)]
                    device = device_at(phase, step, part)
                else:
                    src, dst = source.at[at(to)], target.at[at(u)]
                    device = device_at(phase, step, core)
                if phase == 2 and step == 0:
                    continue
                if step == 0:
                    copy = pltpu.make_async_copy(src, dst, told_local.at[phase])
                    copy.start()
                    told_waits.append((phase, copy.wait))
                    continue
                lane_of = phase * 8 + 2 * step + (core if phase == 2 else 0)
                copy = pltpu.make_async_remote_copy(
                    src_ref=src,
                    dst_ref=dst,
                    send_sem=told_send.at[phase * 8 + 2 * step + part],
                    recv_sem=told_recv.at[lane_of],
                    device_id=(device,),
                    device_id_type=MESH,
                )
                copy.start()
                sent.append(copy)
        if phase == 2:
            copy = pltpu.make_async_copy(source.at[at(u, core)], target.at[at(u, core)], told_local.at[2])
            copy.start()
            told_waits.append((phase, copy.wait))
            copy = pltpu.make_async_remote_copy(
                src_ref=source.at[at(u, 1 - core)],
                dst_ref=target.at[at(u, core)],
                send_sem=told_send.at[phase * 8],
                recv_sem=told_recv.at[phase * 8],
                device_id=(device_at(phase, 0, 1 - core),),
                device_id_type=MESH,
            )
            copy.start()
            sent.append(copy)

    def told_wait(phase):
        target = tolds[phase + 1]
        for at_phase, wait in told_waits:
            if at_phase == phase:
                wait()
        spot = [slice(None)] * 3
        spot[phase] = place[phase]
        lanes = (0, 2, 3, 4, 5, 6, 7) if phase == 2 else (2, 4, 6)
        like = target.at[tuple(spot) + ((core if phase == 2 else slice(None)), slice(None), slice(None))]
        for lane_of in lanes:
            pltpu.make_async_copy(like, like, told_recv.at[phase * 8 + lane_of]).wait()

    told_waits = []
    def window(group, axis, at_axis, core_at):
        at = [slice(None)] * 3
        at[axis] = at_axis
        return tuple(at) + (slice(None) if core_at is None else core_at, pl.ds(*LINES[group]), slice(None))

    sent = []
    arrivals = {}

    def fly(group, phase, kind, source, target, device, lane_of=0):
        base = (group * 3 + phase) * 9
        copy = pltpu.make_async_remote_copy(
            src_ref=source,
            dst_ref=target,
            send_sem=send.at[base + kind],
            recv_sem=recv.at[base + lane_of],
            device_id=(device,),
            device_id_type=MESH,
        )
        copy.start()
        sent.append(copy)

    def land(group, phase, lane_of, like):
        pltpu.make_async_copy(like, like, recv.at[(group * 3 + phase) * 9 + lane_of]).wait()

    def first_wave(groups, phase):
        source, target = hops[phase], hops[phase + 1]
        for group in groups:
            axis = LINE_ORDERS[group][phase]
            u = place[axis]
            for part, step in ((0, 1), (1, 3)):
                relay = relays[(group * 3 + phase) * 2 + part]
                src = source.at[window(group, axis, (u + 2) % RING, part)]
                fly(group, phase, part, src, relay, device_at(axis, step, core), part)
        for side, step in ((0, 1), (1, 3)):
            for group in groups:
                axis = LINE_ORDERS[group][phase]
                u = place[axis]
                to = (u + step) % RING
                if phase < 2:
                    at = window(group, axis, u, None)
                    fly(group, phase, 2 + side, source.at[window(group, axis, to, None)], target.at[at], device_at(axis, step, core), 2 + side)
                else:
                    at = window(group, axis, u, core)
                    for part in range(2):
                        kind = 2 + 2 * side + part
                        src = source.at[window(group, axis, to, part)]
                        fly(group, phase, kind, src, target.at[at], device_at(axis, step, part), 2 + 2 * side + core)
        for group in groups:
            axis = LINE_ORDERS[group][phase]
            u = place[axis]
            at = window(group, axis, u, None if phase < 2 else core)
            keep = pltpu.make_async_copy(source.at[at], target.at[at], local.at[group * 3 + phase])
            keep.start()
            arrivals[group, phase] = keep
            if phase == 2:
                src = source.at[window(group, axis, u, 1 - core)]
                fly(group, phase, 8, src, target.at[at], device_at(axis, 0, 1 - core), 8)

    def second_wave(groups, phase):
        target = hops[phase + 1]
        for group in groups:
            axis = LINE_ORDERS[group][phase]
            u = place[axis]
            for part, step in ((0, 1), (1, 3)):
                relay = relays[(group * 3 + phase) * 2 + part]
                land(group, phase, part, relay)
                origin = (u + RING - step) % RING
                if phase < 2:
                    at = window(group, axis, origin, part)
                    fly(group, phase, 6 + part, relay, target.at[at], device_at(axis, step, core), 6 + part)
                else:
                    at = window(group, axis, origin, core)
                    fly(group, phase, 6 + part, relay, target.at[at], device_at(axis, step, part), 6 + core)

    def third_wave(groups, phase):
        target = hops[phase + 1]
        for group in groups:
            axis = LINE_ORDERS[group][phase]
            u = place[axis]
            arrivals[group, phase].wait()
            for side in range(2):
                if phase < 2:
                    land(group, phase, 2 + side, target.at[window(group, axis, u, None)])
                else:
                    land(group, phase, 2 + 2 * side, target.at[window(group, axis, u, core)])
                    land(group, phase, 3 + 2 * side, target.at[window(group, axis, u, core)])
            land(group, phase, 6, target.at[window(group, axis, u, core)])
            land(group, phase, 7, target.at[window(group, axis, u, core)])
            if phase == 2:
                land(group, phase, 8, target.at[window(group, axis, u, core)])

    def left_row(row, carry):
        low_half = lax.broadcasted_iota(jnp.int32, (TILE_ROWS, LANES), 1) < B
        stack = [rows_ref[row, pl.ds(h, TILE_ROWS, stride=2), :] for h in range(2)]
        high, low = split(jnp.concatenate(stack, axis=0).T)
        factor = jnp.concatenate([high, low], axis=1)
        for k in range(KA):
            block = a_ref[k * (R // 8) + row // 8, pl.ds(row % 8, TILE_ROWS, stride=8), :]
            turned = pltpu.roll(block, B, 1)
            value = jnp.concatenate([jnp.where(low_half, block, turned), jnp.where(low_half, turned, block)], axis=0)
            top = value.astype(jnp.bfloat16).astype(jnp.float32)
            wide = jnp.where(lane, top, value - top).astype(jnp.bfloat16)
            both = jnp.dot(factor, jnp.concatenate([wide, wide], axis=0), preferred_element_type=jnp.float32)
            twice = both + pltpu.roll(both, B, 1)
            m_high = twice.astype(jnp.bfloat16).astype(jnp.float32)
            wide_lane = lax.broadcasted_iota(jnp.int32, (KP * B, LANES), 1) < B
            left_ref[row, k] = jnp.where(wide_lane, m_high, twice - m_high).astype(jnp.bfloat16)
        return carry

    def left_share(n):
        done = sum(SHARES[:n])
        lax.fori_loop(done, done + SHARES[n], left_row, 0)

    for groups in LINE_SETS:
        first_wave(groups, 0)
    tell(0)
    for copy in passing:
        copy.wait()
    left_share(0)
    for phase in range(3):
        for groups in LINE_SETS:
            second_wave(groups, phase)
        if phase < 2:
            left_share(2 * phase + 1)
        if phase == 2:
            for copy in sent:
                copy.wait_send()
        for groups in LINE_SETS:
            third_wave(groups, phase)
            if phase < 2:
                first_wave(groups, phase + 1)
        told_wait(phase)
        if phase < 2:
            tell(phase + 1)
            left_share(2 * phase + 2)


def tile_kernel(count_ref, left_ref, own_ref, far_ref, told_in, slot_in, row_in, acc, told, slot_ref, row_ref, sem):
    me = lax.axis_index("elem")
    tables = [
        pltpu.make_async_copy(source, target, sem.at[n])
        for n, (source, target) in enumerate(((told_in, told), (slot_in, slot_ref), (row_in, row_ref)))
    ]
    for copy in tables:
        copy.start()

    def clear(n, carry):
        acc[pl.ds(n * 8, 8)] = jnp.zeros((8, TILE_ROWS, LANES), jnp.float32)
        return carry

    lax.fori_loop(0, N * TO // 8, clear, 0)
    for copy in tables:
        copy.wait()
    lane = lax.broadcasted_iota(jnp.int32, (TILE_ROWS, LANES), 1)

    def step(row, carry):
        for k in range(KA):
            index = row_ref[k, row]
            away = jnp.maximum(index - R, 0)
            own = own_ref[jnp.minimum(index, R - 1)]
            far = far_ref[lax.rem(me + 2 * N - 1 - lax.div(away, S), N) * S + lax.rem(away, S)]
            high, low = split(jnp.where(index < R, own, far))
            wide = jnp.concatenate([high, low], axis=1)
            both = jnp.dot(left_ref[row, k], jnp.concatenate([wide, wide], axis=0), preferred_element_type=jnp.float32)
            part = both[:, :LANES] + both[:, LANES:]
            turned = pltpu.roll(part, B, 1)
            for p in range(KP):
                top, bottom = p * B, p * B + TILE_ROWS
                upper, lower = part[top : top + TILE_ROWS], part[bottom : bottom + TILE_ROWS]
                upper_t, lower_t = turned[top : top + TILE_ROWS], turned[bottom : bottom + TILE_ROWS]
                tiles = (jnp.where(lane < B, upper, lower_t), jnp.where(lane < B, upper_t, lower))
                for q in range(KP):
                    slot = slot_ref[row, p * (KA * KP) + k * KP + q]
                    owner = lax.rem(me + lax.div(slot, CAP), N)
                    target = owner * TO + told[owner, 0, lax.rem(slot, CAP)]
                    acc[target] += tiles[q]
        return carry

    count = jnp.minimum(count_ref[0], R)

    def pair(n, carry):
        step(2 * n, carry)
        return step(2 * n + 1, carry)

    lax.fori_loop(0, lax.div(count, 2), pair, 0)
    lax.fori_loop(lax.div(count, 2) * 2, count, step, 0)


def ring_shapes():
    shapes = []
    for _, length in GROUPS:
        for stage in range(3):
            lead = (RING,) * (2 - stage)
            slab = lead + (length, LANES)
            shapes += [pltpu.VMEM(slab, jnp.float32)] * 3
    return shapes


def add(target, *terms):
    def one(at):
        value = target[at]
        for term in terms:
            value = value + term[at]
        target[at] = value

    lead = target.shape[:-2]
    whole = (slice(None), slice(None))
    if not lead:
        one(whole)
        return

    def outer(n, carry):
        if len(lead) == 1:
            one((n,) + whole)
        else:
            for m in range(lead[1]):
                one((n, m) + whole)
        return carry

    lax.fori_loop(0, lead[0], outer, 0)


def reduce_kernel(acc_ref, out_ref, mine, *rest):
    bufs, (in_send, in_recv, ring_send, ring_recv) = rest[:-4], rest[-4:]
    me = lax.axis_index("elem")
    core = me % 2
    chip = me // 2
    place = (chip // (RING * RING), (chip // RING) % RING, chip % RING)
    partner = me + 1 - 2 * core

    def device_at(axis, step):
        at = list(place)
        at[axis] = (at[axis] + step) % RING
        return ((at[0] * RING + at[1]) * RING + at[2]) * 2 + core

    barrier = pltpu.get_barrier_semaphore()
    near = [partner] + [device_at(axis, step) for axis in range(3) for step in (1, 2, 3)]
    for other in near:
        pl.semaphore_signal(barrier, inc=1, device_id=(other,), device_id_type=MESH)
    pl.semaphore_wait(barrier, len(near))

    def window(group, fixed, part):
        free = [axis for axis in range(3) if axis not in fixed]
        at = [fixed.get(axis, slice(None)) for axis in range(3)]
        inner = [slice(None)] * len(free)
        first, length = GROUPS[group]
        rows = (0, length)
        if part is not None:
            if free:
                at[free[0]] = inner[0] = pl.ds(part * (RING // 2), RING // 2)
            else:
                half = (length + 8) // 16 * 8
                rows = (half * part, length - half if part else half)
        return (
            tuple(at) + (pl.ds(first + rows[0], rows[1]), slice(None)),
            tuple(inner) + (pl.ds(rows[0], rows[1]), slice(None)),
        )

    def across(group, fixed, core_at):
        at, _ = window(group, fixed, None)
        return at[:3] + (core_at,) + at[3:]

    queue = [(n, step) for n in range(len(SETS)) for step in (2, 1, 3)] + [(n, 0) for n in range(len(SETS))]
    queue = [(group, step) for n, step in queue for group in SETS[n]]
    loads, sends = {}, []

    def fetch():
        if len(loads) == len(queue):
            return
        group, offset = queue[len(loads)]
        axis = ORDERS[group][0]
        fixed = {axis: (place[axis] + offset) % RING}
        n = group * RING + offset
        at, _ = window(group, fixed, None)
        give = pltpu.make_async_remote_copy(
            src_ref=acc_ref.at[across(group, fixed, 1 - core)],
            dst_ref=mine.at[at],
            send_sem=in_send.at[n],
            recv_sem=in_recv.at[n],
            device_id=(partner,),
            device_id_type=MESH,
        )
        give.start()
        loads[group, offset] = (give, acc_ref.at[across(group, fixed, core)], mine.at[at])
        sends.append(give)

    for _ in range(AHEAD):
        fetch()

    def arrive(group, offset):
        give, own, target = loads[group, offset]
        give.wait_recv()
        fetch()
        add(target, own)

    flights = {}

    def fixed_at(group, stage, step):
        order = ORDERS[group]
        fixed = {axis: place[axis] for axis in order[:stage]}
        fixed[order[stage]] = (place[order[stage]] + step) % RING
        return fixed

    def start(group, stage, kind, step, part, towards, buffer):
        n = (group * 3 + stage) * 6 + kind
        at, inner = window(group, fixed_at(group, stage, step), part)
        copy = pltpu.make_async_remote_copy(
            src_ref=mine.at[at],
            dst_ref=bufs[(group * 3 + stage) * 3 + buffer].at[inner],
            send_sem=ring_send.at[n],
            recv_sem=ring_recv.at[n],
            device_id=(device_at(ORDERS[group][stage], towards),),
            device_id_type=MESH,
        )
        copy.start()
        flights[group, stage, kind] = copy
        sends.append(copy)

    def first_wave(groups, stage):
        for step, sends_of in ((2, ((0, 0, 1, 0), (1, 1, 3, 0))), (1, ((2, 1, 1, 1),)), (3, ((3, 0, 3, 2),))):
            for group in groups:
                if stage == 0:
                    arrive(group, step)
                for kind, part, towards, buffer in sends_of:
                    start(group, stage, kind, step, part, towards, buffer)

    def last_sends(groups):
        for kind, step in ((1, 2), (0, 1), (2, 3)):
            for group in groups:
                start(group, 2, kind, step, None, step, kind)

    def finish(groups):
        for group in groups:
            for kind in range(3):
                flights[group, 2, kind].wait_recv()
            at, _ = window(group, fixed_at(group, 2, 0), None)
            first, length = GROUPS[group]
            terms = bufs[(group * 3 + 2) * 3 : (group * 3 + 2) * 3 + 3]
            out_ref[pl.ds(first, length), :] = mine[at] + terms[0][...] + terms[1][...] + terms[2][...]

    def second_wave(group, stage):
        buffer = bufs[(group * 3 + stage) * 3]
        for kind, part, step in ((0, 0, 1), (1, 1, 3)):
            flights[group, stage, kind].wait_recv()
            at, inner = window(group, fixed_at(group, stage, step), part)
            add(mine.at[at], buffer.at[inner])
            start(group, stage, 4 + kind, step, part, step, 1 + kind)

    def third_wave(group, stage):
        for kind in (2, 3, 4, 5):
            flights[group, stage, kind].wait_recv()
        at, _ = window(group, fixed_at(group, stage, 0), None)
        _, plus, minus = bufs[(group * 3 + stage) * 3 : (group * 3 + stage) * 3 + 3]
        add(mine.at[at], plus, minus)

    for groups in SETS:
        first_wave(groups, 0)
    for stage in range(2):
        for groups in SETS:
            for group in groups:
                second_wave(group, stage)
        for groups in SETS:
            for group in groups:
                if stage == 0:
                    arrive(group, 0)
                third_wave(group, stage)
            if stage == 0:
                first_wave(groups, 1)
            else:
                last_sends(groups)
    for copy in sends:
        copy.wait_send()
    for groups in SETS:
        finish(groups)


def reduce_scatter(acc):
    return pl.pallas_call(
        reduce_kernel,
        out_shape=jax.ShapeDtypeStruct((OWNER_ROWS, LANES), jnp.float32),
        in_specs=[pl.BlockSpec(memory_space=pltpu.VMEM)],
        out_specs=pl.BlockSpec(memory_space=pltpu.VMEM),
        scratch_shapes=[
            pltpu.VMEM((RING, RING, RING, OWNER_ROWS, LANES), jnp.float32),
            *ring_shapes(),
            pltpu.SemaphoreType.DMA((RING * len(GROUPS),)),
            pltpu.SemaphoreType.DMA((RING * len(GROUPS),)),
            pltpu.SemaphoreType.DMA((18 * len(GROUPS),)),
            pltpu.SemaphoreType.DMA((18 * len(GROUPS),)),
        ],
        compiler_params=pltpu.CompilerParams(collective_id=0, has_side_effects=True, vmem_limit_bytes=20 * 2**20),
        name="reduce_scatter",
    )(acc.reshape(RING, RING, RING, 2, OWNER_ROWS, LANES))


def body(a_blocks, p_blocks, a_slot, serve_rows, row_count, contrib_slot, recv_tile):
    raw = p_blocks.reshape(R, KP, TILE_ROWS, LANES).transpose(0, 2, 1, 3).reshape(R, B, LANES)
    a_native = a_blocks.transpose(1, 0, 2).reshape(KA, R // 8, 8, TILE_ROWS, LANES).transpose(0, 1, 3, 2, 4)
    block = (RING, RING, RING, 2, S * B, LANES)
    told_block = (RING, RING, RING, 2, 1, LANES)
    vmem = pl.BlockSpec(memory_space=pltpu.VMEM)
    smem = pl.BlockSpec(memory_space=pltpu.SMEM)
    rows, far, left, told, slots, slot_rows = pl.pallas_call(
        exchange_kernel,
        in_specs=[smem, smem, vmem, vmem] + [pl.BlockSpec(memory_space=pl.ANY)] * 3,
        out_specs=(vmem,) * 6,
        out_shape=(
            pltpu.VMEM((R, B, LANES), jnp.float32),
            pltpu.VMEM(block, jnp.float32),
            pltpu.VMEM((R, KA, KP * B, LANES), jnp.bfloat16),
            pltpu.VMEM(told_block, jnp.int32),
            pltpu.VMEM((R, KP * KA * KP), jnp.int32),
            pltpu.VMEM((KA, R), jnp.int32),
        ),
        scratch_shapes=[
            pltpu.VMEM(block, jnp.float32),
            pltpu.VMEM(block, jnp.float32),
            pltpu.VMEM(block, jnp.float32),
            pltpu.VMEM((KA * R // 8, 8 * TILE_ROWS, LANES), jnp.float32),
            pltpu.VMEM((N, LANES), jnp.int32),
            *[pltpu.VMEM(told_block, jnp.int32)] * 3,
            *relay_shapes(),
            pltpu.SemaphoreType.DMA((27 * len(LINES),)),
            pltpu.SemaphoreType.DMA((27 * len(LINES),)),
            pltpu.SemaphoreType.DMA((3 * len(LINES),)),
            pltpu.SemaphoreType.DMA((3,)),
            pltpu.SemaphoreType.DMA((24,)),
            pltpu.SemaphoreType.DMA((24,)),
            pltpu.SemaphoreType.DMA((3,)),
        ],
        compiler_params=pltpu.CompilerParams(collective_id=1, has_side_effects=True, vmem_limit_bytes=50100000),
        name="exchange",
    )(serve_rows[0].T, row_count, raw, recv_tile[0].T, a_native.reshape(KA * R // 8, 8 * TILE_ROWS, LANES), contrib_slot, a_slot.T)
    acc = pl.pallas_call(
        tile_kernel,
        grid_spec=pltpu.PrefetchScalarGridSpec(
            num_scalar_prefetch=1,
            in_specs=[vmem] * 6,
            out_specs=vmem,
            scratch_shapes=[
                pltpu.SMEM((N, 1, LANES), jnp.int32),
                pltpu.SMEM((R, KP * KA * KP), jnp.int32),
                pltpu.SMEM((KA, R), jnp.int32),
                pltpu.SemaphoreType.DMA((3,)),
            ],
        ),
        out_shape=pltpu.VMEM((N * TO, TILE_ROWS, LANES), jnp.float32),
        compiler_params=pltpu.CompilerParams(vmem_limit_bytes=2 * 2**20),
        name="tiles",
    )(row_count, left, rows, far.reshape(N * S, B, LANES), told.reshape(N, 1, LANES), slots, slot_rows)

    summed = reduce_scatter(acc)
    return summed.reshape(TO, TILE_ROWS, 2, B).transpose(0, 2, 1, 3).reshape(TO, B * B)


def solution(mesh):
    in_specs = (
        P("elem", None, None),
        P("elem", None, None),
        P("elem", None),
        P("elem", None, None),
        P("elem"),
        P("elem", None),
        P("elem", None, None),
    )
    return jax.shard_map(body, mesh=mesh, in_specs=in_specs, out_specs=P("elem", None), check_vma=False)
```

```python
import jax
import jax.numpy as jnp
from jax import lax
from jax.experimental import pallas as pl
from jax.experimental.pallas import tpu as pltpu
from jax.sharding import PartitionSpec as P


B = 64
KA = 7
KP = 2
S = 2
CAP = 4
TO = 8
R = 32
N = 128
RING = 4
LANES = 128
TILE_ROWS = B * B // LANES
OWNER_ROWS = TO * TILE_ROWS
MESH = pl.DeviceIdType.MESH

GROUPS = ((0, 40), (40, 48), (88, 40), (128, 48), (176, 40), (216, 40))
ORDERS = ((0, 1, 2), (1, 2, 0), (2, 0, 1)) * 2
SETS = ((0, 1, 2), (3, 4, 5))
AHEAD = 6


def split(value):
    high = value.astype(jnp.bfloat16)
    low = (value - high.astype(jnp.float32)).astype(jnp.bfloat16)
    return high, low


LINES = ((0, 16), (16, 16), (32, 16), (48, 16), (64, 8), (72, 16), (88, 8), (96, 16), (112, 16))
LINE_ORDERS = ((0, 1, 2), (1, 2, 0), (2, 0, 1)) * 3
LINE_SETS = ((0, 1, 2), (3, 4, 5), (6, 7, 8))
SHARES = (8, 8, 6, 6, 4)


def relay_shapes():
    return [pltpu.VMEM((RING, RING, length, LANES), jnp.float32) for _, length in LINES for _ in range(6)]


def exchange_kernel(serve_ref, count_ref, raw_ref, tiles_ref, a_hbm, slot_hbm, row_hbm, rows_ref, far_ref, left_ref, told_ref, slot_ref, row_ref, *rest):
    out, first_hop, second_hop, a_ref, turned_ref, first_told, second_told, third_told = rest[:8]
    relays = rest[8:-7]
    send, recv, local, pass_sem, told_send, told_recv, told_local = rest[-7:]
    hops = (out, first_hop, second_hop, far_ref)
    me = lax.axis_index("elem")
    core = me % 2
    chip = me // 2
    place = (chip // (RING * RING), (chip // RING) % RING, chip % RING)

    def device_at(axis, step, core_at):
        at = list(place)
        at[axis] = (at[axis] + step) % RING
        return ((at[0] * RING + at[1]) * RING + at[2]) * 2 + core_at

    barrier = pltpu.get_barrier_semaphore()

    near = [device_at(0, 0, 1 - core)]
    near += [device_at(axis, step, k) for axis in range(3) for step in (1, 2, 3) for k in range(2)]
    for other in near:
        pl.semaphore_signal(barrier, inc=1, device_id=(other,), device_id_type=MESH)
    passing = [
        pltpu.make_async_copy(source, target, pass_sem.at[n])
        for n, (source, target) in enumerate(((a_hbm, a_ref), (slot_hbm, slot_ref), (row_hbm, row_ref)))
    ]
    for copy in passing:
        copy.start()

    lane = lax.broadcasted_iota(jnp.int32, (B, LANES), 1) < B
    even = lax.broadcasted_iota(jnp.int32, (B, LANES), 0) % 2 == 0

    def turn(n, carry):
        raw = raw_ref[n]
        halves = pltpu.roll(raw, B, 1)
        other = jnp.where(even, pltpu.roll(halves, B - 1, 0), pltpu.roll(halves, 1, 0))
        rows_ref[n] = jnp.where(lane == even, raw, other)
        return carry

    lax.fori_loop(0, R, turn, 0)
    turned_ref[...] = jnp.zeros((N, LANES), jnp.int32)
    turned_ref[0:CAP, :] = tiles_ref[...]
    turned_ref[...] = turned_ref[...].T

    def gather(n, carry):
        y, x = n // RING, n % RING
        for z in range(RING):
            for k in range(2):
                ahead = lax.rem(n * (2 * RING) + (2 * z + k) + N - me, N)
                for c in range(S):
                    out[y, x, z, k, c * B : (c + 1) * B, :] = rows_ref[serve_ref[c, lax.rem(ahead + N - 2, N - 1)]]
                first_told[y, x, z, k] = turned_ref[pl.ds(lax.rem(N - ahead, N), 1), :]
        return carry

    lax.fori_loop(0, RING * RING, gather, 0)
    pl.semaphore_wait(barrier, len(near))
    tolds = (first_told, second_told, third_told, told_ref)

    def tell(phase):
        source, target = tolds[phase], tolds[phase + 1]
        u = place[phase]

        def at(index, core_at=slice(None)):
            spot = [slice(None)] * 3
            spot[phase] = index
            return tuple(spot) + (core_at, slice(None), slice(None))

        flights = []
        for step in range(RING):
            for part in range(2 if phase == 2 else 1):
                to = (u + step) % RING
                if phase == 2:
                    src, dst = source.at[at(to, part)], target.at[at(u, core)]
                    device = device_at(phase, step, part)
                else:
                    src, dst = source.at[at(to)], target.at[at(u)]
                    device = device_at(phase, step, core)
                if phase == 2 and step == 0:
                    continue
                if step == 0:
                    copy = pltpu.make_async_copy(src, dst, told_local.at[phase])
                    copy.start()
                    told_waits.append((phase, copy.wait))
                    continue
                lane_of = phase * 8 + 2 * step + (core if phase == 2 else 0)
                copy = pltpu.make_async_remote_copy(
                    src_ref=src,
                    dst_ref=dst,
                    send_sem=told_send.at[phase * 8 + 2 * step + part],
                    recv_sem=told_recv.at[lane_of],
                    device_id=(device,),
                    device_id_type=MESH,
                )
                copy.start()
                sent.append(copy)
        if phase == 2:
            copy = pltpu.make_async_copy(source.at[at(u, core)], target.at[at(u, core)], told_local.at[2])
            copy.start()
            told_waits.append((phase, copy.wait))
            copy = pltpu.make_async_remote_copy(
                src_ref=source.at[at(u, 1 - core)],
                dst_ref=target.at[at(u, core)],
                send_sem=told_send.at[phase * 8],
                recv_sem=told_recv.at[phase * 8],
                device_id=(device_at(phase, 0, 1 - core),),
                device_id_type=MESH,
            )
            copy.start()
            sent.append(copy)

    def told_wait(phase):
        target = tolds[phase + 1]
        for at_phase, wait in told_waits:
            if at_phase == phase:
                wait()
        spot = [slice(None)] * 3
        spot[phase] = place[phase]
        lanes = (0, 2, 3, 4, 5, 6, 7) if phase == 2 else (2, 4, 6)
        like = target.at[tuple(spot) + ((core if phase == 2 else slice(None)), slice(None), slice(None))]
        for lane_of in lanes:
            pltpu.make_async_copy(like, like, told_recv.at[phase * 8 + lane_of]).wait()

    told_waits = []
    def window(group, axis, at_axis, core_at):
        at = [slice(None)] * 3
        at[axis] = at_axis
        return tuple(at) + (slice(None) if core_at is None else core_at, pl.ds(*LINES[group]), slice(None))

    sent = []
    arrivals = {}

    def fly(group, phase, kind, source, target, device, lane_of=0):
        base = (group * 3 + phase) * 9
        copy = pltpu.make_async_remote_copy(
            src_ref=source,
            dst_ref=target,
            send_sem=send.at[base + kind],
            recv_sem=recv.at[base + lane_of],
            device_id=(device,),
            device_id_type=MESH,
        )
        copy.start()
        sent.append(copy)

    def land(group, phase, lane_of, like):
        pltpu.make_async_copy(like, like, recv.at[(group * 3 + phase) * 9 + lane_of]).wait()

    def first_wave(groups, phase):
        source, target = hops[phase], hops[phase + 1]
        for group in groups:
            axis = LINE_ORDERS[group][phase]
            u = place[axis]
            for part, step in ((0, 1), (1, 3)):
                relay = relays[(group * 3 + phase) * 2 + part]
                src = source.at[window(group, axis, (u + 2) % RING, part)]
                fly(group, phase, part, src, relay, device_at(axis, step, core), part)
        for side, step in ((0, 1), (1, 3)):
            for group in groups:
                axis = LINE_ORDERS[group][phase]
                u = place[axis]
                to = (u + step) % RING
                if phase < 2:
                    at = window(group, axis, u, None)
                    fly(group, phase, 2 + side, source.at[window(group, axis, to, None)], target.at[at], device_at(axis, step, core), 2 + side)
                else:
                    at = window(group, axis, u, core)
                    for part in range(2):
                        kind = 2 + 2 * side + part
                        src = source.at[window(group, axis, to, part)]
                        fly(group, phase, kind, src, target.at[at], device_at(axis, step, part), 2 + 2 * side + core)
        for group in groups:
            axis = LINE_ORDERS[group][phase]
            u = place[axis]
            at = window(group, axis, u, None if phase < 2 else core)
            keep = pltpu.make_async_copy(source.at[at], target.at[at], local.at[group * 3 + phase])
            keep.start()
            arrivals[group, phase] = keep
            if phase == 2:
                src = source.at[window(group, axis, u, 1 - core)]
                fly(group, phase, 8, src, target.at[at], device_at(axis, 0, 1 - core), 8)

    def second_wave(groups, phase):
        target = hops[phase + 1]
        for group in groups:
            axis = LINE_ORDERS[group][phase]
            u = place[axis]
            for part, step in ((0, 1), (1, 3)):
                relay = relays[(group * 3 + phase) * 2 + part]
                land(group, phase, part, relay)
                origin = (u + RING - step) % RING
                if phase < 2:
                    at = window(group, axis, origin, part)
                    fly(group, phase, 6 + part, relay, target.at[at], device_at(axis, step, core), 6 + part)
                else:
                    at = window(group, axis, origin, core)
                    fly(group, phase, 6 + part, relay, target.at[at], device_at(axis, step, part), 6 + core)

    def third_wave(groups, phase):
        target = hops[phase + 1]
        for group in groups:
            axis = LINE_ORDERS[group][phase]
            u = place[axis]
            arrivals[group, phase].wait()
            for side in range(2):
                if phase < 2:
                    land(group, phase, 2 + side, target.at[window(group, axis, u, None)])
                else:
                    land(group, phase, 2 + 2 * side, target.at[window(group, axis, u, core)])
                    land(group, phase, 3 + 2 * side, target.at[window(group, axis, u, core)])
            land(group, phase, 6, target.at[window(group, axis, u, core)])
            land(group, phase, 7, target.at[window(group, axis, u, core)])
            if phase == 2:
                land(group, phase, 8, target.at[window(group, axis, u, core)])

    def left_row(row, carry):
        low_half = lax.broadcasted_iota(jnp.int32, (TILE_ROWS, LANES), 1) < B
        stack = [rows_ref[row, pl.ds(h, TILE_ROWS, stride=2), :] for h in range(2)]
        high, low = split(jnp.concatenate(stack, axis=0).T)
        factor = jnp.concatenate([high, low], axis=1)
        for k in range(KA):
            block = a_ref[k * (R // 8) + row // 8, pl.ds(row % 8, TILE_ROWS, stride=8), :]
            turned = pltpu.roll(block, B, 1)
            value = jnp.concatenate([jnp.where(low_half, block, turned), jnp.where(low_half, turned, block)], axis=0)
            top = value.astype(jnp.bfloat16).astype(jnp.float32)
            wide = jnp.where(lane, top, value - top).astype(jnp.bfloat16)
            both = jnp.dot(factor, jnp.concatenate([wide, wide], axis=0), preferred_element_type=jnp.float32)
            twice = both + pltpu.roll(both, B, 1)
            m_high = twice.astype(jnp.bfloat16).astype(jnp.float32)
            wide_lane = lax.broadcasted_iota(jnp.int32, (KP * B, LANES), 1) < B
            left_ref[row, k] = jnp.where(wide_lane, m_high, twice - m_high).astype(jnp.bfloat16)
        return carry

    def left_share(n):
        done = sum(SHARES[:n])
        lax.fori_loop(done, done + SHARES[n], left_row, 0)

    for groups in LINE_SETS:
        first_wave(groups, 0)
    tell(0)
    for copy in passing:
        copy.wait()
    left_share(0)
    for phase in range(3):
        for groups in LINE_SETS:
            second_wave(groups, phase)
        if phase < 2:
            left_share(2 * phase + 1)
        if phase == 2:
            for copy in sent:
                copy.wait_send()
        for groups in LINE_SETS:
            third_wave(groups, phase)
            if phase < 2:
                first_wave(groups, phase + 1)
        told_wait(phase)
        if phase < 2:
            tell(phase + 1)
            left_share(2 * phase + 2)


def tile_kernel(count_ref, left_ref, own_ref, far_ref, told_in, slot_in, row_in, acc, told, slot_ref, row_ref, sem):
    me = lax.axis_index("elem")
    tables = [
        pltpu.make_async_copy(source, target, sem.at[n])
        for n, (source, target) in enumerate(((told_in, told), (slot_in, slot_ref), (row_in, row_ref)))
    ]
    for copy in tables:
        copy.start()

    def clear(n, carry):
        acc[pl.ds(n * 8, 8)] = jnp.zeros((8, TILE_ROWS, LANES), jnp.float32)
        return carry

    lax.fori_loop(0, N * TO // 8, clear, 0)
    for copy in tables:
        copy.wait()
    lane = lax.broadcasted_iota(jnp.int32, (TILE_ROWS, LANES), 1)

    def step(row, carry):
        for k in range(KA):
            index = row_ref[k, row]
            away = jnp.maximum(index - R, 0)
            own = own_ref[jnp.minimum(index, R - 1)]
            far = far_ref[lax.rem(me + 2 * N - 1 - lax.div(away, S), N) * S + lax.rem(away, S)]
            high, low = split(jnp.where(index < R, own, far))
            wide = jnp.concatenate([high, low], axis=1)
            both = jnp.dot(left_ref[row, k], jnp.concatenate([wide, wide], axis=0), preferred_element_type=jnp.float32)
            part = both[:, :LANES] + both[:, LANES:]
            turned = pltpu.roll(part, B, 1)
            for p in range(KP):
                top, bottom = p * B, p * B + TILE_ROWS
                upper, lower = part[top : top + TILE_ROWS], part[bottom : bottom + TILE_ROWS]
                upper_t, lower_t = turned[top : top + TILE_ROWS], turned[bottom : bottom + TILE_ROWS]
                tiles = (jnp.where(lane < B, upper, lower_t), jnp.where(lane < B, upper_t, lower))
                for q in range(KP):
                    slot = slot_ref[row, p * (KA * KP) + k * KP + q]
                    owner = lax.rem(me + lax.div(slot, CAP), N)
                    target = owner * TO + told[owner, 0, lax.rem(slot, CAP)]
                    acc[target] += tiles[q]
        return carry

    count = jnp.minimum(count_ref[0], R)

    def eight(n, carry):
        for m in range(8):
            step(8 * n + m, carry)
        return carry

    lax.fori_loop(0, lax.div(count, 8), eight, 0)
    lax.fori_loop(lax.div(count, 8) * 8, count, step, 0)


def ring_shapes():
    shapes = []
    for _, length in GROUPS:
        for stage in range(3):
            lead = (RING,) * (2 - stage)
            slab = lead + (length, LANES)
            shapes += [pltpu.VMEM(slab, jnp.float32)] * 3
    return shapes


def add(target, *terms):
    def one(at):
        value = target[at]
        for term in terms:
            value = value + term[at]
        target[at] = value

    lead = target.shape[:-2]
    whole = (slice(None), slice(None))
    if not lead:
        one(whole)
        return

    def outer(n, carry):
        if len(lead) == 1:
            one((n,) + whole)
        else:
            for m in range(lead[1]):
                one((n, m) + whole)
        return carry

    lax.fori_loop(0, lead[0], outer, 0)


def reduce_kernel(acc_ref, out_ref, mine, *rest):
    bufs, (in_send, in_recv, ring_send, ring_recv) = rest[:-4], rest[-4:]
    me = lax.axis_index("elem")
    core = me % 2
    chip = me // 2
    place = (chip // (RING * RING), (chip // RING) % RING, chip % RING)
    partner = me + 1 - 2 * core

    def device_at(axis, step):
        at = list(place)
        at[axis] = (at[axis] + step) % RING
        return ((at[0] * RING + at[1]) * RING + at[2]) * 2 + core

    barrier = pltpu.get_barrier_semaphore()
    near = [partner] + [device_at(axis, step) for axis in range(3) for step in (1, 2, 3)]
    for other in near:
        pl.semaphore_signal(barrier, inc=1, device_id=(other,), device_id_type=MESH)
    pl.semaphore_wait(barrier, len(near))

    def window(group, fixed, part):
        free = [axis for axis in range(3) if axis not in fixed]
        at = [fixed.get(axis, slice(None)) for axis in range(3)]
        inner = [slice(None)] * len(free)
        first, length = GROUPS[group]
        rows = (0, length)
        if part is not None:
            if free:
                at[free[0]] = inner[0] = pl.ds(part * (RING // 2), RING // 2)
            else:
                half = (length + 8) // 16 * 8
                rows = (half * part, length - half if part else half)
        return (
            tuple(at) + (pl.ds(first + rows[0], rows[1]), slice(None)),
            tuple(inner) + (pl.ds(rows[0], rows[1]), slice(None)),
        )

    def across(group, fixed, core_at):
        at, _ = window(group, fixed, None)
        return at[:3] + (core_at,) + at[3:]

    queue = [(n, step) for n in range(len(SETS)) for step in (2, 1, 3)] + [(n, 0) for n in range(len(SETS))]
    queue = [(group, step) for n, step in queue for group in SETS[n]]
    loads, sends = {}, []

    def fetch():
        if len(loads) == len(queue):
            return
        group, offset = queue[len(loads)]
        axis = ORDERS[group][0]
        fixed = {axis: (place[axis] + offset) % RING}
        n = group * RING + offset
        at, _ = window(group, fixed, None)
        give = pltpu.make_async_remote_copy(
            src_ref=acc_ref.at[across(group, fixed, 1 - core)],
            dst_ref=mine.at[at],
            send_sem=in_send.at[n],
            recv_sem=in_recv.at[n],
            device_id=(partner,),
            device_id_type=MESH,
        )
        give.start()
        loads[group, offset] = (give, acc_ref.at[across(group, fixed, core)], mine.at[at])
        sends.append(give)

    for _ in range(AHEAD):
        fetch()

    def arrive(group, offset):
        give, own, target = loads[group, offset]
        give.wait_recv()
        fetch()
        add(target, own)

    flights = {}

    def fixed_at(group, stage, step):
        order = ORDERS[group]
        fixed = {axis: place[axis] for axis in order[:stage]}
        fixed[order[stage]] = (place[order[stage]] + step) % RING
        return fixed

    def start(group, stage, kind, step, part, towards, buffer):
        n = (group * 3 + stage) * 6 + kind
        at, inner = window(group, fixed_at(group, stage, step), part)
        copy = pltpu.make_async_remote_copy(
            src_ref=mine.at[at],
            dst_ref=bufs[(group * 3 + stage) * 3 + buffer].at[inner],
            send_sem=ring_send.at[n],
            recv_sem=ring_recv.at[n],
            device_id=(device_at(ORDERS[group][stage], towards),),
            device_id_type=MESH,
        )
        copy.start()
        flights[group, stage, kind] = copy
        sends.append(copy)

    def first_wave(groups, stage):
        for step, sends_of in ((2, ((0, 0, 1, 0), (1, 1, 3, 0))), (1, ((2, 1, 1, 1),)), (3, ((3, 0, 3, 2),))):
            for group in groups:
                if stage == 0:
                    arrive(group, step)
                for kind, part, towards, buffer in sends_of:
                    start(group, stage, kind, step, part, towards, buffer)

    def last_sends(groups):
        for kind, step in ((1, 2), (0, 1), (2, 3)):
            for group in groups:
                start(group, 2, kind, step, None, step, kind)

    def finish(groups):
        for group in groups:
            for kind in range(3):
                flights[group, 2, kind].wait_recv()
            at, _ = window(group, fixed_at(group, 2, 0), None)
            first, length = GROUPS[group]
            terms = bufs[(group * 3 + 2) * 3 : (group * 3 + 2) * 3 + 3]
            out_ref[pl.ds(first, length), :] = mine[at] + terms[0][...] + terms[1][...] + terms[2][...]

    def second_wave(group, stage):
        buffer = bufs[(group * 3 + stage) * 3]
        for kind, part, step in ((0, 0, 1), (1, 1, 3)):
            flights[group, stage, kind].wait_recv()
            at, inner = window(group, fixed_at(group, stage, step), part)
            add(mine.at[at], buffer.at[inner])
            start(group, stage, 4 + kind, step, part, step, 1 + kind)

    def third_wave(group, stage):
        for kind in (2, 3, 4, 5):
            flights[group, stage, kind].wait_recv()
        at, _ = window(group, fixed_at(group, stage, 0), None)
        _, plus, minus = bufs[(group * 3 + stage) * 3 : (group * 3 + stage) * 3 + 3]
        add(mine.at[at], plus, minus)

    for groups in SETS:
        first_wave(groups, 0)
    for stage in range(2):
        for groups in SETS:
            for group in groups:
                second_wave(group, stage)
        for groups in SETS:
            for group in groups:
                if stage == 0:
                    arrive(group, 0)
                third_wave(group, stage)
            if stage == 0:
                first_wave(groups, 1)
            else:
                last_sends(groups)
    for copy in sends:
        copy.wait_send()
    for groups in SETS:
        finish(groups)


def reduce_scatter(acc):
    return pl.pallas_call(
        reduce_kernel,
        out_shape=jax.ShapeDtypeStruct((OWNER_ROWS, LANES), jnp.float32),
        in_specs=[pl.BlockSpec(memory_space=pltpu.VMEM)],
        out_specs=pl.BlockSpec(memory_space=pltpu.VMEM),
        scratch_shapes=[
            pltpu.VMEM((RING, RING, RING, OWNER_ROWS, LANES), jnp.float32),
            *ring_shapes(),
            pltpu.SemaphoreType.DMA((RING * len(GROUPS),)),
            pltpu.SemaphoreType.DMA((RING * len(GROUPS),)),
            pltpu.SemaphoreType.DMA((18 * len(GROUPS),)),
            pltpu.SemaphoreType.DMA((18 * len(GROUPS),)),
        ],
        compiler_params=pltpu.CompilerParams(collective_id=0, has_side_effects=True, vmem_limit_bytes=20 * 2**20),
        name="reduce_scatter",
    )(acc.reshape(RING, RING, RING, 2, OWNER_ROWS, LANES))


def body(a_blocks, p_blocks, a_slot, serve_rows, row_count, contrib_slot, recv_tile):
    raw = p_blocks.reshape(R, KP, TILE_ROWS, LANES).transpose(0, 2, 1, 3).reshape(R, B, LANES)
    a_native = a_blocks.transpose(1, 0, 2).reshape(KA, R // 8, 8, TILE_ROWS, LANES).transpose(0, 1, 3, 2, 4)
    block = (RING, RING, RING, 2, S * B, LANES)
    told_block = (RING, RING, RING, 2, 1, LANES)
    vmem = pl.BlockSpec(memory_space=pltpu.VMEM)
    smem = pl.BlockSpec(memory_space=pltpu.SMEM)
    rows, far, left, told, slots, slot_rows = pl.pallas_call(
        exchange_kernel,
        in_specs=[smem, smem, vmem, vmem] + [pl.BlockSpec(memory_space=pl.ANY)] * 3,
        out_specs=(vmem,) * 6,
        out_shape=(
            pltpu.VMEM((R, B, LANES), jnp.float32),
            pltpu.VMEM(block, jnp.float32),
            pltpu.VMEM((R, KA, KP * B, LANES), jnp.bfloat16),
            pltpu.VMEM(told_block, jnp.int32),
            pltpu.VMEM((R, KP * KA * KP), jnp.int32),
            pltpu.VMEM((KA, R), jnp.int32),
        ),
        scratch_shapes=[
            pltpu.VMEM(block, jnp.float32),
            pltpu.VMEM(block, jnp.float32),
            pltpu.VMEM(block, jnp.float32),
            pltpu.VMEM((KA * R // 8, 8 * TILE_ROWS, LANES), jnp.float32),
            pltpu.VMEM((N, LANES), jnp.int32),
            *[pltpu.VMEM(told_block, jnp.int32)] * 3,
            *relay_shapes(),
            pltpu.SemaphoreType.DMA((27 * len(LINES),)),
            pltpu.SemaphoreType.DMA((27 * len(LINES),)),
            pltpu.SemaphoreType.DMA((3 * len(LINES),)),
            pltpu.SemaphoreType.DMA((3,)),
            pltpu.SemaphoreType.DMA((24,)),
            pltpu.SemaphoreType.DMA((24,)),
            pltpu.SemaphoreType.DMA((3,)),
        ],
        compiler_params=pltpu.CompilerParams(collective_id=1, has_side_effects=True, vmem_limit_bytes=50100000),
        name="exchange",
    )(serve_rows[0].T, row_count, raw, recv_tile[0].T, a_native.reshape(KA * R // 8, 8 * TILE_ROWS, LANES), contrib_slot, a_slot.T)
    acc = pl.pallas_call(
        tile_kernel,
        grid_spec=pltpu.PrefetchScalarGridSpec(
            num_scalar_prefetch=1,
            in_specs=[vmem] * 6,
            out_specs=vmem,
            scratch_shapes=[
                pltpu.SMEM((N, 1, LANES), jnp.int32),
                pltpu.SMEM((R, KP * KA * KP), jnp.int32),
                pltpu.SMEM((KA, R), jnp.int32),
                pltpu.SemaphoreType.DMA((3,)),
            ],
        ),
        out_shape=pltpu.VMEM((N * TO, TILE_ROWS, LANES), jnp.float32),
        compiler_params=pltpu.CompilerParams(vmem_limit_bytes=2 * 2**20),
        name="tiles",
    )(row_count, left, rows, far.reshape(N * S, B, LANES), told.reshape(N, 1, LANES), slots, slot_rows)

    summed = reduce_scatter(acc)
    return summed.reshape(TO, TILE_ROWS, 2, B).transpose(0, 2, 1, 3).reshape(TO, B * B)


def solution(mesh):
    in_specs = (
        P("elem", None, None),
        P("elem", None, None),
        P("elem", None),
        P("elem", None, None),
        P("elem"),
        P("elem", None),
        P("elem", None, None),
    )
    return jax.shard_map(body, mesh=mesh, in_specs=in_specs, out_specs=P("elem", None), check_vma=False)
```

```python
import jax
import jax.numpy as jnp
from jax import lax
from jax.experimental import pallas as pl
from jax.experimental.pallas import tpu as pltpu
from jax.sharding import PartitionSpec as P


B = 64
KA = 7
KP = 2
S = 2
CAP = 4
TO = 8
R = 32
N = 128
RING = 4
LANES = 128
TILE_ROWS = B * B // LANES
OWNER_ROWS = TO * TILE_ROWS
MESH = pl.DeviceIdType.MESH

GROUPS = ((0, 40), (40, 48), (88, 40), (128, 48), (176, 40), (216, 40))
ORDERS = ((0, 1, 2), (1, 2, 0), (2, 0, 1)) * 2
SETS = ((0, 1, 2), (3, 4, 5))
AHEAD = 6


def split(value):
    high = value.astype(jnp.bfloat16)
    low = (value - high.astype(jnp.float32)).astype(jnp.bfloat16)
    return high, low


LINES = ((0, 16), (16, 16), (32, 16), (48, 16), (64, 8), (72, 16), (88, 8), (96, 16), (112, 16))
LINE_ORDERS = ((0, 1, 2), (1, 2, 0), (2, 0, 1)) * 3
LINE_SETS = ((0, 1, 2), (3, 4, 5), (6, 7, 8))
SHARES = (8, 8, 6, 6, 4)


def relay_shapes():
    return [pltpu.VMEM((RING, RING, length, LANES), jnp.float32) for _, length in LINES for _ in range(6)]


def exchange_kernel(serve_ref, count_ref, raw_ref, tiles_ref, a_hbm, slot_hbm, row_hbm, rows_ref, far_ref, left_ref, told_ref, slot_ref, row_ref, *rest):
    out, first_hop, second_hop, a_ref, turned_ref, first_told, second_told, third_told = rest[:8]
    relays = rest[8:-7]
    send, recv, local, pass_sem, told_send, told_recv, told_local = rest[-7:]
    hops = (out, first_hop, second_hop, far_ref)
    me = lax.axis_index("elem")
    core = me % 2
    chip = me // 2
    place = (chip // (RING * RING), (chip // RING) % RING, chip % RING)

    def device_at(axis, step, core_at):
        at = list(place)
        at[axis] = (at[axis] + step) % RING
        return ((at[0] * RING + at[1]) * RING + at[2]) * 2 + core_at

    barrier = pltpu.get_barrier_semaphore()

    near = [device_at(0, 0, 1 - core)]
    near += [device_at(axis, step, k) for axis in range(3) for step in (1, 2, 3) for k in range(2)]
    for other in near:
        pl.semaphore_signal(barrier, inc=1, device_id=(other,), device_id_type=MESH)
    passing = [
        pltpu.make_async_copy(source, target, pass_sem.at[n])
        for n, (source, target) in enumerate(((a_hbm, a_ref), (slot_hbm, slot_ref), (row_hbm, row_ref)))
    ]
    for copy in passing:
        copy.start()

    lane = lax.broadcasted_iota(jnp.int32, (B, LANES), 1) < B
    even = lax.broadcasted_iota(jnp.int32, (B, LANES), 0) % 2 == 0

    def turn(n, carry):
        raw = raw_ref[n]
        halves = pltpu.roll(raw, B, 1)
        other = jnp.where(even, pltpu.roll(halves, B - 1, 0), pltpu.roll(halves, 1, 0))
        rows_ref[n] = jnp.where(lane == even, raw, other)
        return carry

    lax.fori_loop(0, R, turn, 0)
    turned_ref[...] = jnp.zeros((N, LANES), jnp.int32)
    turned_ref[0:CAP, :] = tiles_ref[...]
    turned_ref[...] = turned_ref[...].T

    def gather(n, carry):
        y, x = n // RING, n % RING
        for z in range(RING):
            for k in range(2):
                ahead = lax.rem(n * (2 * RING) + (2 * z + k) + N - me, N)
                for c in range(S):
                    out[y, x, z, k, c * B : (c + 1) * B, :] = rows_ref[serve_ref[c, lax.rem(ahead + N - 2, N - 1)]]
                first_told[y, x, z, k] = turned_ref[pl.ds(lax.rem(N - ahead, N), 1), :]
        return carry

    lax.fori_loop(0, RING * RING, gather, 0)
    pl.semaphore_wait(barrier, len(near))
    tolds = (first_told, second_told, third_told, told_ref)

    def tell(phase):
        source, target = tolds[phase], tolds[phase + 1]
        u = place[phase]

        def at(index, core_at=slice(None)):
            spot = [slice(None)] * 3
            spot[phase] = index
            return tuple(spot) + (core_at, slice(None), slice(None))

        flights = []
        for step in range(RING):
            for part in range(2 if phase == 2 else 1):
                to = (u + step) % RING
                if phase == 2:
                    src, dst = source.at[at(to, part)], target.at[at(u, core)]
                    device = device_at(phase, step, part)
                else:
                    src, dst = source.at[at(to)], target.at[at(u)]
                    device = device_at(phase, step, core)
                if phase == 2 and step == 0:
                    continue
                if step == 0:
                    copy = pltpu.make_async_copy(src, dst, told_local.at[phase])
                    copy.start()
                    told_waits.append((phase, copy.wait))
                    continue
                lane_of = phase * 8 + 2 * step + (core if phase == 2 else 0)
                copy = pltpu.make_async_remote_copy(
                    src_ref=src,
                    dst_ref=dst,
                    send_sem=told_send.at[phase * 8 + 2 * step + part],
                    recv_sem=told_recv.at[lane_of],
                    device_id=(device,),
                    device_id_type=MESH,
                )
                copy.start()
                sent.append(copy)
        if phase == 2:
            copy = pltpu.make_async_copy(source.at[at(u, core)], target.at[at(u, core)], told_local.at[2])
            copy.start()
            told_waits.append((phase, copy.wait))
            copy = pltpu.make_async_remote_copy(
                src_ref=source.at[at(u, 1 - core)],
                dst_ref=target.at[at(u, core)],
                send_sem=told_send.at[phase * 8],
                recv_sem=told_recv.at[phase * 8],
                device_id=(device_at(phase, 0, 1 - core),),
                device_id_type=MESH,
            )
            copy.start()
            sent.append(copy)

    def told_wait(phase):
        target = tolds[phase + 1]
        for at_phase, wait in told_waits:
            if at_phase == phase:
                wait()
        spot = [slice(None)] * 3
        spot[phase] = place[phase]
        lanes = (0, 2, 3, 4, 5, 6, 7) if phase == 2 else (2, 4, 6)
        like = target.at[tuple(spot) + ((core if phase == 2 else slice(None)), slice(None), slice(None))]
        for lane_of in lanes:
            pltpu.make_async_copy(like, like, told_recv.at[phase * 8 + lane_of]).wait()

    told_waits = []
    def window(group, axis, at_axis, core_at):
        at = [slice(None)] * 3
        at[axis] = at_axis
        return tuple(at) + (slice(None) if core_at is None else core_at, pl.ds(*LINES[group]), slice(None))

    sent = []
    arrivals = {}

    def fly(group, phase, kind, source, target, device, lane_of=0):
        base = (group * 3 + phase) * 9
        copy = pltpu.make_async_remote_copy(
            src_ref=source,
            dst_ref=target,
            send_sem=send.at[base + kind],
            recv_sem=recv.at[base + lane_of],
            device_id=(device,),
            device_id_type=MESH,
        )
        copy.start()
        sent.append(copy)

    def land(group, phase, lane_of, like):
        pltpu.make_async_copy(like, like, recv.at[(group * 3 + phase) * 9 + lane_of]).wait()

    def first_wave(groups, phase):
        source, target = hops[phase], hops[phase + 1]
        for group in groups:
            axis = LINE_ORDERS[group][phase]
            u = place[axis]
            for part, step in ((0, 1), (1, 3)):
                relay = relays[(group * 3 + phase) * 2 + part]
                src = source.at[window(group, axis, (u + 2) % RING, part)]
                fly(group, phase, part, src, relay, device_at(axis, step, core), part)
        for side, step in ((0, 1), (1, 3)):
            for group in groups:
                axis = LINE_ORDERS[group][phase]
                u = place[axis]
                to = (u + step) % RING
                if phase < 2:
                    at = window(group, axis, u, None)
                    fly(group, phase, 2 + side, source.at[window(group, axis, to, None)], target.at[at], device_at(axis, step, core), 2 + side)
                else:
                    at = window(group, axis, u, core)
                    for part in range(2):
                        kind = 2 + 2 * side + part
                        src = source.at[window(group, axis, to, part)]
                        fly(group, phase, kind, src, target.at[at], device_at(axis, step, part), 2 + 2 * side + core)
        for group in groups:
            axis = LINE_ORDERS[group][phase]
            u = place[axis]
            at = window(group, axis, u, None if phase < 2 else core)
            keep = pltpu.make_async_copy(source.at[at], target.at[at], local.at[group * 3 + phase])
            keep.start()
            arrivals[group, phase] = keep
            if phase == 2:
                src = source.at[window(group, axis, u, 1 - core)]
                fly(group, phase, 8, src, target.at[at], device_at(axis, 0, 1 - core), 8)

    def second_wave(groups, phase):
        target = hops[phase + 1]
        for group in groups:
            axis = LINE_ORDERS[group][phase]
            u = place[axis]
            for part, step in ((0, 1), (1, 3)):
                relay = relays[(group * 3 + phase) * 2 + part]
                land(group, phase, part, relay)
                origin = (u + RING - step) % RING
                if phase < 2:
                    at = window(group, axis, origin, part)
                    fly(group, phase, 6 + part, relay, target.at[at], device_at(axis, step, core), 6 + part)
                else:
                    at = window(group, axis, origin, core)
                    fly(group, phase, 6 + part, relay, target.at[at], device_at(axis, step, part), 6 + core)

    def third_wave(groups, phase):
        target = hops[phase + 1]
        for group in groups:
            axis = LINE_ORDERS[group][phase]
            u = place[axis]
            arrivals[group, phase].wait()
            for side in range(2):
                if phase < 2:
                    land(group, phase, 2 + side, target.at[window(group, axis, u, None)])
                else:
                    land(group, phase, 2 + 2 * side, target.at[window(group, axis, u, core)])
                    land(group, phase, 3 + 2 * side, target.at[window(group, axis, u, core)])
            land(group, phase, 6, target.at[window(group, axis, u, core)])
            land(group, phase, 7, target.at[window(group, axis, u, core)])
            if phase == 2:
                land(group, phase, 8, target.at[window(group, axis, u, core)])

    def left_row(row, carry):
        low_half = lax.broadcasted_iota(jnp.int32, (TILE_ROWS, LANES), 1) < B
        stack = [rows_ref[row, pl.ds(h, TILE_ROWS, stride=2), :] for h in range(2)]
        high, low = split(jnp.concatenate(stack, axis=0).T)
        factor = jnp.concatenate([high, low], axis=1)
        for k in range(KA):
            block = a_ref[k * (R // 8) + row // 8, pl.ds(row % 8, TILE_ROWS, stride=8), :]
            turned = pltpu.roll(block, B, 1)
            value = jnp.concatenate([jnp.where(low_half, block, turned), jnp.where(low_half, turned, block)], axis=0)
            top = value.astype(jnp.bfloat16).astype(jnp.float32)
            wide = jnp.where(lane, top, value - top).astype(jnp.bfloat16)
            both = jnp.dot(factor, jnp.concatenate([wide, wide], axis=0), preferred_element_type=jnp.float32)
            twice = both + pltpu.roll(both, B, 1)
            m_high = twice.astype(jnp.bfloat16).astype(jnp.float32)
            wide_lane = lax.broadcasted_iota(jnp.int32, (KP * B, LANES), 1) < B
            left_ref[row, k] = jnp.where(wide_lane, m_high, twice - m_high).astype(jnp.bfloat16)
        return carry

    def left_share(n):
        done = sum(SHARES[:n])
        lax.fori_loop(done, done + SHARES[n], left_row, 0)

    for groups in LINE_SETS:
        first_wave(groups, 0)
    tell(0)
    for copy in passing:
        copy.wait()
    left_share(0)
    for phase in range(3):
        for groups in LINE_SETS:
            second_wave(groups, phase)
        if phase < 2:
            left_share(2 * phase + 1)
        if phase == 2:
            for copy in sent:
                copy.wait_send()
        for group in range(len(LINES)):
            third_wave((group,), phase)
            if phase < 2:
                first_wave((group,), phase + 1)
        told_wait(phase)
        if phase < 2:
            tell(phase + 1)
            left_share(2 * phase + 2)


def tile_kernel(count_ref, left_ref, own_ref, far_ref, told_in, slot_in, row_in, acc, told, slot_ref, row_ref, sem):
    me = lax.axis_index("elem")
    tables = [
        pltpu.make_async_copy(source, target, sem.at[n])
        for n, (source, target) in enumerate(((told_in, told), (slot_in, slot_ref), (row_in, row_ref)))
    ]
    for copy in tables:
        copy.start()

    def clear(n, carry):
        acc[pl.ds(n * 8, 8)] = jnp.zeros((8, TILE_ROWS, LANES), jnp.float32)
        return carry

    lax.fori_loop(0, N * TO // 8, clear, 0)
    for copy in tables:
        copy.wait()
    lane = lax.broadcasted_iota(jnp.int32, (TILE_ROWS, LANES), 1)

    def step(row, carry):
        for k in range(KA):
            index = row_ref[k, row]
            away = jnp.maximum(index - R, 0)
            own = own_ref[jnp.minimum(index, R - 1)]
            far = far_ref[lax.rem(me + 2 * N - 1 - lax.div(away, S), N) * S + lax.rem(away, S)]
            high, low = split(jnp.where(index < R, own, far))
            wide = jnp.concatenate([high, low], axis=1)
            both = jnp.dot(left_ref[row, k], jnp.concatenate([wide, wide], axis=0), preferred_element_type=jnp.float32)
            part = both[:, :LANES] + both[:, LANES:]
            turned = pltpu.roll(part, B, 1)
            for p in range(KP):
                top, bottom = p * B, p * B + TILE_ROWS
                upper, lower = part[top : top + TILE_ROWS], part[bottom : bottom + TILE_ROWS]
                upper_t, lower_t = turned[top : top + TILE_ROWS], turned[bottom : bottom + TILE_ROWS]
                tiles = (jnp.where(lane < B, upper, lower_t), jnp.where(lane < B, upper_t, lower))
                targets = []
                for q in range(KP):
                    slot = slot_ref[row, p * (KA * KP) + k * KP + q]
                    owner = lax.rem(me + lax.div(slot, CAP), N)
                    targets.append(owner * TO + told[owner, 0, lax.rem(slot, CAP)])
                first, second = (acc[target] for target in targets)
                acc[targets[0]] = first + tiles[0]
                acc[targets[1]] = second + (tiles[1] + jnp.where(targets[0] == targets[1], tiles[0], 0.0))
        return carry

    count = jnp.minimum(count_ref[0], R)

    def eight(n, carry):
        for m in range(8):
            step(8 * n + m, carry)
        return carry

    lax.fori_loop(0, lax.div(count, 8), eight, 0)
    lax.fori_loop(lax.div(count, 8) * 8, count, step, 0)


def ring_shapes():
    shapes = []
    for _, length in GROUPS:
        for stage in range(3):
            lead = (RING,) * (2 - stage)
            slab = lead + (length, LANES)
            shapes += [pltpu.VMEM(slab, jnp.float32)] * 3
    return shapes


def add(target, *terms):
    def one(at):
        value = target[at]
        for term in terms:
            value = value + term[at]
        target[at] = value

    lead = target.shape[:-2]
    whole = (slice(None), slice(None))
    if not lead:
        one(whole)
        return

    def outer(n, carry):
        if len(lead) == 1:
            one((n,) + whole)
        else:
            for m in range(lead[1]):
                one((n, m) + whole)
        return carry

    lax.fori_loop(0, lead[0], outer, 0)


def reduce_kernel(acc_ref, out_ref, mine, *rest):
    bufs, (in_send, in_recv, ring_send, ring_recv) = rest[:-4], rest[-4:]
    me = lax.axis_index("elem")
    core = me % 2
    chip = me // 2
    place = (chip // (RING * RING), (chip // RING) % RING, chip % RING)
    partner = me + 1 - 2 * core

    def device_at(axis, step):
        at = list(place)
        at[axis] = (at[axis] + step) % RING
        return ((at[0] * RING + at[1]) * RING + at[2]) * 2 + core

    barrier = pltpu.get_barrier_semaphore()
    near = [partner] + [device_at(axis, step) for axis in range(3) for step in (1, 2, 3)]
    for other in near:
        pl.semaphore_signal(barrier, inc=1, device_id=(other,), device_id_type=MESH)
    pl.semaphore_wait(barrier, len(near))

    def window(group, fixed, part):
        free = [axis for axis in range(3) if axis not in fixed]
        at = [fixed.get(axis, slice(None)) for axis in range(3)]
        inner = [slice(None)] * len(free)
        first, length = GROUPS[group]
        rows = (0, length)
        if part is not None:
            if free:
                at[free[0]] = inner[0] = pl.ds(part * (RING // 2), RING // 2)
            else:
                half = (length + 8) // 16 * 8
                rows = (half * part, length - half if part else half)
        return (
            tuple(at) + (pl.ds(first + rows[0], rows[1]), slice(None)),
            tuple(inner) + (pl.ds(rows[0], rows[1]), slice(None)),
        )

    def across(group, fixed, core_at):
        at, _ = window(group, fixed, None)
        return at[:3] + (core_at,) + at[3:]

    queue = [(n, step) for n in range(len(SETS)) for step in (2, 1, 3)] + [(n, 0) for n in range(len(SETS))]
    queue = [(group, step) for n, step in queue for group in SETS[n]]
    loads, sends = {}, []

    def fetch():
        if len(loads) == len(queue):
            return
        group, offset = queue[len(loads)]
        axis = ORDERS[group][0]
        fixed = {axis: (place[axis] + offset) % RING}
        n = group * RING + offset
        at, _ = window(group, fixed, None)
        give = pltpu.make_async_remote_copy(
            src_ref=acc_ref.at[across(group, fixed, 1 - core)],
            dst_ref=mine.at[at],
            send_sem=in_send.at[n],
            recv_sem=in_recv.at[n],
            device_id=(partner,),
            device_id_type=MESH,
        )
        give.start()
        loads[group, offset] = (give, acc_ref.at[across(group, fixed, core)], mine.at[at])
        sends.append(give)

    for _ in range(AHEAD):
        fetch()

    def arrive(group, offset):
        give, own, target = loads[group, offset]
        give.wait_recv()
        fetch()
        add(target, own)

    flights = {}

    def fixed_at(group, stage, step):
        order = ORDERS[group]
        fixed = {axis: place[axis] for axis in order[:stage]}
        fixed[order[stage]] = (place[order[stage]] + step) % RING
        return fixed

    def start(group, stage, kind, step, part, towards, buffer):
        n = (group * 3 + stage) * 6 + kind
        at, inner = window(group, fixed_at(group, stage, step), part)
        copy = pltpu.make_async_remote_copy(
            src_ref=mine.at[at],
            dst_ref=bufs[(group * 3 + stage) * 3 + buffer].at[inner],
            send_sem=ring_send.at[n],
            recv_sem=ring_recv.at[n],
            device_id=(device_at(ORDERS[group][stage], towards),),
            device_id_type=MESH,
        )
        copy.start()
        flights[group, stage, kind] = copy
        sends.append(copy)

    def first_wave(groups, stage):
        for step, sends_of in ((2, ((0, 0, 1, 0), (1, 1, 3, 0))), (1, ((2, 1, 1, 1),)), (3, ((3, 0, 3, 2),))):
            for group in groups:
                if stage == 0:
                    arrive(group, step)
                for kind, part, towards, buffer in sends_of:
                    start(group, stage, kind, step, part, towards, buffer)

    def last_sends(groups):
        for kind, step in ((1, 2), (0, 1), (2, 3)):
            for group in groups:
                start(group, 2, kind, step, None, step, kind)

    def finish(groups):
        for group in groups:
            for kind in range(3):
                flights[group, 2, kind].wait_recv()
            at, _ = window(group, fixed_at(group, 2, 0), None)
            first, length = GROUPS[group]
            terms = bufs[(group * 3 + 2) * 3 : (group * 3 + 2) * 3 + 3]
            out_ref[pl.ds(first, length), :] = mine[at] + terms[0][...] + terms[1][...] + terms[2][...]

    def second_wave(group, stage):
        buffer = bufs[(group * 3 + stage) * 3]
        for kind, part, step in ((0, 0, 1), (1, 1, 3)):
            flights[group, stage, kind].wait_recv()
            at, inner = window(group, fixed_at(group, stage, step), part)
            add(mine.at[at], buffer.at[inner])
            start(group, stage, 4 + kind, step, part, step, 1 + kind)

    def third_wave(group, stage):
        for kind in (2, 3, 4, 5):
            flights[group, stage, kind].wait_recv()
        at, _ = window(group, fixed_at(group, stage, 0), None)
        _, plus, minus = bufs[(group * 3 + stage) * 3 : (group * 3 + stage) * 3 + 3]
        add(mine.at[at], plus, minus)

    for groups in SETS:
        first_wave(groups, 0)
    for stage in range(2):
        for groups in SETS:
            for group in groups:
                second_wave(group, stage)
        if stage == 0:
            for group in range(len(GROUPS)):
                arrive(group, 0)
        for group in range(len(GROUPS)):
            third_wave(group, stage)
            if stage == 0:
                first_wave((group,), 1)
            else:
                last_sends((group,))
    for copy in sends:
        copy.wait_send()
    for groups in SETS:
        finish(groups)


def reduce_scatter(acc):
    return pl.pallas_call(
        reduce_kernel,
        out_shape=jax.ShapeDtypeStruct((OWNER_ROWS, LANES), jnp.float32),
        in_specs=[pl.BlockSpec(memory_space=pltpu.VMEM)],
        out_specs=pl.BlockSpec(memory_space=pltpu.VMEM),
        scratch_shapes=[
            pltpu.VMEM((RING, RING, RING, OWNER_ROWS, LANES), jnp.float32),
            *ring_shapes(),
            pltpu.SemaphoreType.DMA((RING * len(GROUPS),)),
            pltpu.SemaphoreType.DMA((RING * len(GROUPS),)),
            pltpu.SemaphoreType.DMA((18 * len(GROUPS),)),
            pltpu.SemaphoreType.DMA((18 * len(GROUPS),)),
        ],
        compiler_params=pltpu.CompilerParams(collective_id=0, has_side_effects=True, vmem_limit_bytes=20 * 2**20),
        name="reduce_scatter",
    )(acc.reshape(RING, RING, RING, 2, OWNER_ROWS, LANES))


def body(a_blocks, p_blocks, a_slot, serve_rows, row_count, contrib_slot, recv_tile):
    raw = p_blocks.reshape(R, KP, TILE_ROWS, LANES).transpose(0, 2, 1, 3).reshape(R, B, LANES)
    a_native = a_blocks.transpose(1, 0, 2).reshape(KA, R // 8, 8, TILE_ROWS, LANES).transpose(0, 1, 3, 2, 4)
    block = (RING, RING, RING, 2, S * B, LANES)
    told_block = (RING, RING, RING, 2, 1, LANES)
    vmem = pl.BlockSpec(memory_space=pltpu.VMEM)
    smem = pl.BlockSpec(memory_space=pltpu.SMEM)
    rows, far, left, told, slots, slot_rows = pl.pallas_call(
        exchange_kernel,
        in_specs=[smem, smem, vmem, vmem] + [pl.BlockSpec(memory_space=pl.ANY)] * 3,
        out_specs=(vmem,) * 6,
        out_shape=(
            pltpu.VMEM((R, B, LANES), jnp.float32),
            pltpu.VMEM(block, jnp.float32),
            pltpu.VMEM((R, KA, KP * B, LANES), jnp.bfloat16),
            pltpu.VMEM(told_block, jnp.int32),
            pltpu.VMEM((R, KP * KA * KP), jnp.int32),
            pltpu.VMEM((KA, R), jnp.int32),
        ),
        scratch_shapes=[
            pltpu.VMEM(block, jnp.float32),
            pltpu.VMEM(block, jnp.float32),
            pltpu.VMEM(block, jnp.float32),
            pltpu.VMEM((KA * R // 8, 8 * TILE_ROWS, LANES), jnp.float32),
            pltpu.VMEM((N, LANES), jnp.int32),
            *[pltpu.VMEM(told_block, jnp.int32)] * 3,
            *relay_shapes(),
            pltpu.SemaphoreType.DMA((27 * len(LINES),)),
            pltpu.SemaphoreType.DMA((27 * len(LINES),)),
            pltpu.SemaphoreType.DMA((3 * len(LINES),)),
            pltpu.SemaphoreType.DMA((3,)),
            pltpu.SemaphoreType.DMA((24,)),
            pltpu.SemaphoreType.DMA((24,)),
            pltpu.SemaphoreType.DMA((3,)),
        ],
        compiler_params=pltpu.CompilerParams(collective_id=1, has_side_effects=True, vmem_limit_bytes=50100000),
        name="exchange",
    )(serve_rows[0].T, row_count, raw, recv_tile[0].T, a_native.reshape(KA * R // 8, 8 * TILE_ROWS, LANES), contrib_slot, a_slot.T)
    acc = pl.pallas_call(
        tile_kernel,
        grid_spec=pltpu.PrefetchScalarGridSpec(
            num_scalar_prefetch=1,
            in_specs=[vmem] * 6,
            out_specs=vmem,
            scratch_shapes=[
                pltpu.SMEM((N, 1, LANES), jnp.int32),
                pltpu.SMEM((R, KP * KA * KP), jnp.int32),
                pltpu.SMEM((KA, R), jnp.int32),
                pltpu.SemaphoreType.DMA((3,)),
            ],
        ),
        out_shape=pltpu.VMEM((N * TO, TILE_ROWS, LANES), jnp.float32),
        compiler_params=pltpu.CompilerParams(vmem_limit_bytes=2 * 2**20),
        name="tiles",
    )(row_count, left, rows, far.reshape(N * S, B, LANES), told.reshape(N, 1, LANES), slots, slot_rows)

    summed = reduce_scatter(acc)
    return summed.reshape(TO, TILE_ROWS, 2, B).transpose(0, 2, 1, 3).reshape(TO, B * B)


def solution(mesh):
    in_specs = (
        P("elem", None, None),
        P("elem", None, None),
        P("elem", None),
        P("elem", None, None),
        P("elem"),
        P("elem", None),
        P("elem", None, None),
    )
    return jax.shard_map(body, mesh=mesh, in_specs=in_specs, out_specs=P("elem", None), check_vma=False)
```

```python
import jax
import jax.numpy as jnp
from jax import lax
from jax.experimental import pallas as pl
from jax.experimental.pallas import tpu as pltpu
from jax.sharding import PartitionSpec as P


B = 64
KA = 7
KP = 2
S = 2
CAP = 4
TO = 8
R = 32
N = 128
RING = 4
LANES = 128
TILE_ROWS = B * B // LANES
OWNER_ROWS = TO * TILE_ROWS
MESH = pl.DeviceIdType.MESH

GROUPS = ((0, 40), (40, 48), (88, 40), (128, 48), (176, 40), (216, 40))
ORDERS = ((0, 1, 2), (1, 2, 0), (2, 0, 1)) * 2
SETS = ((0, 1, 2), (3, 4, 5))
AHEAD = 6


def split(value):
    high = value.astype(jnp.bfloat16)
    low = (value - high.astype(jnp.float32)).astype(jnp.bfloat16)
    return high, low


LINES = ((0, 16), (16, 16), (32, 16), (48, 16), (64, 8), (72, 16), (88, 8), (96, 16), (112, 16))
LINE_ORDERS = ((0, 1, 2), (1, 2, 0), (2, 0, 1)) * 3
LINE_SETS = ((0, 1, 2), (3, 4, 5), (6, 7, 8))
SHARES = (8, 8, 6, 6, 4)


def relay_shapes():
    return [pltpu.VMEM((RING, RING, length, LANES), jnp.float32) for _, length in LINES for _ in range(6)]


def exchange_kernel(serve_ref, count_ref, raw_ref, tiles_ref, a_hbm, slot_hbm, row_hbm, rows_ref, far_ref, left_ref, told_ref, slot_ref, row_ref, *rest):
    out, first_hop, second_hop, a_ref, turned_ref, first_told, second_told, third_told = rest[:8]
    relays = rest[8:-7]
    send, recv, local, pass_sem, told_send, told_recv, told_local = rest[-7:]
    hops = (out, first_hop, second_hop, far_ref)
    me = lax.axis_index("elem")
    core = me % 2
    chip = me // 2
    place = (chip // (RING * RING), (chip // RING) % RING, chip % RING)

    def device_at(axis, step, core_at):
        at = list(place)
        at[axis] = (at[axis] + step) % RING
        return ((at[0] * RING + at[1]) * RING + at[2]) * 2 + core_at

    barrier = pltpu.get_barrier_semaphore()

    near = [device_at(0, 0, 1 - core)]
    near += [device_at(axis, step, k) for axis in range(3) for step in (1, 2, 3) for k in range(2)]
    for other in near:
        pl.semaphore_signal(barrier, inc=1, device_id=(other,), device_id_type=MESH)
    passing = [
        pltpu.make_async_copy(source, target, pass_sem.at[n])
        for n, (source, target) in enumerate(((a_hbm, a_ref), (slot_hbm, slot_ref), (row_hbm, row_ref)))
    ]
    for copy in passing:
        copy.start()

    lane = lax.broadcasted_iota(jnp.int32, (B, LANES), 1) < B
    even = lax.broadcasted_iota(jnp.int32, (B, LANES), 0) % 2 == 0

    def turn(n, carry):
        raw = raw_ref[n]
        halves = pltpu.roll(raw, B, 1)
        other = jnp.where(even, pltpu.roll(halves, B - 1, 0), pltpu.roll(halves, 1, 0))
        rows_ref[n] = jnp.where(lane == even, raw, other)
        return carry

    lax.fori_loop(0, R, turn, 0)
    turned_ref[...] = jnp.zeros((N, LANES), jnp.int32)
    turned_ref[0:CAP, :] = tiles_ref[...]
    turned_ref[...] = turned_ref[...].T

    def gather(n, carry):
        y, x = n // RING, n % RING
        for z in range(RING):
            for k in range(2):
                ahead = lax.rem(n * (2 * RING) + (2 * z + k) + N - me, N)
                for c in range(S):
                    out[y, x, z, k, c * B : (c + 1) * B, :] = rows_ref[serve_ref[c, lax.rem(ahead + N - 2, N - 1)]]
                first_told[y, x, z, k] = turned_ref[pl.ds(lax.rem(N - ahead, N), 1), :]
        return carry

    lax.fori_loop(0, RING * RING, gather, 0)
    pl.semaphore_wait(barrier, len(near))
    tolds = (first_told, second_told, third_told, told_ref)

    def tell(phase):
        source, target = tolds[phase], tolds[phase + 1]
        u = place[phase]

        def at(index, core_at=slice(None)):
            spot = [slice(None)] * 3
            spot[phase] = index
            return tuple(spot) + (core_at, slice(None), slice(None))

        flights = []
        for step in range(RING):
            for part in range(2 if phase == 2 else 1):
                to = (u + step) % RING
                if phase == 2:
                    src, dst = source.at[at(to, part)], target.at[at(u, core)]
                    device = device_at(phase, step, part)
                else:
                    src, dst = source.at[at(to)], target.at[at(u)]
                    device = device_at(phase, step, core)
                if phase == 2 and step == 0:
                    continue
                if step == 0:
                    copy = pltpu.make_async_copy(src, dst, told_local.at[phase])
                    copy.start()
                    told_waits.append((phase, copy.wait))
                    continue
                lane_of = phase * 8 + 2 * step + (core if phase == 2 else 0)
                copy = pltpu.make_async_remote_copy(
                    src_ref=src,
                    dst_ref=dst,
                    send_sem=told_send.at[phase * 8 + 2 * step + part],
                    recv_sem=told_recv.at[lane_of],
                    device_id=(device,),
                    device_id_type=MESH,
                )
                copy.start()
                sent.append(copy)
        if phase == 2:
            copy = pltpu.make_async_copy(source.at[at(u, core)], target.at[at(u, core)], told_local.at[2])
            copy.start()
            told_waits.append((phase, copy.wait))
            copy = pltpu.make_async_remote_copy(
                src_ref=source.at[at(u, 1 - core)],
                dst_ref=target.at[at(u, core)],
                send_sem=told_send.at[phase * 8],
                recv_sem=told_recv.at[phase * 8],
                device_id=(device_at(phase, 0, 1 - core),),
                device_id_type=MESH,
            )
            copy.start()
            sent.append(copy)

    def told_wait(phase):
        target = tolds[phase + 1]
        for at_phase, wait in told_waits:
            if at_phase == phase:
                wait()
        spot = [slice(None)] * 3
        spot[phase] = place[phase]
        lanes = (0, 2, 3, 4, 5, 6, 7) if phase == 2 else (2, 4, 6)
        like = target.at[tuple(spot) + ((core if phase == 2 else slice(None)), slice(None), slice(None))]
        for lane_of in lanes:
            pltpu.make_async_copy(like, like, told_recv.at[phase * 8 + lane_of]).wait()

    told_waits = []
    def window(group, axis, at_axis, core_at):
        at = [slice(None)] * 3
        at[axis] = at_axis
        return tuple(at) + (slice(None) if core_at is None else core_at, pl.ds(*LINES[group]), slice(None))

    sent = []
    arrivals = {}

    def fly(group, phase, kind, source, target, device, lane_of=0):
        base = (group * 3 + phase) * 9
        copy = pltpu.make_async_remote_copy(
            src_ref=source,
            dst_ref=target,
            send_sem=send.at[base + kind],
            recv_sem=recv.at[base + lane_of],
            device_id=(device,),
            device_id_type=MESH,
        )
        copy.start()
        sent.append(copy)

    def land(group, phase, lane_of, like):
        pltpu.make_async_copy(like, like, recv.at[(group * 3 + phase) * 9 + lane_of]).wait()

    def first_wave(groups, phase):
        source, target = hops[phase], hops[phase + 1]
        for group in groups:
            axis = LINE_ORDERS[group][phase]
            u = place[axis]
            for part, step in ((0, 1), (1, 3)):
                relay = relays[(group * 3 + phase) * 2 + part]
                src = source.at[window(group, axis, (u + 2) % RING, part)]
                fly(group, phase, part, src, relay, device_at(axis, step, core), part)
        for side, step in ((0, 1), (1, 3)):
            for group in groups:
                axis = LINE_ORDERS[group][phase]
                u = place[axis]
                to = (u + step) % RING
                if phase < 2:
                    at = window(group, axis, u, None)
                    fly(group, phase, 2 + side, source.at[window(group, axis, to, None)], target.at[at], device_at(axis, step, core), 2 + side)
                else:
                    at = window(group, axis, u, core)
                    for part in range(2):
                        kind = 2 + 2 * side + part
                        src = source.at[window(group, axis, to, part)]
                        fly(group, phase, kind, src, target.at[at], device_at(axis, step, part), 2 + 2 * side + core)
        for group in groups:
            axis = LINE_ORDERS[group][phase]
            u = place[axis]
            at = window(group, axis, u, None if phase < 2 else core)
            keep = pltpu.make_async_copy(source.at[at], target.at[at], local.at[group * 3 + phase])
            keep.start()
            arrivals[group, phase] = keep
            if phase == 2:
                src = source.at[window(group, axis, u, 1 - core)]
                fly(group, phase, 8, src, target.at[at], device_at(axis, 0, 1 - core), 8)

    def second_wave(groups, phase):
        target = hops[phase + 1]
        for group in groups:
            axis = LINE_ORDERS[group][phase]
            u = place[axis]
            for part, step in ((0, 1), (1, 3)):
                relay = relays[(group * 3 + phase) * 2 + part]
                land(group, phase, part, relay)
                origin = (u + RING - step) % RING
                if phase < 2:
                    at = window(group, axis, origin, part)
                    fly(group, phase, 6 + part, relay, target.at[at], device_at(axis, step, core), 6 + part)
                else:
                    at = window(group, axis, origin, core)
                    fly(group, phase, 6 + part, relay, target.at[at], device_at(axis, step, part), 6 + core)

    def third_wave(groups, phase):
        target = hops[phase + 1]
        for group in groups:
            axis = LINE_ORDERS[group][phase]
            u = place[axis]
            arrivals[group, phase].wait()
            for side in range(2):
                if phase < 2:
                    land(group, phase, 2 + side, target.at[window(group, axis, u, None)])
                else:
                    land(group, phase, 2 + 2 * side, target.at[window(group, axis, u, core)])
                    land(group, phase, 3 + 2 * side, target.at[window(group, axis, u, core)])
            land(group, phase, 6, target.at[window(group, axis, u, core)])
            land(group, phase, 7, target.at[window(group, axis, u, core)])
            if phase == 2:
                land(group, phase, 8, target.at[window(group, axis, u, core)])

    def left_row(row, carry):
        low_half = lax.broadcasted_iota(jnp.int32, (TILE_ROWS, LANES), 1) < B
        stack = [rows_ref[row, pl.ds(h, TILE_ROWS, stride=2), :] for h in range(2)]
        high, low = split(jnp.concatenate(stack, axis=0).T)
        factor = jnp.concatenate([high, low], axis=1)
        for k in range(KA):
            block = a_ref[k * (R // 8) + row // 8, pl.ds(row % 8, TILE_ROWS, stride=8), :]
            turned = pltpu.roll(block, B, 1)
            value = jnp.concatenate([jnp.where(low_half, block, turned), jnp.where(low_half, turned, block)], axis=0)
            top = value.astype(jnp.bfloat16).astype(jnp.float32)
            wide = jnp.where(lane, top, value - top).astype(jnp.bfloat16)
            both = jnp.dot(factor, jnp.concatenate([wide, wide], axis=0), preferred_element_type=jnp.float32)
            twice = both + pltpu.roll(both, B, 1)
            m_high = twice.astype(jnp.bfloat16).astype(jnp.float32)
            wide_lane = lax.broadcasted_iota(jnp.int32, (KP * B, LANES), 1) < B
            left_ref[row, k] = jnp.where(wide_lane, m_high, twice - m_high).astype(jnp.bfloat16)
        return carry

    def left_share(n):
        done = sum(SHARES[:n])
        lax.fori_loop(done, done + SHARES[n], left_row, 0)

    for groups in LINE_SETS:
        first_wave(groups, 0)
    tell(0)
    for copy in passing:
        copy.wait()
    left_share(0)
    for phase in range(3):
        for groups in LINE_SETS:
            second_wave(groups, phase)
        if phase < 2:
            left_share(2 * phase + 1)
        if phase == 2:
            for copy in sent:
                copy.wait_send()
        for group in range(len(LINES)):
            third_wave((group,), phase)
            if phase < 2:
                first_wave((group,), phase + 1)
        told_wait(phase)
        if phase < 2:
            tell(phase + 1)
            left_share(2 * phase + 2)


def tile_kernel(count_ref, left_ref, own_ref, far_ref, told_in, slot_in, row_in, acc, told, slot_ref, row_ref, sem):
    me = lax.axis_index("elem")
    tables = [
        pltpu.make_async_copy(source, target, sem.at[n])
        for n, (source, target) in enumerate(((told_in, told), (slot_in, slot_ref), (row_in, row_ref)))
    ]
    for copy in tables:
        copy.start()

    def clear(n, carry):
        acc[pl.ds(n * 8, 8)] = jnp.zeros((8, TILE_ROWS, LANES), jnp.float32)
        return carry

    lax.fori_loop(0, N * TO // 8, clear, 0)
    for copy in tables:
        copy.wait()
    lane = lax.broadcasted_iota(jnp.int32, (TILE_ROWS, LANES), 1)

    def step(row, carry):
        for k in range(KA):
            index = row_ref[k, row]
            away = jnp.maximum(index - R, 0)
            own = own_ref[jnp.minimum(index, R - 1)]
            far = far_ref[lax.rem(me + 2 * N - 1 - lax.div(away, S), N) * S + lax.rem(away, S)]
            high, low = split(jnp.where(index < R, own, far))
            wide = jnp.concatenate([high, low], axis=1)
            both = jnp.dot(left_ref[row, k], jnp.concatenate([wide, wide], axis=0), preferred_element_type=jnp.float32)
            part = both[:, :LANES] + both[:, LANES:]
            turned = pltpu.roll(part, B, 1)
            for p in range(KP):
                top, bottom = p * B, p * B + TILE_ROWS
                upper, lower = part[top : top + TILE_ROWS], part[bottom : bottom + TILE_ROWS]
                upper_t, lower_t = turned[top : top + TILE_ROWS], turned[bottom : bottom + TILE_ROWS]
                tiles = (jnp.where(lane < B, upper, lower_t), jnp.where(lane < B, upper_t, lower))
                targets = []
                for q in range(KP):
                    slot = slot_ref[row, p * (KA * KP) + k * KP + q]
                    owner = lax.rem(me + lax.div(slot, CAP), N)
                    targets.append(owner * TO + told[owner, 0, lax.rem(slot, CAP)])
                first, second = (acc[target] for target in targets)
                acc[targets[0]] = first + tiles[0]
                acc[targets[1]] = second + (tiles[1] + jnp.where(targets[0] == targets[1], tiles[0], 0.0))
        return carry

    count = jnp.minimum(count_ref[0], R)

    def sixteen(n, carry):
        for m in range(16):
            step(16 * n + m, carry)
        return carry

    lax.fori_loop(0, lax.div(count, 16), sixteen, 0)
    lax.fori_loop(lax.div(count, 16) * 16, count, step, 0)


def ring_shapes():
    shapes = []
    for _, length in GROUPS:
        for stage in range(3):
            lead = (RING,) * (2 - stage)
            slab = lead + (length, LANES)
            shapes += [pltpu.VMEM(slab, jnp.float32)] * 3
    return shapes


def add(target, *terms):
    def one(at):
        value = target[at]
        for term in terms:
            value = value + term[at]
        target[at] = value

    lead = target.shape[:-2]
    whole = (slice(None), slice(None))
    if not lead:
        one(whole)
        return

    def outer(n, carry):
        if len(lead) == 1:
            one((n,) + whole)
        else:
            for m in range(lead[1]):
                one((n, m) + whole)
        return carry

    lax.fori_loop(0, lead[0], outer, 0)


def reduce_kernel(acc_ref, out_ref, mine, *rest):
    bufs, (in_send, in_recv, ring_send, ring_recv) = rest[:-4], rest[-4:]
    me = lax.axis_index("elem")
    core = me % 2
    chip = me // 2
    place = (chip // (RING * RING), (chip // RING) % RING, chip % RING)
    partner = me + 1 - 2 * core

    def device_at(axis, step):
        at = list(place)
        at[axis] = (at[axis] + step) % RING
        return ((at[0] * RING + at[1]) * RING + at[2]) * 2 + core

    barrier = pltpu.get_barrier_semaphore()
    near = [partner] + [device_at(axis, step) for axis in range(3) for step in (1, 2, 3)]
    for other in near:
        pl.semaphore_signal(barrier, inc=1, device_id=(other,), device_id_type=MESH)
    pl.semaphore_wait(barrier, len(near))

    def window(group, fixed, part):
        free = [axis for axis in range(3) if axis not in fixed]
        at = [fixed.get(axis, slice(None)) for axis in range(3)]
        inner = [slice(None)] * len(free)
        first, length = GROUPS[group]
        rows = (0, length)
        if part is not None:
            if free:
                at[free[0]] = inner[0] = pl.ds(part * (RING // 2), RING // 2)
            else:
                half = (length + 8) // 16 * 8
                rows = (half * part, length - half if part else half)
        return (
            tuple(at) + (pl.ds(first + rows[0], rows[1]), slice(None)),
            tuple(inner) + (pl.ds(rows[0], rows[1]), slice(None)),
        )

    def across(group, fixed, core_at):
        at, _ = window(group, fixed, None)
        return at[:3] + (core_at,) + at[3:]

    queue = [(n, step) for n in range(len(SETS)) for step in (2, 1, 3)] + [(n, 0) for n in range(len(SETS))]
    queue = [(group, step) for n, step in queue for group in SETS[n]]
    loads, sends = {}, []

    def fetch():
        if len(loads) == len(queue):
            return
        group, offset = queue[len(loads)]
        axis = ORDERS[group][0]
        fixed = {axis: (place[axis] + offset) % RING}
        n = group * RING + offset
        at, _ = window(group, fixed, None)
        give = pltpu.make_async_remote_copy(
            src_ref=acc_ref.at[across(group, fixed, 1 - core)],
            dst_ref=mine.at[at],
            send_sem=in_send.at[n],
            recv_sem=in_recv.at[n],
            device_id=(partner,),
            device_id_type=MESH,
        )
        give.start()
        loads[group, offset] = (give, acc_ref.at[across(group, fixed, core)], mine.at[at])
        sends.append(give)

    for _ in range(AHEAD):
        fetch()

    def arrive(group, offset):
        give, own, target = loads[group, offset]
        give.wait_recv()
        fetch()
        add(target, own)

    flights = {}

    def fixed_at(group, stage, step):
        order = ORDERS[group]
        fixed = {axis: place[axis] for axis in order[:stage]}
        fixed[order[stage]] = (place[order[stage]] + step) % RING
        return fixed

    def start(group, stage, kind, step, part, towards, buffer):
        n = (group * 3 + stage) * 6 + kind
        at, inner = window(group, fixed_at(group, stage, step), part)
        copy = pltpu.make_async_remote_copy(
            src_ref=mine.at[at],
            dst_ref=bufs[(group * 3 + stage) * 3 + buffer].at[inner],
            send_sem=ring_send.at[n],
            recv_sem=ring_recv.at[n],
            device_id=(device_at(ORDERS[group][stage], towards),),
            device_id_type=MESH,
        )
        copy.start()
        flights[group, stage, kind] = copy
        sends.append(copy)

    def first_wave(groups, stage):
        for step, sends_of in ((2, ((0, 0, 1, 0), (1, 1, 3, 0))), (1, ((2, 1, 1, 1),)), (3, ((3, 0, 3, 2),))):
            for group in groups:
                if stage == 0:
                    arrive(group, step)
                for kind, part, towards, buffer in sends_of:
                    start(group, stage, kind, step, part, towards, buffer)

    def last_sends(groups):
        for kind, step in ((1, 2), (0, 1), (2, 3)):
            for group in groups:
                start(group, 2, kind, step, None, step, kind)

    def finish(groups):
        for group in groups:
            for kind in range(3):
                flights[group, 2, kind].wait_recv()
            at, _ = window(group, fixed_at(group, 2, 0), None)
            first, length = GROUPS[group]
            terms = bufs[(group * 3 + 2) * 3 : (group * 3 + 2) * 3 + 3]
            out_ref[pl.ds(first, length), :] = mine[at] + terms[0][...] + terms[1][...] + terms[2][...]

    def second_wave(group, stage):
        buffer = bufs[(group * 3 + stage) * 3]
        for kind, part, step in ((0, 0, 1), (1, 1, 3)):
            flights[group, stage, kind].wait_recv()
            at, inner = window(group, fixed_at(group, stage, step), part)
            add(mine.at[at], buffer.at[inner])
            start(group, stage, 4 + kind, step, part, step, 1 + kind)

    def third_wave(group, stage):
        for kind in (2, 3, 4, 5):
            flights[group, stage, kind].wait_recv()
        at, _ = window(group, fixed_at(group, stage, 0), None)
        _, plus, minus = bufs[(group * 3 + stage) * 3 : (group * 3 + stage) * 3 + 3]
        add(mine.at[at], plus, minus)

    for groups in SETS:
        first_wave(groups, 0)
    for stage in range(2):
        for groups in SETS:
            for group in groups:
                second_wave(group, stage)
        if stage == 0:
            for group in range(len(GROUPS)):
                arrive(group, 0)
        for group in range(len(GROUPS)):
            third_wave(group, stage)
            if stage == 0:
                first_wave((group,), 1)
            else:
                last_sends((group,))
    for copy in sends:
        copy.wait_send()
    for groups in SETS:
        finish(groups)


def reduce_scatter(acc):
    return pl.pallas_call(
        reduce_kernel,
        out_shape=jax.ShapeDtypeStruct((OWNER_ROWS, LANES), jnp.float32),
        in_specs=[pl.BlockSpec(memory_space=pltpu.VMEM)],
        out_specs=pl.BlockSpec(memory_space=pltpu.VMEM),
        scratch_shapes=[
            pltpu.VMEM((RING, RING, RING, OWNER_ROWS, LANES), jnp.float32),
            *ring_shapes(),
            pltpu.SemaphoreType.DMA((RING * len(GROUPS),)),
            pltpu.SemaphoreType.DMA((RING * len(GROUPS),)),
            pltpu.SemaphoreType.DMA((18 * len(GROUPS),)),
            pltpu.SemaphoreType.DMA((18 * len(GROUPS),)),
        ],
        compiler_params=pltpu.CompilerParams(collective_id=0, has_side_effects=True, vmem_limit_bytes=20 * 2**20),
        name="reduce_scatter",
    )(acc.reshape(RING, RING, RING, 2, OWNER_ROWS, LANES))


def body(a_blocks, p_blocks, a_slot, serve_rows, row_count, contrib_slot, recv_tile):
    raw = p_blocks.reshape(R, KP, TILE_ROWS, LANES).transpose(0, 2, 1, 3).reshape(R, B, LANES)
    a_native = a_blocks.transpose(1, 0, 2).reshape(KA, R // 8, 8, TILE_ROWS, LANES).transpose(0, 1, 3, 2, 4)
    block = (RING, RING, RING, 2, S * B, LANES)
    told_block = (RING, RING, RING, 2, 1, LANES)
    vmem = pl.BlockSpec(memory_space=pltpu.VMEM)
    smem = pl.BlockSpec(memory_space=pltpu.SMEM)
    rows, far, left, told, slots, slot_rows = pl.pallas_call(
        exchange_kernel,
        in_specs=[smem, smem, vmem, vmem] + [pl.BlockSpec(memory_space=pl.ANY)] * 3,
        out_specs=(vmem,) * 6,
        out_shape=(
            pltpu.VMEM((R, B, LANES), jnp.float32),
            pltpu.VMEM(block, jnp.float32),
            pltpu.VMEM((R, KA, KP * B, LANES), jnp.bfloat16),
            pltpu.VMEM(told_block, jnp.int32),
            pltpu.VMEM((R, KP * KA * KP), jnp.int32),
            pltpu.VMEM((KA, R), jnp.int32),
        ),
        scratch_shapes=[
            pltpu.VMEM(block, jnp.float32),
            pltpu.VMEM(block, jnp.float32),
            pltpu.VMEM(block, jnp.float32),
            pltpu.VMEM((KA * R // 8, 8 * TILE_ROWS, LANES), jnp.float32),
            pltpu.VMEM((N, LANES), jnp.int32),
            *[pltpu.VMEM(told_block, jnp.int32)] * 3,
            *relay_shapes(),
            pltpu.SemaphoreType.DMA((27 * len(LINES),)),
            pltpu.SemaphoreType.DMA((27 * len(LINES),)),
            pltpu.SemaphoreType.DMA((3 * len(LINES),)),
            pltpu.SemaphoreType.DMA((3,)),
            pltpu.SemaphoreType.DMA((24,)),
            pltpu.SemaphoreType.DMA((24,)),
            pltpu.SemaphoreType.DMA((3,)),
        ],
        compiler_params=pltpu.CompilerParams(collective_id=1, has_side_effects=True, vmem_limit_bytes=50100000),
        name="exchange",
    )(serve_rows[0].T, row_count, raw, recv_tile[0].T, a_native.reshape(KA * R // 8, 8 * TILE_ROWS, LANES), contrib_slot, a_slot.T)
    acc = pl.pallas_call(
        tile_kernel,
        grid_spec=pltpu.PrefetchScalarGridSpec(
            num_scalar_prefetch=1,
            in_specs=[vmem] * 6,
            out_specs=vmem,
            scratch_shapes=[
                pltpu.SMEM((N, 1, LANES), jnp.int32),
                pltpu.SMEM((R, KP * KA * KP), jnp.int32),
                pltpu.SMEM((KA, R), jnp.int32),
                pltpu.SemaphoreType.DMA((3,)),
            ],
        ),
        out_shape=pltpu.VMEM((N * TO, TILE_ROWS, LANES), jnp.float32),
        compiler_params=pltpu.CompilerParams(vmem_limit_bytes=2 * 2**20),
        name="tiles",
    )(row_count, left, rows, far.reshape(N * S, B, LANES), told.reshape(N, 1, LANES), slots, slot_rows)

    summed = reduce_scatter(acc)
    return summed.reshape(TO, TILE_ROWS, 2, B).transpose(0, 2, 1, 3).reshape(TO, B * B)


def solution(mesh):
    in_specs = (
        P("elem", None, None),
        P("elem", None, None),
        P("elem", None),
        P("elem", None, None),
        P("elem"),
        P("elem", None),
        P("elem", None, None),
    )
    return jax.shard_map(body, mesh=mesh, in_specs=in_specs, out_specs=P("elem", None), check_vma=False)
```
